32 devices in a mesh: slot: 4 (over z), pb: 8 (over y, x, core).
Axes of the slice: x: 2, y: 2, z: 4, core: 2. Of those that a mesh axis runs over, the one named last changes fastest.
Arguments:
- inputs: bfloat16 [8, 4, 64, 1024], P('pb', 'slot'), may hold values from -6 to 6
- memory: bfloat16 [8, 4, 128, 1024], P('pb', 'slot'), may hold values from -6 to 6
- attn_weight: bfloat16 [1024, 6, 1024], P('pb'), may hold values from -0.1875 to 0.1875
- attn_out: bfloat16 [1024, 2, 1024], P('pb'), may hold values from -0.75 to 0.75
- ffn_in: bfloat16 [1024, 4096], P('pb'), may hold values from -0.1875 to 0.1875
- ffn_out: bfloat16 [4096, 1024], P('pb'), may hold values from -0.09375 to 0.09375
- attn_bias: float32 [1024, 6], replicated, may hold values from -3 to 3
- norm_gain: float32 [1024, 3], replicated, may hold values from 0.5 to 1.5
- norm_bias: float32 [1024, 3], replicated, may hold values from -2 to 2
- bias_in: float32 [4096], replicated, may hold values from -3 to 3
- bias_out: float32 [1024], replicated, may hold values from -2 to 2
- embedding: bfloat16 [32768, 1024], P('pb'), may hold values from -0.375 to 0.375
- targets: int32 [8, 64], replicated, may hold values from 0 to 32767
- slot_counts: int32 [8], replicated, may hold values from 2 to 4
- pad_mask: int32 [8, 64], P('pb'), may hold values 0 or 1
- log_prior: float32 [8, 4], P('pb', 'slot'), may hold values from -4 to 4
Outputs:
- token_logprob: float32 [8, 64], P('pb')
- grad_inputs: float32 [8, 4, 64, 1024], P('pb', 'slot')
- grad_memory: float32 [8, 4, 128, 1024], P('pb', 'slot')
- grad_log_prior: float32 [8, 4], P('pb', 'slot')
- grad_attn_weight: float32 [1024, 6, 1024], P(('slot', 'pb'))
- grad_attn_out: float32 [1024, 2, 1024], P(('slot', 'pb'))
- grad_ffn_in: float32 [1024, 4096], P(('slot', 'pb'))
- grad_ffn_out: float32 [4096, 1024], P(('slot', 'pb'))
- grad_attn_bias: float32 [1024, 6], P(('slot', 'pb'))
- grad_norm_gain: float32 [1024, 3], P(('slot', 'pb'))
- grad_norm_bias: float32 [1024, 3], P(('slot', 'pb'))
- grad_bias_in: float32 [4096], P(('slot', 'pb'))
- grad_bias_out: float32 [1024], P(('slot', 'pb'))
- grad_embedding: float32 [32768, 1024], P('pb')
The draws below stay inside these ranges and needn't reach their ends.
Inputs may be any that keep to these rules, and one draw needn't show every extreme that they name: Slots 0 to slot_counts[q] - 1 of question q hold passages; the others are padding.
All inputs are finite; a program needn't handle non-finite values. No bound on the sum of `pad_mask` on one device may be relied on, other than what follows from the above.
Results may differ from the reference program's by a relative error of at most 0.029.
Values may be sent and summed in bfloat16 or wider, within the bound.
No kernel may reach another device: no remote copies, remote signals or barrier semaphores. Data moves between devices by JAX's collectives and lax.ppermute only.
A program may use at most 320 MiB of HBM per device.

```python
import math
import jax
import jax.numpy as jnp
import numpy as np
from jax import lax

D = 1024
HEADS = 16
HEAD = 64
FF = 4096
VOCAB = 32768
LEN = 64
MEM = 128
QUESTIONS = 8
SLOTS = 4
N_SLOT = 4


def set_ends(values, rng, smallest, top_value):
    longest = values.shape.index(max(values.shape))
    spots = []
    for shift in (0, 1):
        where = [jax.random.randint(jax.random.fold_in(rng, axis), (), 0, length) for axis, length in enumerate(values.shape)]
        where[longest] = (where[longest] + shift) % values.shape[longest]
        spots.append(tuple(where))
    return values.at[spots[0]].set(smallest).at[spots[1]].set(top_value)


def steps_of(key, extent, pieces, least, top_value):
    level, own = 1.0, jax.random.fold_in(key, 6)
    for position, shards_of in pieces:
        steps = jnp.exp(jax.random.uniform(jax.random.fold_in(own, position), (shards_of,), jnp.float32, least / len(pieces), top_value / len(pieces)))
        level = level * jnp.repeat(steps, extent[position] // shards_of).reshape([-1 if axis == position else 1 for axis in range(len(extent))])
    return level


def cumulative_ranks(number_of, skew):
    weights = [(1 << 20) // math.isqrt(rank ** skew) + 1 for rank in range(1, number_of + 1)]
    spread = 1 + sum(weights) // (1 << 30)
    return np.cumsum(np.array([max(1, weight // spread) for weight in weights]))


def ranked(rng, shape, number_of, lean):
    table = cumulative_ranks(number_of, lean)
    lot = jax.random.randint(jax.random.fold_in(rng, 1), shape, 0, int(table[number_of - 1]))
    rank = jnp.searchsorted(jnp.asarray(table, jnp.int32), lot, side="right")
    return jax.random.permutation(jax.random.fold_in(rng, 2), number_of)[rank].astype(jnp.int32)


def scatter_about(rng, extent, scale, bound, pieces=(), held_as=jnp.bfloat16):
    values = scale * jax.random.normal(rng, extent, jnp.float32)
    if pieces:
        values = values * steps_of(rng, extent, pieces, -0.22, 0.18)
    return jnp.clip(values, -bound, bound).astype(held_as)


def setup_inputs(seed: int = 0) -> dict:
    seeds = jax.random.split(jax.random.key(seed), 17)
    return {
        "inputs": scatter_about(seeds[0], (QUESTIONS, SLOTS, LEN, D), 1.0, 6.0, ((0, 8), (1, 4))),
        "memory": scatter_about(seeds[1], (QUESTIONS, SLOTS, MEM, D), 1.0, 6.0, ((0, 8), (1, 4))),
        "attn_weight": scatter_about(seeds[2], (D, 6, D), D ** -0.5, 0.1875, ((0, 8),)),
        "attn_out": scatter_about(seeds[3], (D, 2, D), (D // 16) ** -0.5, 0.75, ((0, 8),)),
        "ffn_in": scatter_about(seeds[4], (D, FF), D ** -0.5, 0.1875, ((0, 8),)),
        "ffn_out": scatter_about(seeds[5], (FF, D), FF ** -0.5, 0.09375, ((0, 8),)),
        "attn_bias": scatter_about(seeds[6], (D, 6), 0.5, 3.0, (), jnp.float32),
        "norm_gain": jnp.clip(1.0 + 0.1 * jax.random.normal(seeds[7], (D, 3), jnp.float32), 0.5, 1.5),
        "norm_bias": scatter_about(seeds[8], (D, 3), 0.3, 2.0, (), jnp.float32),
        "bias_in": scatter_about(seeds[9], (FF,), 0.5, 3.0, (), jnp.float32),
        "bias_out": scatter_about(seeds[10], (D,), 0.3, 2.0, (), jnp.float32),
        "embedding": scatter_about(seeds[11], (VOCAB, D), (D // 4) ** -0.5, 0.375, ((0, 8),)),
        "targets": set_ends(ranked(seeds[12], (QUESTIONS, LEN), VOCAB, 2), jax.random.fold_in(seeds[12], 3), 0, VOCAB - 1).astype(jnp.int32),
        "slot_counts": set_ends(jax.random.randint(seeds[13], (QUESTIONS,), 2, N_SLOT + 1), jax.random.fold_in(seeds[13], 1), 2, N_SLOT).astype(jnp.int32),
        "pad_mask": set_ends((jax.random.randint(seeds[14], (QUESTIONS, LEN), 0, 8) < 7).astype(jnp.int32), jax.random.fold_in(seeds[14], 1), 0, 1),
        "log_prior": scatter_about(seeds[15], (QUESTIONS, SLOTS), 1.0, 4.0, ((0, 8), (1, 4)), jnp.float32),
    }


@jax.custom_vjp
def low(v):
    return lax.optimization_barrier(v.astype(jnp.bfloat16)).astype(jnp.float32)

@jax.custom_vjp
def low_back(v):
    return v

def low_keep(v):
    return (low(v), None)

def low_pass(kept, grad):
    return (grad,)

def back_keep(v):
    return (v, None)

def back_low(kept, grad):
    return (low(grad),)
low.defvjp(low_keep, low_pass)
low_back.defvjp(back_keep, back_low)

def both_ways(tensor):
    return low_back(low(tensor))

def matmul(matrix_left, matrix_right):
    return jnp.dot(matrix_left, matrix_right, precision=lax.Precision.HIGHEST)

def layer_norm(tensor, gain_row, shift_row):
    centered = tensor - lax.optimization_barrier(jnp.mean(tensor, axis=-1, keepdims=True))
    variance = lax.optimization_barrier(jnp.mean(centered * centered, axis=-1, keepdims=True))
    return centered * lax.rsqrt(variance + 1e-05) * gain_row + shift_row

def attention(queries, key_rows, value_rows, causal):
    query_count = queries.shape[0]
    key_count = key_rows.shape[0]
    query_heads = queries.reshape(query_count, HEADS, HEAD)
    key_heads = key_rows.reshape(key_count, HEADS, HEAD)
    value_heads = value_rows.reshape(key_count, HEADS, HEAD)
    scores = low_back(jnp.einsum('qhd,khd->hqk', query_heads, key_heads, precision=lax.Precision.HIGHEST) * 0.125)
    if causal:
        causal_keep = jnp.arange(query_count)[:, None] >= jnp.arange(key_count)[None, :]
        scores = jnp.where(causal_keep[None, :, :], scores, -1e+30)
    attn_probs = low(jax.nn.softmax(scores, axis=-1))
    blended = jnp.einsum('hqk,khd->qhd', attn_probs, value_heads, precision=lax.Precision.HIGHEST)
    return blended.reshape(query_count, HEADS * HEAD)

def slot_logp(weights, source, passage, slot_prior, token_ids):
    attn_weight, attn_out, ffn_in, ffn_out, attn_bias, norm_gain, norm_bias, bias_in, bias_out, embedding = weights
    queries = both_ways(matmul(source, attn_weight[:, 0, :]) + attn_bias[:, 0])
    key_rows = both_ways(matmul(source, attn_weight[:, 1, :]))
    value_rows = both_ways(matmul(source, attn_weight[:, 2, :]) + attn_bias[:, 1])
    self_mix = both_ways(attention(queries, key_rows, value_rows, True))
    resid_one = source + low_back(matmul(self_mix, attn_out[:, 0, :]) + attn_bias[:, 2])
    hidden_one = layer_norm(resid_one, norm_gain[:, 0], norm_bias[:, 0])
    cross_queries = both_ways(matmul(low(hidden_one), attn_weight[:, 3, :]) + attn_bias[:, 3])
    cross_keys = both_ways(matmul(passage, attn_weight[:, 4, :]))
    cross_values = both_ways(matmul(passage, attn_weight[:, 5, :]) + attn_bias[:, 4])
    cross_mix = both_ways(attention(cross_queries, cross_keys, cross_values, False))
    resid_two = hidden_one + low_back(matmul(cross_mix, attn_out[:, 1, :]) + attn_bias[:, 5])
    hidden_two = layer_norm(resid_two, norm_gain[:, 1], norm_bias[:, 1])
    upward = low_back(matmul(low(hidden_two), ffn_in) + bias_in)
    active = both_ways(jax.nn.gelu(upward, approximate=False))
    resid_three = hidden_two + low_back(matmul(active, ffn_out) + bias_out)
    hidden_three = layer_norm(resid_three, norm_gain[:, 2], norm_bias[:, 2])
    logits = low_back(matmul(low(hidden_three), embedding.T))
    normalizer = jax.nn.logsumexp(logits, axis=-1)
    picked = jnp.take_along_axis(logits, token_ids[:, None].astype(jnp.int32), axis=1)[:, 0]
    return picked - normalizer + slot_prior

def reference(inputs, memory, attn_weight, attn_out, ffn_in, ffn_out, attn_bias, norm_gain, norm_bias, bias_in, bias_out, embedding, targets, slot_counts, pad_mask, log_prior):
    params = (attn_weight.astype(jnp.float32), attn_out.astype(jnp.float32), ffn_in.astype(jnp.float32), ffn_out.astype(jnp.float32), attn_bias.astype(jnp.float32), norm_gain.astype(jnp.float32), norm_bias.astype(jnp.float32), bias_in.astype(jnp.float32), bias_out.astype(jnp.float32), embedding.astype(jnp.float32))

    def question(running, question_data):
        sources, passages, priors, token_ids, loss_mask, slot_total = question_data
        sources = sources.astype(jnp.float32)
        passages = passages.astype(jnp.float32)

        def loss_of(weights, source_all, passage_all, prior_all):
            logps = jax.vmap(lambda source_one, passage_one, prior_one: slot_logp(weights, source_one, passage_one, prior_one, token_ids))(source_all, passage_all, prior_all)
            usable = jnp.arange(N_SLOT).astype(jnp.int32)[:, None] < slot_total
            merged = jax.nn.logsumexp(jnp.where(usable, logps, -1e+30), axis=0)
            total_loss = -jnp.sum(loss_mask.astype(jnp.float32) * merged)
            return (total_loss, merged)
        total_loss, pullback, merged = jax.vjp(loss_of, params, sources, passages, priors, has_aux=True)
        grad_params, grad_sources, grad_passages, grad_priors = pullback(jnp.ones_like(total_loss))
        running = jax.tree.map(lambda first_part, second_part: first_part + second_part, running, grad_params)
        return (running, (merged, grad_sources, grad_passages, grad_priors))
    initial = jax.tree.map(jnp.zeros_like, params)
    totals, stacked = lax.scan(question, initial, (inputs, memory, log_prior.astype(jnp.float32), targets, pad_mask, slot_counts))
    merged, grad_sources, grad_passages, grad_priors = stacked
    return (merged, grad_sources, grad_passages, grad_priors, totals[0], totals[1], totals[2], totals[3], totals[4], totals[5], totals[6], totals[7], totals[8], totals[9])
```

```python
import jax
import jax.numpy as jnp
from jax import lax
from jax.sharding import PartitionSpec as P

HEAD = 64
CHIPS = 4
CORES = 2
TEAM = CHIPS * CORES
BF = jnp.bfloat16
F32 = jnp.float32


def chip_pairs(size, k):
    return [(i, (i // TEAM) * TEAM + ((i % TEAM) // CORES ^ k) * CORES + i % CORES) for i in range(size)]


def from_chip(x, k):
    return lax.ppermute(x, "pb", chip_pairs(lax.axis_size("pb"), k))


def from_core(x):
    return lax.ppermute(x, "pb", [(i, i ^ 1) for i in range(lax.axis_size("pb"))])


def from_slot(x, k):
    size = lax.axis_size("slot")
    return lax.ppermute(x, "slot", [(i, (i + k) % size) for i in range(size)])


def team_groups():
    size = lax.axis_size("pb")
    return [[g * TEAM + j for g in range(size // TEAM)] for j in range(TEAM)]


def product(a, b):
    return jnp.dot(a, b, preferred_element_type=F32)


def product_t(a, b):
    return jnp.einsum("re,de->rd", a, b, preferred_element_type=F32)


def weight_product(a, g):
    return jnp.einsum("rd,re->de", a, g, preferred_element_type=F32)


def at(x, index):
    return lax.dynamic_index_in_dim(x, index, 0, False)


def collect(x):
    return jnp.stack([x] + [from_chip(x, k) for k in range(1, CHIPS)])


def reduce_chips(parts):
    total = parts[0]
    for k in range(1, CHIPS):
        total = total + from_chip(parts[k].astype(BF), k).astype(F32)
    return total


def layer_norm(r, gain, shift):
    centered = r - jnp.mean(r, axis=-1, keepdims=True)
    inv = lax.rsqrt(jnp.mean(centered * centered, axis=-1, keepdims=True) + 1e-05)
    z = centered * inv
    return z * gain + shift, z, inv


def layer_norm_back(dh, z, inv, gain):
    dz = dh * gain
    dr = (dz - jnp.mean(dz, axis=-1, keepdims=True) - z * jnp.mean(dz * z, axis=-1, keepdims=True)) * inv
    return dr, jnp.sum(dh * z, axis=0), jnp.sum(dh, axis=0)


def exact_gelu(u):
    return jax.nn.gelu(u, approximate=False)


def heads(x, questions):
    return x.reshape(questions, x.shape[0] // questions, x.shape[1] // HEAD, HEAD)


def attend(q, k, v, questions, causal):
    qh, kh, vh = heads(q, questions), heads(k, questions), heads(v, questions)
    scores = jnp.einsum("bqhd,bkhd->bhqk", qh, kh, preferred_element_type=F32) * 0.125
    if causal:
        keep = jnp.arange(scores.shape[2])[:, None] >= jnp.arange(scores.shape[3])[None, :]
        scores = jnp.where(keep, scores, -1e30)
    probs = jax.nn.softmax(scores, axis=-1)
    mixed = jnp.einsum("bhqk,bkhd->bqhd", probs.astype(BF), vh, preferred_element_type=F32)
    return mixed.reshape(q.shape).astype(BF), probs


def attend_back(g, q, k, v, probs, questions):
    gh, qh, kh, vh = (heads(t, questions) for t in (g, q, k, v))
    dp = jnp.einsum("bqhd,bkhd->bhqk", gh, vh, preferred_element_type=F32)
    dv = jnp.einsum("bhqk,bqhd->bkhd", probs.astype(BF), gh, preferred_element_type=F32)
    ds = (probs * (dp - jnp.sum(dp * probs, axis=-1, keepdims=True))).astype(BF)
    dq = jnp.einsum("bhqk,bkhd->bqhd", ds, kh, preferred_element_type=F32) * 0.125
    dk = jnp.einsum("bhqk,bqhd->bkhd", ds, qh, preferred_element_type=F32) * 0.125
    return dq.reshape(q.shape).astype(BF), dk.reshape(k.shape).astype(BF), dv.reshape(v.shape).astype(BF)


def shards(
    inputs, memory, attn_weight, attn_out, ffn_in, ffn_out, attn_bias, norm_gain, norm_bias,
    bias_in, bias_out, embedding, targets, slot_counts, pad_mask, log_prior,
):
    n_pb, n_slot = lax.axis_size("pb"), lax.axis_size("slot")
    n_all = n_pb * n_slot
    teams = n_pb // TEAM
    me = lax.axis_index("pb")
    chip, core, team = (me % TEAM) // CORES, me % CORES, me // TEAM
    slot = lax.axis_index("slot")
    length, width = inputs.shape[2], inputs.shape[3]
    quarter = width // CHIPS

    def across_teams(w):
        return lax.all_gather(w, "pb", axis_index_groups=team_groups()) if teams > 1 else w[None]

    def natural(blocks):
        flat = blocks.reshape((TEAM,) + blocks.shape[2:])
        ordered = jnp.stack([at(flat, (core ^ c) * CHIPS + (chip ^ b)) for b in range(CHIPS) for c in range(CORES)])
        ordered = jnp.swapaxes(ordered, 0, 1)
        return ordered.reshape((-1,) + ordered.shape[3:])

    def column_shard(w):
        w = across_teams(w)
        pieces = jnp.moveaxis(w.reshape(w.shape[:-1] + (CHIPS, w.shape[-1] // CHIPS)), -2, 0)
        mine = [at(pieces, chip)]
        for k in range(1, CHIPS):
            mine.append(from_chip(at(pieces, chip ^ k), k))
        mine = jnp.stack(mine)
        return natural(jnp.stack([mine, from_core(mine)]))

    def all_rows(w):
        w = across_teams(w)
        mine = collect(w)
        return natural(jnp.stack([mine, from_core(mine)]))

    def chip_rows(w):
        other = from_core(w)
        pair = jnp.stack([w, other])
        return jnp.stack([at(pair, core), at(pair, 1 - core)]).reshape((-1,) + w.shape[1:])

    x_all = collect(inputs[0, 0]).reshape(CHIPS * length, width)
    w_cols = column_shard(attn_weight)
    m_all = collect(memory[0, 0]).reshape(-1, width)
    w_out = all_rows(attn_out)
    w_up = column_shard(ffn_in)
    if teams > 1:
        full_down = all_rows(ffn_out)
        w_down = lax.dynamic_slice_in_dim(full_down, chip * (full_down.shape[0] // CHIPS), full_down.shape[0] // CHIPS)
    else:
        w_down = chip_rows(ffn_out)
    out_mine = lax.dynamic_slice_in_dim(w_out, chip * quarter, quarter)

    def my_columns(b):
        return lax.dynamic_slice_in_dim(b, chip * (b.shape[0] // CHIPS), b.shape[0] // CHIPS)

    bias_cols = my_columns(attn_bias)

    def gather_columns(y):
        y = y.reshape(CHIPS, -1, y.shape[-1])
        got = []
        for k in range(CHIPS):
            r = from_chip(y, k) if k else y
            got.append(jnp.stack([r[k ^ p] for p in range(CHIPS)]))
        got = jnp.stack(got)
        cols = jnp.stack([at(got, chip ^ b) for b in range(CHIPS)])
        return jnp.moveaxis(cols, 0, -2).reshape(y.shape[0] * y.shape[1], -1)

    queries = (product(x_all, w_cols[:, 0]) + bias_cols[:, 0]).astype(BF)
    keys = product(x_all, w_cols[:, 1]).astype(BF)
    values = (product(x_all, w_cols[:, 2]) + bias_cols[:, 1]).astype(BF)
    cross_keys = product(m_all, w_cols[:, 4]).astype(BF)
    cross_values = (product(m_all, w_cols[:, 5]) + bias_cols[:, 4]).astype(BF)
    self_low, self_probs = attend(queries, keys, values, CHIPS, True)
    resid_one = x_all.astype(F32) + product(gather_columns(self_low), w_out[:, 0]) + attn_bias[:, 2]
    hidden_one, z_one, inv_one = layer_norm(resid_one, norm_gain[:, 0], norm_bias[:, 0])
    hidden_one_low = hidden_one.astype(BF)
    cross_queries = (product(hidden_one_low, w_cols[:, 3]) + bias_cols[:, 3]).astype(BF)
    cross_low, cross_probs = attend(cross_queries, cross_keys, cross_values, CHIPS, False)
    resid_two = hidden_one + product(gather_columns(cross_low), w_out[:, 1]) + attn_bias[:, 5]
    hidden_two, z_two, inv_two = layer_norm(resid_two, norm_gain[:, 1], norm_bias[:, 1])
    hidden_two_low = hidden_two.astype(BF)
    upward = product(hidden_two_low, w_up) + my_columns(bias_in)
    active, gelu_back = jax.vjp(exact_gelu, upward)
    active_low = active.astype(BF)
    branch = reduce_chips(product(active_low, w_down).reshape(CHIPS, length, width))
    resid_three = hidden_two[:length] + branch + bias_out
    hidden_three, z_three, inv_three = layer_norm(resid_three, norm_gain[:, 2], norm_bias[:, 2])
    final_low = hidden_three.astype(BF)

    vocab_rows = embedding.shape[0]
    plane = collect(final_low)
    plane = jnp.stack([plane, from_core(plane)]).reshape(TEAM, length, width)
    plane = across_teams(plane)
    questions = jnp.stack([(chip ^ k) * CORES + (core ^ d) for d in range(CORES) for k in range(CHIPS)])
    question_of = (jnp.arange(teams)[:, None] * TEAM + questions[None, :]).reshape(-1)
    if teams > 1:
        pass
    tokens = plane.reshape(-1, width)
    count = n_pb * length
    local_targets = targets - me * vocab_rows
    ids_here = local_targets[question_of].reshape(-1)
    scores = product_t(tokens, embedding)
    hit = ids_here[:, None] == jnp.arange(vocab_rows)[None, :]
    peak = jnp.max(scores, axis=1)
    total = jnp.sum(jnp.exp(scores - peak[:, None]), axis=1)
    block_norm = peak + jnp.log(total)
    block_pick = jnp.sum(jnp.where(hit, scores, 0.0), axis=1)
    place_of = jnp.argsort(question_of)
    stats = jnp.stack([block_norm, block_pick]).reshape(2, n_pb, length)[:, place_of]
    payload = jnp.concatenate([stats.reshape(-1), pad_mask[0].astype(F32), log_prior[0]])
    everyone = lax.all_to_all(
        jnp.broadcast_to(payload[None], (n_all, payload.shape[0])), ("slot", "pb"), 0, 0, tiled=True
    )
    split = 2 * n_pb * length
    got = everyone[:, :split].reshape(n_slot, n_pb, 2, n_pb, length)
    norms = jax.nn.logsumexp(got[:, :, 0], axis=1)
    picks = jnp.sum(got[:, :, 1], axis=1)
    masks = everyone[:n_pb, split : split + length]
    priors = everyone[:, split + length].reshape(n_slot, n_pb)
    usable = jnp.arange(n_slot)[:, None] < slot_counts[None, :]
    logp = picks - norms + priors[:, :, None]
    logp = jnp.where(usable[:, :, None], logp, -1e30)
    merged = jax.nn.logsumexp(logp, axis=0)
    token_grads = -masks[None] * jnp.where(usable[:, :, None], jnp.exp(logp - merged[None]), 0.0)
    token_logprob = at(merged, me)
    prior_grad = jnp.sum(at(at(token_grads, slot), me)).reshape(1, 1)

    def slot_view(values, s):
        return at(values, s)[question_of].reshape(-1)

    def logit_gradient(raw, is_hit, s):
        soft = jnp.exp(raw - slot_view(norms, s)[:, None])
        return (slot_view(token_grads, s)[:, None] * (jnp.where(is_hit, 1.0, 0.0) - soft)).astype(BF)

    logit_grad = logit_gradient(scores, hit, slot)
    partial = product(logit_grad, embedding).reshape(teams, TEAM, length, width)
    if teams > 1:
        partial = lax.psum_scatter(partial.astype(BF), "pb", axis_index_groups=team_groups(), tiled=False).astype(F32)
    else:
        partial = partial[0]
    pair = partial[:CHIPS] + from_core(partial[CHIPS:].astype(BF)).astype(F32)
    grad_final = reduce_chips(pair)

    grad_embedding = weight_product(logit_grad, tokens)
    for k in range(1, n_slot):
        others = from_slot(tokens, k)
        other_grad = logit_gradient(product_t(others, embedding), hit, (slot - k) % n_slot)
        grad_embedding = grad_embedding + weight_product(other_grad, others)

    dr_three, gain_three, shift_three = layer_norm_back(grad_final, z_three, inv_three, norm_gain[:, 2])
    e_three = dr_three.astype(BF)
    e_all = collect(e_three).reshape(-1, width)
    grad_down = weight_product(active_low, e_all)
    grad_active = product_t(e_all, w_down).astype(BF)
    grad_upward = gelu_back(grad_active.astype(F32))[0].astype(BF)
    grad_up = weight_product(hidden_two_low, grad_upward)
    sum_bias_in = jnp.sum(grad_upward.astype(F32), axis=0)
    dh_two = dr_three + reduce_chips(product_t(grad_upward, w_up).reshape(CHIPS, length, width))
    dr_two, gain_two, shift_two = layer_norm_back(dh_two, z_two[:length], inv_two[:length], norm_gain[:, 1])
    e_two = dr_two.astype(BF)
    e_all_two = collect(e_two).reshape(-1, width)
    grad_cross_out = weight_product(cross_low, e_all_two)
    grad_cross_mix = product_t(e_all_two, out_mine[:, 1]).astype(BF)
    dqc, dkc, dvc = attend_back(grad_cross_mix, cross_queries, cross_keys, cross_values, cross_probs, CHIPS)
    dh_one = dr_two + reduce_chips(product_t(dqc, w_cols[:, 3]).reshape(CHIPS, length, width))
    grad_passage = reduce_chips(
        (product_t(dkc, w_cols[:, 4]) + product_t(dvc, w_cols[:, 5])).reshape(CHIPS, -1, width)
    )
    dr_one, gain_one, shift_one = layer_norm_back(dh_one, z_one[:length], inv_one[:length], norm_gain[:, 0])
    e_one = dr_one.astype(BF)
    e_all_one = collect(e_one).reshape(-1, width)
    grad_self_out = weight_product(self_low, e_all_one)
    grad_self_mix = product_t(e_all_one, out_mine[:, 0]).astype(BF)
    dqs, dks, dvs = attend_back(grad_self_mix, queries, keys, values, self_probs, CHIPS)
    grad_source = dr_one + reduce_chips(
        (product_t(dqs, w_cols[:, 0]) + product_t(dks, w_cols[:, 1]) + product_t(dvs, w_cols[:, 2])).reshape(
            CHIPS, length, width
        )
    )

    slot_perm_up = lambda t: [(z, z + 1) for z in range(min(t, n_slot - 1))]
    slot_perm_down = lambda t: [(z, z - 1) for z in range(n_slot - 1, max(n_slot - 1 - t, 0), -1)]

    def reduce_slots(blocks):
        up = down = 0.0
        for t in range(1, n_slot):
            send = up + at(blocks, jnp.clip(n_slot - t + slot, 0, n_slot - 1))
            up = lax.ppermute(send.astype(BF), "slot", slot_perm_up(t)).astype(F32)
            send = down + at(blocks, jnp.clip(slot - n_slot + t, 0, n_slot - 1))
            down = lax.ppermute(send.astype(BF), "slot", slot_perm_down(t)).astype(F32)
        return at(blocks, slot) + up + down

    def reduce_core(blocks):
        return at(blocks, core) + from_core(at(blocks, 1 - core).astype(BF)).astype(F32)

    def over_teams(blocks):
        if teams == 1:
            return blocks[0]
        return lax.psum_scatter(blocks.astype(BF), "pb", axis_index_groups=team_groups(), tiled=False).astype(F32)

    def finish_columns(grad):
        cols = grad.shape[-1]
        rows = grad.shape[0] // n_all
        g = grad.reshape(n_slot, teams, CHIPS, CORES, rows, cols)
        g = over_teams(jnp.moveaxis(g, 1, 0))
        g = reduce_core(jnp.moveaxis(g, 2, 0))
        g = reduce_slots(g).astype(BF)
        got = [at(g, chip)] + [from_chip(at(g, chip ^ k), k) for k in range(1, CHIPS)]
        got = jnp.stack(got)
        ordered = jnp.stack([at(got, chip ^ b) for b in range(CHIPS)], axis=1)
        return ordered.reshape(rows, CHIPS * cols).astype(F32)

    def finish_rows(grad):
        rows = grad.shape[0] * CHIPS // n_all
        g = grad.reshape((teams, CHIPS, CORES, rows) + grad.shape[1:])
        g = over_teams(g)
        g = reduce_core(jnp.moveaxis(g, 1, 0))
        g = reduce_slots(g).astype(BF)
        pairs = []
        for s in range(n_slot):
            for i in range(n_pb):
                t, b, c = i // TEAM, (i % TEAM) // CORES, i % CORES
                pairs.append((s * n_pb + i, b * n_pb + t * TEAM + s * CORES + c))
        return lax.ppermute(g, ("slot", "pb"), pairs).astype(F32)

    out_up = finish_columns(grad_up)
    out_down = finish_rows(grad_down)
    out_cross = finish_rows(grad_cross_out)
    col_grads = [
        weight_product(hidden_one_low, dqc),
        weight_product(m_all, dkc),
        weight_product(m_all, dvc),
    ]
    out_cols_cross = [finish_columns(g) for g in col_grads]
    out_self = finish_rows(grad_self_out)
    out_cols_self = [finish_columns(weight_product(x_all, g)) for g in (dqs, dks, dvs)]
    out_attn = jnp.stack(out_cols_self + out_cols_cross, axis=1)
    out_outputs = jnp.stack([out_self, out_cross], axis=1)

    def spread(v):
        full = jnp.zeros((CHIPS, v.shape[0]), F32)
        return lax.dynamic_update_index_in_dim(full, v, chip, 0).reshape(-1)

    def total_rows(g):
        return jnp.sum(g.astype(F32), axis=0)

    small = jnp.stack(
        [
            spread(total_rows(dqs)),
            spread(total_rows(dvs)),
            total_rows(e_one),
            spread(total_rows(dqc)),
            spread(total_rows(dvc)),
            total_rows(e_two),
            gain_one,
            gain_two,
            gain_three,
            shift_one,
            shift_two,
            shift_three,
            total_rows(e_three),
        ]
    )
    rows = width // n_all
    small = jnp.moveaxis(small.reshape(-1, n_all, rows), 1, 0).reshape(n_all, -1)
    small = jnp.concatenate([small, spread(sum_bias_in).reshape(n_all, -1)], axis=1)
    small = jnp.sum(lax.all_to_all(small, ("slot", "pb"), 0, 0, tiled=True), axis=0)
    vectors = small[: 13 * rows].reshape(13, rows)
    return (
        token_logprob[None, :],
        grad_source[None, None],
        grad_passage[None, None],
        prior_grad,
        out_attn,
        out_outputs,
        out_up,
        out_down,
        vectors[:6].T,
        vectors[6:9].T,
        vectors[9:12].T,
        small[13 * rows :],
        vectors[12],
        grad_embedding,
    )


def solution(mesh):
    placed = (
        P("pb", "slot", None, None),
        P("pb", "slot", None, None),
        P("pb", None, None),
        P("pb", None, None),
        P("pb", None),
        P("pb", None),
        P(),
        P(),
        P(),
        P(),
        P(),
        P("pb", None),
        P(),
        P(),
        P("pb", None),
        P("pb", "slot"),
    )
    both = ("slot", "pb")
    return jax.shard_map(
        shards,
        mesh=mesh,
        in_specs=placed,
        out_specs=(
            P("pb", None),
            P("pb", "slot", None, None),
            P("pb", "slot", None, None),
            P("pb", "slot"),
            P(both, None, None),
            P(both, None, None),
            P(both, None),
            P(both, None),
            P(both, None),
            P(both, None),
            P(both, None),
            P(both),
            P(both),
            P("pb", None),
        ),
        check_vma=False,
    )
```

```python
import functools

import jax
import jax.numpy as jnp
from jax import lax
from jax.experimental import pallas as pl
from jax.experimental.pallas import tpu as pltpu
from jax.sharding import PartitionSpec as P

HEAD = 64
CHIPS = 4
CORES = 2
TEAM = CHIPS * CORES
BF = jnp.bfloat16
F32 = jnp.float32
TOKENS = 512
VOCAB_TILE = 512


def from_chip(x, k):
    pairs = []
    for i in range(lax.axis_size("pb")):
        place = i % TEAM
        pairs.append((i, i - place + ((place // CORES) ^ k) * CORES + place % CORES))
    return lax.ppermute(x, "pb", pairs)


def from_core(x):
    return lax.ppermute(x, "pb", [(i, i ^ 1) for i in range(lax.axis_size("pb"))])


def from_slot(x, k):
    size = lax.axis_size("slot")
    return lax.ppermute(x, "slot", [(i, (i + k) % size) for i in range(size)])


def across_slot(x, k):
    return lax.ppermute(x, "slot", [(i, i ^ k) for i in range(lax.axis_size("slot"))])


def same_place_groups():
    size = lax.axis_size("pb")
    return [[g * TEAM + j for g in range(size // TEAM)] for j in range(TEAM)]


def team_groups():
    size = lax.axis_size("pb")
    return [[g * TEAM + j for j in range(TEAM)] for g in range(size // TEAM)]


def others(x):
    return [from_chip(x, k) for k in range(1, CHIPS)]


def after(x, *earlier):
    return lax.optimization_barrier((x,) + earlier)[0]


def at(x, index):
    return lax.dynamic_index_in_dim(x, index, 0, False)


NN = (((1,), (0,)), ((), ()))
NT = (((1,), (1,)), ((), ()))
TN = (((0,), (0,)), ((), ()))


def dot(a, b, dims=NN):
    return lax.dot_general(a, b, dims, preferred_element_type=F32)


def place():
    j = lax.axis_index("pb") % TEAM
    return j // CORES, j % CORES


def rows_at(start, size, unit):
    return pl.ds(pl.multiple_of(start, unit), size)


MIB = 2**20


def limit(mib):
    return pltpu.CompilerParams(vmem_limit_bytes=min(60, mib) * MIB)


def work(us):
    return pl.CostEstimate(flops=int(us * 6e8), bytes_accessed=0, transcendentals=0)


def call(kernel, outs, *args, us=2.0):
    shapes = [jax.ShapeDtypeStruct(s, t) for s, t in outs]
    held = sum(a.size * a.dtype.itemsize for a in (*args, *shapes))
    params = limit(12 + held * 5 // 4 // MIB)
    return pl.pallas_call(kernel, out_shape=shapes, compiler_params=params, cost_estimate=work(us))(*args)


def in_hbm(x):
    return pltpu.with_memory_space_constraint(x, pltpu.HBM)


def norm_rows(r, gain, shift):
    centered = r - jnp.mean(r, axis=-1, keepdims=True)
    inv = lax.rsqrt(jnp.mean(centered * centered, axis=-1, keepdims=True) + 1e-05)
    z = centered * inv
    return z * gain + shift, z, inv


def norm_back(dh, z, inv, gain):
    dz = dh * gain
    return (dz - jnp.mean(dz, axis=-1, keepdims=True) - z * jnp.mean(dz * z, axis=-1, keepdims=True)) * inv


def lane_head(shape, keys):
    return lax.broadcasted_iota(jnp.int32, shape, 1) // keys


def per_head(x):
    head = lane_head(x.shape, HEAD)
    return jnp.concatenate([jnp.where(head == h, x, jnp.zeros_like(x)) for h in range(x.shape[1] // HEAD)], axis=0)


def own_heads(big, keys):
    count = big.shape[1] // HEAD
    head = lane_head((keys, big.shape[1]), HEAD)
    total = jnp.zeros((keys, big.shape[1]), F32)
    for h in range(count):
        total = total + jnp.where(head == h, big[h * keys : (h + 1) * keys], 0.0)
    return total


def head_probs(q, kbig, keys, causal):
    s = dot(q, kbig, NT) * 0.125
    head = lane_head(s.shape, keys)
    count = s.shape[1] // keys
    if causal:
        query = lax.broadcasted_iota(jnp.int32, s.shape, 0)
        key = lax.broadcasted_iota(jnp.int32, s.shape, 1) % keys
        s = jnp.where(query >= key, s, -1e30)
    peak = jnp.zeros_like(s)
    for h in range(count):
        m = jnp.max(jnp.where(head == h, s, -3e38), axis=1, keepdims=True)
        peak = jnp.where(head == h, m, peak)
    e = jnp.exp(s - peak)
    return e / head_sums(e, head, count)


def head_sums(x, head, count):
    total = jnp.zeros_like(x)
    for h in range(count):
        total = jnp.where(head == h, jnp.sum(jnp.where(head == h, x, 0.0), axis=1, keepdims=True), total)
    return total


def attend(q, k, v, causal):
    probs = head_probs(q, per_head(k), k.shape[0], causal)
    return dot(probs.astype(BF), per_head(v)).astype(BF)


def attend_back(g, q, k, v, causal):
    keys = k.shape[0]
    kbig, vbig = per_head(k), per_head(v)
    probs = head_probs(q, kbig, keys, causal)
    dp = dot(g, vbig, NT)
    head = lane_head(dp.shape, keys)
    ds = (probs * (dp - head_sums(dp * probs, head, dp.shape[1] // keys))).astype(BF)
    dq = dot(ds, kbig) * 0.125
    dk = own_heads(dot(ds, q, TN), keys) * 0.125
    dv = own_heads(dot(probs.astype(BF), g, TN), keys)
    return dq.astype(BF), dk.astype(BF), dv.astype(BF)


def pack_kernel(count, first, *refs):
    *rows_in, w_ref, o0, o1, o2, o3 = refs
    outs = (o0, o1, o2, o3)
    chip, _ = place()
    rows, quarter = w_ref.shape[1], w_ref.shape[2] // CHIPS
    for k in range(CHIPS):
        top = 0
        for x_ref in rows_in:
            x = x_ref[...]
            for b in range(CHIPS):
                outs[k][top : top + x.shape[0], :] = x[:, b * quarter : (b + 1) * quarter]
                top += x.shape[0]
        for j in range(count):
            outs[k][top : top + rows, :] = w_ref[first + j, :, rows_at((chip ^ k) * quarter, quarter, 128)]
            top += rows


def natural_columns(own, pair, w_out, top, count):
    chip, core = place()
    rows = (own[0].shape[0] - top) // count
    quarter = own[0].shape[1]
    for k in range(CHIPS):
        for refs, c in ((own, core), (pair, 1 - core)):
            start = (chip ^ k) * (CORES * rows) + c * rows
            for j in range(count):
                w_out[rows_at(start, rows, 16), j * quarter : (j + 1) * quarter] = refs[k][
                    top + j * rows : top + (j + 1) * rows, :
                ]


def half_columns(parts, out, top, count):
    chip, _ = place()
    rows = (parts[0].shape[0] - top) // count
    quarter = parts[0].shape[1]
    for k in range(CHIPS):
        for j in range(count):
            out[chip ^ k, :, j * quarter : (j + 1) * quarter] = parts[k][top + j * rows : top + (j + 1) * rows, :]


def whole_columns(mine, pair, out):
    _, core = place()
    rows = mine.shape[1]
    for b in range(CHIPS):
        for part, c in ((mine, core), (pair, 1 - core)):
            out[rows_at(b * CORES * rows + c * rows, rows, 16), :] = part[b]


def pair_rows(own, pair):
    _, core = place()
    a, b = own[...], pair[...]
    return jnp.concatenate([jnp.where(core == 0, a, b), jnp.where(core == 0, b, a)], axis=0)


def self_kernel(*refs):
    own, pair, (o_own, o_pair, vec) = refs[:4], refs[4:8], refs[8:11]
    x_out, w_out, q_out, k_out, v_out, o_out, wo_out, mine_out = refs[11:19]
    send = refs[19:]
    chip, _ = place()
    quarter = own[0].shape[1]
    length = x_out.shape[0] // CHIPS
    natural_columns(own, pair, w_out, CHIPS * length, 3)
    for k in range(CHIPS):
        for b in range(CHIPS):
            x_out[k * length : (k + 1) * length, b * quarter : (b + 1) * quarter] = own[k][b * length : (b + 1) * length, :]
    for j in range(2):
        wo_out[j] = pair_rows(o_own.at[j], o_pair.at[j])
    lanes = rows_at(chip * quarter, quarter, 128)
    y = dot(x_out[...], w_out[...])
    q = (y[:, :quarter] + vec[0:1, lanes]).astype(BF)
    k = y[:, quarter : 2 * quarter].astype(BF)
    v = (y[:, 2 * quarter :] + vec[1:2, lanes]).astype(BF)
    q_out[...], k_out[...], v_out[...] = q, k, v
    for p in range(CHIPS):
        s = slice(p * length, (p + 1) * length)
        o_out[s, :] = attend(q[s], k[s], v[s], True)
    split_rows(dot(o_out[...], wo_out[0]), mine_out, send)


def memory_half_kernel(*refs):
    parts, (m_out, w_out) = refs[:4], refs[4:]
    quarter = parts[0].shape[1]
    rows = m_out.shape[0] // CHIPS
    for k in range(CHIPS):
        for b in range(CHIPS):
            m_out[k * rows : (k + 1) * rows, b * quarter : (b + 1) * quarter] = parts[k][b * rows : (b + 1) * rows, :]
    half_columns(parts, w_out, CHIPS * rows, 3)


def memory_kernel(m, mine, pair, vec, w_out, k_out, v_out):
    chip, _ = place()
    quarter = k_out.shape[1]
    whole_columns(mine, pair, w_out)
    y = dot(m[...], w_out[:, quarter:])
    k_out[...] = y[:, :quarter].astype(BF)
    v_out[...] = (y[:, quarter:] + vec[4:5, rows_at(chip * quarter, quarter, 128)]).astype(BF)


def norm_kernel(rows, *refs):
    base, mine, r1, r2, r3, vec, h_out, low_out, z_out, inv_out = refs
    y = mine[...] + r1[...].astype(F32) + r2[...].astype(F32) + r3[...].astype(F32)
    r = base[...].astype(F32) + y + vec[rows[0] : rows[0] + 1, :]
    h, z, inv = norm_rows(r, vec[rows[1] : rows[1] + 1, :], vec[rows[2] : rows[2] + 1, :])
    h_out[...] = h
    low_out[...] = h.astype(BF)
    z_out[...] = z
    inv_out[...] = inv


def cross_kernel(*refs):
    parts, (wo, w_cols, keys, values, vec), (low_out, q_out, o_out, mine_out), send = refs[:4], refs[4:9], refs[9:13], refs[13:]
    chip, _ = place()
    quarter = keys.shape[1]
    length = parts[0].shape[0]
    memory = keys.shape[0] // CHIPS
    low = stack_rows(parts)
    low_out[...] = low
    q = (dot(low, w_cols[:, :quarter]) + vec[3:4, rows_at(chip * quarter, quarter, 128)]).astype(BF)
    q_out[...] = q
    for p in range(CHIPS):
        s, t = slice(p * length, (p + 1) * length), slice(p * memory, (p + 1) * memory)
        o_out[s, :] = attend(q[s], keys[t, :], values[t, :], False)
    split_rows(dot(o_out[...], wo[1]), mine_out, send)


def gelu_parts(u):
    phi = 0.5 * (1.0 + lax.erf(u * 0.7071067811865476))
    return phi


def up_half_kernel(*refs):
    half_columns(refs[:4], refs[4], 0, 1)


def ffn_kernel(*refs):
    parts, (up_mine, up_pair, down_own, down_pair, vec) = refs[:4], refs[4:9]
    low_out, u_out, a_out, up_out, down_out, mine_out = refs[9:15]
    send = refs[15:]
    chip, _ = place()
    whole_columns(up_mine, up_pair, up_out)
    down_out[...] = pair_rows(down_own, down_pair)
    low = stack_rows(parts)
    low_out[...] = low
    u = dot(low, up_out[...]) + vec[pl.ds(13 + chip, 1), :]
    u_out[...] = u
    a_out[...] = (u * gelu_parts(u)).astype(BF)
    split_rows(dot(a_out[...], down_out[...]), mine_out, send)


def stack_kernel(*refs):
    n = refs[0].shape[0]
    for k in range(CHIPS):
        refs[-1][k * n : (k + 1) * n, :] = refs[k][...]


def logits_kernel(length, h0_ref, h1_ref, ids_ref, own_ref, e_ref, l_ref, pay_ref, h_ref, m_ref, s_ref, p_ref):
    i = pl.program_id(0)
    half = h0_ref.shape[0]

    @pl.when(i == 0)
    def _():
        h_ref[:half, :] = h0_ref[...]
        h_ref[half:, :] = h1_ref[...]
        m_ref[...] = jnp.full_like(m_ref, -3e38)
        s_ref[...] = jnp.zeros_like(s_ref)
        p_ref[...] = jnp.zeros_like(p_ref)

    x = dot(e_ref[...], h_ref[...], NT)
    l_ref[...] = x
    entry = lax.broadcasted_iota(jnp.int32, x.shape, 0) + i * x.shape[0]
    peak = jnp.maximum(m_ref[0:1, :], jnp.max(x, axis=0, keepdims=True))
    total = s_ref[0:1, :] * jnp.exp(m_ref[0:1, :] - peak) + jnp.sum(jnp.exp(x - peak), axis=0, keepdims=True)
    pick = p_ref[0:1, :] + jnp.sum(jnp.where(entry == ids_ref[...], x, 0.0), axis=0, keepdims=True)
    m_ref[0:1, :], s_ref[0:1, :], p_ref[0:1, :] = peak, total, pick

    @pl.when(i == pl.num_programs(0) - 1)
    def _():
        pay_ref[...] = jnp.zeros_like(pay_ref)
        pay_ref[pay_ref.shape[0] - 8 : pay_ref.shape[0] - 7, :] = own_ref[...]
        norm = peak + jnp.log(total)
        lane = lax.broadcasted_iota(jnp.int32, (1, 2 * length), 1)
        chip, core = place()
        for n in range(2 * half // (2 * length)):
            s = slice(n * 2 * length, (n + 1) * 2 * length)
            d, rest = divmod(2 * n * length, half)
            first = rest // length
            team, k = first // CHIPS, first % CHIPS
            rows = (
                jnp.where(lane < length, norm[:, s], pltpu.roll(pick[:, s], length, 1)),
                jnp.where(lane < length, pltpu.roll(norm[:, s], length, 1), pick[:, s]),
            )
            for j in range(2):
                q = team * TEAM + (chip ^ (k + j)) * CORES + (core ^ d)
                pay_ref[pl.ds(q, 1), :] = rows[j]


def logits(held, pair, ids, own_row, embedding, length, questions):
    half, vocab, width = held.shape[0], embedding.shape[0], embedding.shape[1]
    tile = min(VOCAB_TILE, vocab)
    stat = pltpu.VMEM((8, 2 * half), F32)
    whole = pl.BlockSpec(memory_space=pltpu.VMEM)
    return pl.pallas_call(
        functools.partial(logits_kernel, length),
        grid=(vocab // tile,),
        in_specs=[whole, whole, whole, whole, pl.BlockSpec((tile, width), lambda i: (i, 0))],
        out_specs=[
            pl.BlockSpec((tile, 2 * half), lambda i: (i, 0)),
            pl.BlockSpec((questions + 8, 2 * length), lambda i: (0, 0)),
        ],
        out_shape=[
            pltpu.HBM((vocab, 2 * half), F32),
            jax.ShapeDtypeStruct((questions + 8, 2 * length), F32),
        ],
        scratch_shapes=[pltpu.VMEM((2 * half, width), BF), stat, stat, stat],
        compiler_params=limit(14 + 24 * half * tile // MIB),
        cost_estimate=work(10),
    )(held, pair, ids, own_row, embedding)


def merge_kernel(length, all_ref, counts_ref, ids_ref, rows_out, logp_out, prior_out, n_ref, g_ref):
    n_slot, n_pb = n_ref.shape[0], n_ref.shape[1]
    chip, core = place()
    me, slot = lax.axis_index("pb"), lax.axis_index("slot")
    lane = lax.broadcasted_iota(jnp.int32, (1, 2 * length), 1)
    logps, priors = [], None
    for s in range(n_slot):
        blocks = [all_ref[s * n_pb + j, :n_pb, :] for j in range(n_pb)]
        peak = blocks[0]
        for b in blocks[1:]:
            peak = jnp.maximum(peak, b)
        total = jnp.zeros_like(peak)
        pick = jnp.zeros_like(peak)
        for b in blocks:
            total = total + jnp.exp(b - peak)
            pick = pick + b
        norm = peak + jnp.log(total)
        n_ref[s] = norm
        own = jnp.concatenate([all_ref[s * n_pb + j, n_pb : n_pb + 1, :] for j in range(n_pb)], axis=0)
        mask = own
        prior = pltpu.roll(own, length, 1)
        logp = pltpu.roll(pick, length, 1) - norm + prior
        logps.append(jnp.where(counts_ref[...] > s, logp, -1e30))
    top = logps[0]
    for p in logps[1:]:
        top = jnp.maximum(top, p)
    total = jnp.zeros_like(top)
    for p in logps:
        total = total + jnp.exp(p - top)
    merged = top + jnp.log(total)
    for s in range(n_slot):
        g_ref[s] = jnp.where(counts_ref[...] > s, -mask * jnp.exp(logps[s] - merged), 0.0)
    n_rows = n_ref.shape[1]
    row = lax.broadcasted_iota(jnp.int32, merged.shape, 0)
    logp_out[...] = jnp.sum(jnp.where(row == me, merged, 0.0), axis=0, keepdims=True)
    own_grad = jnp.where(lane < length, g_ref[slot, pl.ds(me, 1), :], 0.0)
    prior_out[...] = jnp.sum(own_grad, axis=1, keepdims=True)
    rows_out[...] = jnp.zeros_like(rows_out)
    half = rows_out.shape[3]
    for k in range(n_slot):
        s = lax.rem(slot + (n_slot - k), n_slot)
        for d in range(CORES):
            for n in range(half // (2 * length)):
                team, c = (2 * n) // CHIPS, (2 * n) % CHIPS
                q = [team * TEAM + (chip ^ (c + j)) * CORES + (core ^ d) for j in range(2)]
                t = slice(n * 2 * length, (n + 1) * 2 * length)
                for r, (first, second) in enumerate(
                    (
                        (n_ref[s, pl.ds(q[0], 1), :], n_ref[s, pl.ds(q[1], 1), :]),
                        (g_ref[s, pl.ds(q[0], 1), :], g_ref[s, pl.ds(q[1], 1), :]),
                        (ids_ref[pl.ds(q[0], 1), :], ids_ref[pl.ds(q[1], 1), :]),
                    )
                ):
                    rows_out[k, d, r : r + 1, t] = jnp.where(lane < length, first, pltpu.roll(second, length, 1))


def merge(everyone, counts, ids, length, n_slot, n_pb, half):
    held = pltpu.VMEM((n_slot, n_pb, 2 * length), F32)
    return pl.pallas_call(
        functools.partial(merge_kernel, length),
        out_shape=[
            jax.ShapeDtypeStruct((n_slot, CORES, 8, half), F32),
            jax.ShapeDtypeStruct((1, 2 * length), F32),
            jax.ShapeDtypeStruct((1, 1), F32),
        ],
        scratch_shapes=[held, held],
        compiler_params=limit(16 + 2 * everyone.size * 4 // MIB),
        cost_estimate=work(2),
    )(everyone, counts, ids)


def logit_gradient(x, rows, first):
    entry = (lax.broadcasted_iota(jnp.int32, x.shape, 0) + first).astype(F32)
    hit = jnp.where(entry == rows[2:3, :], 1.0, 0.0)
    return (rows[1:2, :] * (hit - jnp.exp(x - rows[0:1, :]))).astype(BF)


def state_grad_kernel(l_ref, rows_ref, e_ref, own_ref, pair_ref, acc_ref):
    i = pl.program_id(0)
    half = own_ref.shape[0]

    @pl.when(i == 0)
    def _():
        acc_ref[...] = jnp.zeros_like(acc_ref)

    tile = l_ref.shape[0]
    d = [logit_gradient(l_ref[:, c * half : (c + 1) * half], rows_ref[0, c], i * tile) for c in range(CORES)]
    acc_ref[...] += dot(jnp.concatenate(d, axis=1), e_ref[...], TN)

    @pl.when(i == pl.num_programs(0) - 1)
    def _():
        own_ref[...] = acc_ref[:half, :].astype(own_ref.dtype)
        pair_ref[...] = acc_ref[half:, :].astype(BF)


def state_grad(scores, rows, embedding, own_type):
    vocab, count = scores.shape
    width = embedding.shape[1]
    half = count // CORES
    tile = min(2 * VOCAB_TILE, vocab)
    last = pl.BlockSpec((half, width), lambda i: (0, 0))
    return pl.pallas_call(
        state_grad_kernel,
        grid=(vocab // tile,),
        in_specs=[
            pl.BlockSpec((tile, count), lambda i: (i, 0)),
            pl.BlockSpec((1,) + rows.shape[1:], lambda i: (0, 0, 0, 0)),
            pl.BlockSpec((tile, width), lambda i: (i, 0)),
        ],
        out_specs=[last, last],
        out_shape=[jax.ShapeDtypeStruct((half, width), own_type), jax.ShapeDtypeStruct((half, width), BF)],
        scratch_shapes=[pltpu.VMEM((count, width), F32)],
        compiler_params=limit(16 + 20 * half * tile // MIB + count * width * 4 // MIB),
        cost_estimate=work(11),
    )(scores, rows, embedding)


def embedding_kernel(base, states, rows_ref, *refs):
    h_refs, e_ref, o_ref = refs[:states], refs[states], refs[-1]
    first = base + pl.program_id(0) * e_ref.shape[0]
    e = e_ref[...]
    total = None
    for n in range(0, states, CORES):
        k = n // CORES
        for top in range(0, h_refs[n].shape[0], TOKENS // CORES):
            t = slice(top, top + TOKENS // CORES)
            h = jnp.concatenate([h_refs[n][t, :], h_refs[n + 1][t, :]], axis=0)
            rows = jnp.concatenate([rows_ref[k, 0, :, t], rows_ref[k, 1, :, t]], axis=1)
            d = logit_gradient(dot(e, h, NT), rows, first)
            term = dot(d, h)
            total = term if total is None else total + term
    o_ref[...] = total


def embedding_piece(rows, states, embedding, held, piece, size):
    width = embedding.shape[1]
    tile = min(VOCAB_TILE, size)
    steps = size // tile
    ahead = [] if held is None else [held]
    whole = pl.BlockSpec(memory_space=pltpu.VMEM)
    block = pl.BlockSpec((tile, width), lambda i: (piece * steps + i, 0))
    return pl.pallas_call(
        functools.partial(embedding_kernel, piece * size, len(states)),
        grid=(steps,),
        in_specs=[whole] * (1 + len(states)) + [block] + [pl.BlockSpec(memory_space=pl.ANY)] * len(ahead),
        out_specs=block,
        out_shape=pltpu.HBM(embedding.shape, F32),
        input_output_aliases={2 + len(states): 0} if ahead else {},
        compiler_params=limit(24 if rows.shape[3] <= TOKENS else 24),
        cost_estimate=work(14 * size / 1024),
    )(rows, *states, embedding, *ahead)


def add_kernel(mine, got, own_out, *send):
    length = own_out.shape[0]
    for k in range(CHIPS):
        s = slice(k * length, (k + 1) * length)
        y = mine[s, :] + got[s, :].astype(F32)
        if k == 0:
            own_out[...] = y
        else:
            send[k - 1][...] = y.astype(BF)


def norm_back_kernel(row, has_base, *refs):
    base = refs[0] if has_base else None
    mine, r1, r2, r3, z, inv, vec, dr_out, e_out, sums_out = refs[1 if has_base else 0 :]
    dh = mine[...] + r1[...].astype(F32) + r2[...].astype(F32) + r3[...].astype(F32)
    if has_base:
        dh = dh + base[...]
    dr = norm_back(dh, z[...], inv[...], vec[6 + row : 7 + row, :])
    e = dr.astype(BF)
    dr_out[...] = dr
    e_out[...] = e
    sums_out[...] = jnp.zeros_like(sums_out)
    sums_out[0:1, :] = jnp.sum(dh * z[...], axis=0, keepdims=True)
    sums_out[1:2, :] = jnp.sum(dh, axis=0, keepdims=True)
    sums_out[2:3, :] = jnp.sum(e.astype(F32), axis=0, keepdims=True)


def stack_rows(parts):
    return jnp.concatenate([p[...] for p in parts], axis=0)


def split_rows(y, mine_out, send):
    length = mine_out.shape[0]
    mine_out[...] = y[:length]
    for k in range(1, CHIPS):
        send[k - 1][...] = y[k * length : (k + 1) * length].astype(BF)


def column_sum(y):
    return jnp.sum(y.astype(F32), axis=0, keepdims=True)


def ffn_back_kernel(*refs):
    parts, (u_ref, up, down), (e_out, du_out, sum_out, mine_out), send = refs[:4], refs[4:7], refs[7:11], refs[11:]
    e = stack_rows(parts)
    e_out[...] = e
    da = dot(e, down[...], NT).astype(BF).astype(F32)
    u = u_ref[...]
    slope = gelu_parts(u) + u * (jnp.exp(-0.5 * u * u) * 0.3989422804014327)
    du = (da * slope).astype(BF)
    du_out[...] = du
    sum_out[...] = column_sum(du)
    split_rows(dot(du, up[...], NT), mine_out, send)


def pick_core(g, mine_out, other_out, top):
    _, core = place()
    lo, hi = g[:, :, 0], g[:, :, 1]
    n = lo.shape[1] * lo.shape[2]
    mine = jnp.where(core == 0, lo, hi).reshape(CHIPS, n, g.shape[-1])
    other = jnp.where(core == 0, hi, lo).reshape(CHIPS, n, g.shape[-1])
    mine_out[:, top : top + n, :] = mine.astype(BF)
    other_out[:, top : top + n, :] = other.astype(BF)


def place_columns(g, mine_out, other_out, top):
    unit = g.shape[0] // (CHIPS * CHIPS * CORES)
    pick_core(g.reshape(CHIPS, CHIPS, CORES, unit, g.shape[1]), mine_out, other_out, top)


def place_rows(g, mine_out, other_out, top):
    unit = g.shape[0] // (CHIPS * CORES)
    pick_core(g.reshape(CHIPS, 1, CORES, unit, g.shape[1]), mine_out, other_out, top)


def place_row_blocks(g, mine_out, other_out, top, lanes):
    unit = g.shape[0] // (CHIPS * CORES)
    for b in range(g.shape[1] // lanes):
        place_rows(g[:, b * lanes : (b + 1) * lanes], mine_out, other_out, top + b * unit)


def ffn_grads_kernel(low, du, a, e, mine_out, other_out):
    g = dot(low[...], du[...], TN)
    place_columns(g, mine_out, other_out, 0)
    g2 = dot(a[...], e[...], TN)
    place_rows(g2, mine_out, other_out, g.shape[0] // (CHIPS * CORES))


def cross_back_kernel(*refs):
    parts, (w_mine, w_cols, q_ref, k_ref, v_ref) = refs[:4], refs[4:9]
    (e_out, dq_out, dk_out, dv_out, mine_out), send = refs[9:14], refs[14:]
    quarter = q_ref.shape[1]
    length, memory = q_ref.shape[0] // CHIPS, k_ref.shape[0] // CHIPS
    e = stack_rows(parts)
    e_out[...] = e
    g = dot(e, w_mine[1], NT).astype(BF)
    for p in range(CHIPS):
        s, t = slice(p * length, (p + 1) * length), slice(p * memory, (p + 1) * memory)
        dq_out[s, :], dk_out[t, :], dv_out[t, :] = attend_back(g[s], q_ref[s, :], k_ref[t, :], v_ref[t, :], False)
    split_rows(dot(dq_out[...], w_cols[:, :quarter], NT), mine_out, send)


def cross_grads_kernel(low, dq, m, dk, dv, o, e, mine_out, other_out, sums_out):
    n = low.shape[1] // (CHIPS * CORES)
    for j, (a, g) in enumerate(((low, dq), (m, dk), (m, dv))):
        place_columns(dot(a[...], g[...], TN), mine_out, other_out, j * n)
    place_row_blocks(dot(o[...], e[...], TN), mine_out, other_out, 3 * n, dq.shape[1])
    sums_out[...] = jnp.zeros_like(sums_out)
    sums_out[0:1, :] = column_sum(dq[...])
    sums_out[1:2, :] = column_sum(dv[...])


def memory_back_kernel(dk, dv, w_cols, mine_out, *send):
    quarter = dk.shape[1]
    y = dot(dk[...], w_cols[:, quarter : 2 * quarter], NT) + dot(dv[...], w_cols[:, 2 * quarter :], NT)
    split_rows(y, mine_out, send)


def self_back_kernel(*refs):
    parts, (w_mine, q_ref, k_ref, v_ref), (e_out, d_out) = refs[:4], refs[4:8], refs[8:]
    quarter = q_ref.shape[1]
    length = q_ref.shape[0] // CHIPS
    e = stack_rows(parts)
    e_out[...] = e
    g = dot(e, w_mine[0], NT).astype(BF)
    for p in range(CHIPS):
        s = slice(p * length, (p + 1) * length)
        dq, dk, dv = attend_back(g[s], q_ref[s, :], k_ref[s, :], v_ref[s, :], True)
        d_out[s, :quarter] = dq
        d_out[s, quarter : 2 * quarter] = dk
        d_out[s, 2 * quarter :] = dv


def self_grads_kernel(x, d, o, e, mine_out, other_out, sums_out):
    quarter = d.shape[1] // 3
    n = x.shape[1] // (CHIPS * CORES)
    g = dot(x[...], d[...], TN)
    for j in range(3):
        place_columns(g[:, j * quarter : (j + 1) * quarter], mine_out, other_out, j * n)
    place_row_blocks(dot(o[...], e[...], TN), mine_out, other_out, 3 * n, quarter)
    sums_out[...] = jnp.zeros_like(sums_out)
    sums_out[0:1, :] = column_sum(d[:, :quarter])
    sums_out[1:2, :] = column_sum(d[:, 2 * quarter :])


def source_back_kernel(d, w_cols, mine_out, *send):
    split_rows(dot(d[...], w_cols[...], NT), mine_out, send)


def total_kernel(has_base, *refs):
    refs, out = refs[:-1], refs[-1]
    y = refs[0][...]
    for r in refs[1:]:
        y = y + r[...].astype(F32)
    out[...] = y


def slot_first_kernel(mine, got, keep_out, send_out):
    z = lax.axis_index("slot")
    for n, out in ((0, keep_out), (1, send_out)):
        for h in range(2):
            b = z ^ (n + 2 * h)
            out[h] = (mine[b].astype(F32) + got[b].astype(F32)).astype(BF)


def slot_second_kernel(keep, got, keep_out, send_out):
    keep_out[...] = (keep[0].astype(F32) + got[0].astype(F32)).astype(BF)
    send_out[...] = (keep[1].astype(F32) + got[1].astype(F32)).astype(BF)


def column_pieces_kernel(count, keep, got, *outs):
    *pieces, rest = outs
    chip, _ = place()
    unit = pieces[0].shape[0] // count
    y = keep[...].astype(F32) + got[...].astype(F32)
    top = count * CHIPS * unit
    rest[...] = y[top:].astype(BF)
    hold = y[:top].astype(BF).reshape(count, CHIPS, unit, y.shape[1])
    for k in range(CHIPS):
        for j in range(count):
            block = jnp.zeros((unit, y.shape[1]), BF)
            for b in range(CHIPS):
                block = jnp.where((chip ^ k) == b, hold[j, b], block)
            pieces[k][j * unit : (j + 1) * unit, :] = block


def small_kernel(s_sums, c_sums, sum_in, one, two, three, out):
    chip, _ = place()
    places = out.shape[0]
    width, quarter = one.shape[1], s_sums.shape[1]
    unit = width // places
    chunk = quarter * CHIPS // places

    def spread(row):
        zero = jnp.zeros_like(row)
        return jnp.concatenate([jnp.where(chip == b, row, zero) for b in range(CHIPS)], axis=1)

    rows = [
        spread(s_sums[0:1, :]), spread(s_sums[1:2, :]), one[2:3, :], spread(c_sums[0:1, :]), spread(c_sums[1:2, :]),
        two[2:3, :], one[0:1, :], two[0:1, :], three[0:1, :], one[1:2, :], two[1:2, :], three[1:2, :], three[2:3, :],
    ]
    rows = jnp.concatenate(rows + [jnp.zeros((3, width), F32)], axis=0)
    wide = sum_in.shape[1] * CHIPS // places
    last = sum_in[...]
    out[...] = jnp.zeros_like(out)
    for n in range(places):
        out[n, :, :unit] = rows[:, n * unit : (n + 1) * unit]
        b, inner = divmod(n * wide, sum_in.shape[1])
        out[n, 13:14, :wide] = jnp.where(chip == b, last[:, inner : inner + wide], 0.0)


def small_final_kernel(x, attn_out, gain_out, shift_out, in_out, bias_out):
    total = x[0]
    for n in range(1, x.shape[0]):
        total = total + x[n]
    unit = attn_out.shape[0]
    columns = jnp.transpose(total)
    attn_out[...] = columns[:unit, 0:6]
    gain_out[...] = columns[:unit, 6:9]
    shift_out[...] = columns[:unit, 9:12]
    bias_out[...] = total[12:13, :unit]
    in_out[...] = total[13:14, : in_out.shape[1]]


def attn_out_kernel(*refs):
    own, cross, out = refs[:4], refs[4:8], refs[8]
    chip, _ = place()
    unit, quarter = out.shape[1], own[0].shape[1]
    for k in range(CHIPS):
        lanes = rows_at((chip ^ k) * quarter, quarter, 128)
        for j in range(3):
            out[j, :, lanes] = own[k][j * unit : (j + 1) * unit, :].astype(F32)
            out[3 + j, :, lanes] = cross[k][j * unit : (j + 1) * unit, :].astype(F32)


def up_out_kernel(p0, p1, p2, p3, out):
    chip, _ = place()
    quarter = p0.shape[1]
    for k, p in enumerate((p0, p1, p2, p3)):
        out[:, rows_at((chip ^ k) * quarter, quarter, 128)] = p[...].astype(F32)


def shards(
    inputs, memory, attn_weight, attn_out, ffn_in, ffn_out, attn_bias, norm_gain, norm_bias,
    bias_in, bias_out, embedding, targets, slot_counts, pad_mask, log_prior,
):
    n_pb, n_slot = lax.axis_size("pb"), lax.axis_size("slot")
    n_all = n_pb * n_slot
    teams = n_pb // TEAM
    me = lax.axis_index("pb")
    length, width = inputs.shape[2], inputs.shape[3]
    passage = memory.shape[2]
    quarter = width // CHIPS
    unit = width // (TEAM * n_slot)
    vocab_rows = embedding.shape[0]
    embedding = in_hbm(embedding)

    def team_rows(w):
        if teams == 1:
            return w
        w = lax.all_gather(w, "pb", axis=0, tiled=True)
        n = w.shape[0] // TEAM
        return lax.dynamic_slice_in_dim(w, (me % TEAM) * n, n)

    x, m = inputs[0, 0], memory[0, 0]
    attn_w = jnp.moveaxis(team_rows(attn_weight), 1, 0)
    out_w = jnp.moveaxis(team_rows(attn_out), 1, 0)
    up_w = team_rows(ffn_in)
    down_w = team_rows(ffn_out)
    rows = attn_w.shape[1]
    ff = up_w.shape[1] // CHIPS
    vec = jnp.concatenate(
        [attn_bias.T, norm_gain.T, norm_bias.T, bias_out[None], bias_in.reshape(CHIPS, -1)], axis=0
    )
    ids = (targets - me * vocab_rows).astype(jnp.int32)
    own_row = jnp.concatenate([pad_mask.astype(F32), jnp.broadcast_to(log_prior, (1, length))], axis=1)

    block = (length, width)
    every = (CHIPS * length, width)
    cols = (CHIPS * length, quarter)
    m_cols = (CHIPS * passage, quarter)
    sends = [(block, BF)] * 3

    def give(send):
        return [from_chip(send[k - 1], k) for k in range(1, CHIPS)]

    first = call(functools.partial(pack_kernel, 3, 0), [((CHIPS * length + 3 * rows, quarter), BF)] * CHIPS, x, attn_w)
    got_first = [first[0]] + give(first[1:])
    pair_first = [from_core(g) for g in got_first]
    out_pair = from_core(out_w)
    down_pair = from_core(down_w)
    second = call(functools.partial(pack_kernel, 3, 3), [((CHIPS * passage + 3 * rows, quarter), BF)] * CHIPS, m, attn_w)
    third = call(functools.partial(pack_kernel, 1, 0), [((rows, ff), BF)] * CHIPS, up_w[None])
    got_second = [second[0]] + give(list(lax.optimization_barrier((*second[1:], *got_first[1:]))[:3]))

    x_all, w_self, queries, keys, values, mixed, w_out, mine, *send = call(
        self_kernel,
        [(every, BF), ((width, 3 * quarter), BF)] + [(cols, BF)] * 4 + [((2, quarter, width), BF), (block, F32)] + sends,
        *got_first, *pair_first, out_w, out_pair, vec,
    )
    got = give(send)
    m_all, w_half = call(
        memory_half_kernel, [((CHIPS * passage, width), BF), ((CHIPS, rows, 3 * quarter), BF)], *got_second
    )
    w_half_pair = from_core(w_half)
    norm_outs = [(block, F32), (block, BF), (block, F32), ((length, 1), F32)]
    hidden_one, low_one, z_one, inv_one = call(
        functools.partial(norm_kernel, (2, 6, 9)), norm_outs, x, mine, *got, vec, us=1
    )
    got_low = [low_one] + others(low_one)
    w_cross, cross_keys, cross_values = call(
        memory_kernel, [((width, 3 * quarter), BF)] + [(m_cols, BF)] * 2, m_all, w_half, w_half_pair, vec
    )
    got_third = [third[0]] + give(list(lax.optimization_barrier((*third[1:], *got_low[1:]))[:3]))
    low_one_all, cross_queries, cross_mixed, mine, *send = call(
        cross_kernel, [(every, BF), (cols, BF), (cols, BF), (block, F32)] + sends,
        *got_low, w_out, w_cross, cross_keys, cross_values, vec,
    )
    got = give(send)
    (up_half,) = call(up_half_kernel, [((CHIPS, rows, ff), BF)], *got_third)
    up_half_pair = from_core(up_half)
    hidden_two, low_two, z_two, inv_two = call(
        functools.partial(norm_kernel, (5, 7, 10)), norm_outs, hidden_one, mine, *got, vec, us=1
    )
    got_low = [low_two] + others(low_two)
    low_two_all, upward, active, w_up, w_down, mine, *send = call(
        ffn_kernel,
        [(every, BF), ((CHIPS * length, ff), F32), ((CHIPS * length, ff), BF), ((width, ff), BF), ((ff, width), BF), (block, F32)]
        + sends,
        *got_low, up_half, up_half_pair, down_w, down_pair, vec,
    )
    got = give(send)
    _, final_low, z_three, inv_three = call(
        functools.partial(norm_kernel, (12, 8, 11)), norm_outs, hidden_two, mine, *got, vec, us=1
    )

    (held,) = call(stack_kernel, [(every, BF)], final_low, *others(final_low), us=1)
    pair = from_core(held)

    def all_teams(h):
        return lax.all_gather(h, "pb", axis_index_groups=same_place_groups(), axis=0, tiled=True) if teams > 1 else h

    states = [all_teams(held), all_teams(pair)]
    half = teams * CHIPS * length
    chip, core = place()
    order = [
        t * TEAM + (chip ^ k) * CORES + (core ^ d) for d in range(CORES) for t in range(teams) for k in range(CHIPS)
    ]
    ids_row = jnp.concatenate([lax.dynamic_slice_in_dim(ids, q, 1) for q in order], axis=1)
    scores, payload = logits(*states, ids_row, own_row, embedding, length, n_pb)
    everyone = lax.all_to_all(
        jnp.broadcast_to(payload[None], (n_all,) + payload.shape), ("slot", "pb"), 0, 0, tiled=True
    )
    ids_wide = jnp.pad(ids.astype(F32), ((0, 0), (0, length)))
    token_rows, token_logprob, prior_grad = merge(
        everyone, slot_counts.astype(jnp.int32)[:, None], ids_wide, length, n_slot, n_pb, half
    )
    for k in range(1, n_slot):
        h = from_slot(after(held, pair), k)
        states += [all_teams(h), all_teams(from_core(h))]

    def home(partial):
        if teams == 1:
            return partial
        return lax.psum_scatter(partial, "pb", axis_index_groups=same_place_groups(), scatter_dimension=0, tiled=True)

    own_part, for_pair = state_grad(scores, token_rows, embedding, F32)
    own_part, got_pair = home(own_part), from_core(home(for_pair))
    mine, *send = call(add_kernel, [(block, F32)] + sends, own_part, got_pair, us=1)
    got = give(send)

    piece_count = 8
    piece_size = vocab_rows // piece_count
    made = []

    def fill(got, *wait):
        n = len(made)
        if n == piece_count:
            return got
        rows_in = after(token_rows, *wait)
        done = embedding_piece(rows_in, states, embedding, made[-1] if made else None, n, piece_size)
        *got, done = lax.optimization_barrier((*got, done))
        made.append(done)
        return list(got)

    grads = [(block, F32), (block, BF), ((8, width), F32)]
    dr_three, e_three, sums_three = call(
        functools.partial(norm_back_kernel, 2, False), grads, mine, *got, z_three, inv_three, vec, us=1
    )
    got_e = [e_three] + fill(others(e_three), e_three)
    e_all, du, sum_in, mine, *send = call(
        ffn_back_kernel,
        [(every, BF), ((CHIPS * length, ff), BF), ((1, ff), F32), (block, F32)] + sends,
        *got_e, upward, w_up, w_down,
    )
    got = give(send)
    f_shape = (n_slot, CHIPS * unit + ff // TEAM, width)
    f_mine, f_other = call(ffn_grads_kernel, [(f_shape, BF)] * 2, low_two_all, du, active, e_all, us=3)
    f_got = from_core(f_other)
    got = fill(got, send[0], f_other)
    dr_two, e_two, sums_two = call(
        functools.partial(norm_back_kernel, 1, True), grads, dr_three, mine, *got, z_two, inv_two, vec, us=1
    )
    got_e = others(e_two)
    half_shape = (2,) + f_shape[1:]
    f_keep, f_send = call(slot_first_kernel, [(half_shape, BF)] * 2, f_mine, f_got)
    f_got = across_slot(f_send, 1)
    got_e = [e_two] + fill(got_e, e_two, f_send)
    e_all_two, dqc, dkc, dvc, mine, *send = call(
        cross_back_kernel,
        [(every, BF), (cols, BF), (m_cols, BF), (m_cols, BF), (block, F32)] + sends,
        *got_e, w_out, w_cross, cross_queries, cross_keys, cross_values, us=5,
    )
    got = give(send)
    g_shape = (n_slot, 4 * CHIPS * unit, quarter)
    c_mine, c_other, c_sums = call(
        cross_grads_kernel, [(g_shape, BF)] * 2 + [((8, quarter), F32)],
        low_one_all, dqc, m_all, dkc, dvc, cross_mixed, e_all_two,
    )
    c_got = from_core(c_other)
    f_keep, f_send = call(slot_second_kernel, [(f_shape[1:], BF)] * 2, f_keep, f_got)
    f_got = across_slot(f_send, 2)
    got = fill(got, send[0], c_other)
    dr_one, e_one, sums_one = call(
        functools.partial(norm_back_kernel, 0, True), grads, dr_two, mine, *got, z_one, inv_one, vec, us=1
    )
    got_e = others(e_one)
    m_block = (passage, width)
    m_mine, *m_send = call(memory_back_kernel, [(m_block, F32)] + [(m_block, BF)] * 3, dkc, dvc, w_cross)
    m_got = give(m_send)
    g_half = (2,) + g_shape[1:]
    c_keep, c_send = call(slot_first_kernel, [(g_half, BF)] * 2, c_mine, c_got)
    c_got = across_slot(c_send, 1)
    got_e = [e_one] + fill(got_e, e_one, c_send)
    e_all_one, d_self = call(
        self_back_kernel, [(every, BF), ((CHIPS * length, 3 * quarter), BF)], *got_e, w_out, queries, keys, values, us=4
    )
    s_mine, s_other, s_sums = call(
        self_grads_kernel, [(g_shape, BF)] * 2 + [((8, quarter), F32)], x_all, d_self, mixed, e_all_one
    )
    s_got = from_core(s_other)
    mine, *send = call(source_back_kernel, [(block, F32)] + sends, d_self, w_self)
    got = give(send)
    s_keep, s_send = call(slot_first_kernel, [(g_half, BF)] * 2, s_mine, s_got)
    s_got = across_slot(s_send, 1)
    c_keep, c_send = call(slot_second_kernel, [(g_shape[1:], BF)] * 2, c_keep, c_got)
    c_got = across_slot(c_send, 2)
    (s_got,) = fill([s_got], s_send)
    s_keep, s_send = call(slot_second_kernel, [(g_shape[1:], BF)] * 2, s_keep, s_got)
    s_got = across_slot(s_send, 2)
    (grad_source,) = call(functools.partial(total_kernel, True), [(block, F32)], mine, dr_one, *got, us=1)
    (grad_passage,) = call(functools.partial(total_kernel, False), [(m_block, F32)], m_mine, *m_got, us=1)

    lanes = max(128, bias_in.shape[0] // n_all)
    (small,) = call(
        small_kernel, [((n_all, 16, lanes), F32)], s_sums, c_sums, sum_in, sums_one, sums_two, sums_three, us=1
    )
    small = lax.all_to_all(small, ("slot", "pb"), 0, 0, tiled=True)
    final = width // n_all
    vectors = call(
        small_final_kernel,
        [((final, 6), F32), ((final, 3), F32), ((final, 3), F32), ((1, bias_in.shape[0] // n_all), F32), ((1, final), F32)],
        small, us=1,
    )
    while len(made) < piece_count:
        (s_got,) = fill([s_got], s_send)

    def settle(g):
        if teams == 1:
            return g
        g = lax.psum(g, "pb", axis_index_groups=same_place_groups())
        g = lax.all_gather(g, "pb", axis_index_groups=team_groups(), axis=0, tiled=True)
        n = g.shape[0] // n_pb
        return lax.dynamic_slice_in_dim(g, me * n, n)

    def to_owner(g):
        pairs = []
        for s in range(n_slot):
            for i in range(n_pb):
                t, b, c = i // TEAM, (i % TEAM) // CORES, i % CORES
                pairs.append((s * n_pb + i, b * n_pb + t * TEAM + s * CORES + c))
        return lax.ppermute(g, ("slot", "pb"), pairs)

    def column_pieces(count, keep, got, n, cols):
        rest = keep.shape[0] - count * CHIPS * n
        *piece, rest = call(
            functools.partial(column_pieces_kernel, count),
            [((count * n, cols), BF)] * CHIPS + [((rest, cols), BF)], keep, got,
        )
        return [piece[0]] + give(piece[1:]), rest

    f_pieces, f_rest = column_pieces(1, f_keep, f_got, unit, width)
    c_pieces, c_rest = column_pieces(3, c_keep, c_got, unit, quarter)
    s_pieces, s_rest = column_pieces(3, s_keep, s_got, unit, quarter)
    (out_up,) = call(up_out_kernel, [((unit, up_w.shape[1]), F32)], *f_pieces, us=1)
    (out_attn,) = call(attn_out_kernel, [((6, unit, width), F32)], *s_pieces, *c_pieces, us=1)
    out_attn = settle(jnp.moveaxis(out_attn, 0, 1))
    out_up = settle(out_up)
    out_down = settle(to_owner(f_rest).astype(F32))
    outs = to_owner(jnp.stack([s_rest, c_rest])).astype(F32).reshape(2, CHIPS, unit, quarter)
    out_outputs = settle(jnp.moveaxis(outs, 2, 0).reshape(unit, 2, width))
    return (
        token_logprob[:, :length],
        grad_source[None, None],
        grad_passage[None, None],
        prior_grad,
        out_attn,
        out_outputs,
        out_up,
        out_down,
        vectors[0],
        vectors[1],
        vectors[2],
        vectors[3][0],
        vectors[4][0],
        made[-1],
    )


def solution(mesh):
    placed = (
        P("pb", "slot", None, None),
        P("pb", "slot", None, None),
        P("pb", None, None),
        P("pb", None, None),
        P("pb", None),
        P("pb", None),
        P(),
        P(),
        P(),
        P(),
        P(),
        P("pb", None),
        P(),
        P(),
        P("pb", None),
        P("pb", "slot"),
    )
    both = ("slot", "pb")
    return jax.shard_map(
        shards,
        mesh=mesh,
        in_specs=placed,
        out_specs=(
            P("pb", None),
            P("pb", "slot", None, None),
            P("pb", "slot", None, None),
            P("pb", "slot"),
            P(both, None, None),
            P(both, None, None),
            P(both, None),
            P(both, None),
            P(both, None),
            P(both, None),
            P(both, None),
            P(both),
            P(both),
            P("pb", None),
        ),
        check_vma=False,
    )
```

```python
import functools

import jax
import jax.numpy as jnp
from jax import lax
from jax.experimental import pallas as pl
from jax.experimental.pallas import tpu as pltpu
from jax.sharding import PartitionSpec as P

HEAD = 64
CHIPS = 4
CORES = 2
TEAM = CHIPS * CORES
SLOTS = 4
BF = jnp.bfloat16
F32 = jnp.float32
TOKENS = 512
VOCAB_TILE = 512


def from_chip(x, k):
    pairs = []
    for i in range(lax.axis_size("pb")):
        place = i % TEAM
        pairs.append((i, i - place + ((place // CORES) ^ k) * CORES + place % CORES))
    return lax.ppermute(x, "pb", pairs)


def from_core(x):
    return lax.ppermute(x, "pb", [(i, i ^ 1) for i in range(lax.axis_size("pb"))])


def across_slot(x, k):
    return lax.ppermute(x, "slot", [(i, i ^ k) for i in range(lax.axis_size("slot"))])


def same_place_groups():
    size = lax.axis_size("pb")
    return [[g * TEAM + j for g in range(size // TEAM)] for j in range(TEAM)]


def team_groups():
    size = lax.axis_size("pb")
    return [[g * TEAM + j for j in range(TEAM)] for g in range(size // TEAM)]


def others(x):
    return [from_chip(x, k) for k in range(1, CHIPS)]


def tie(*values):
    return list(lax.optimization_barrier(values))


def across_slots(x):
    return lax.all_to_all(x, "slot", 0, 0, tiled=True)


def at(x, index):
    return lax.dynamic_index_in_dim(x, index, 0, False)


NN = (((1,), (0,)), ((), ()))
NT = (((1,), (1,)), ((), ()))
TN = (((0,), (0,)), ((), ()))


def dot(a, b, dims=NN):
    return lax.dot_general(a, b, dims, preferred_element_type=F32)


def place():
    j = lax.axis_index("pb") % TEAM
    return j // CORES, j % CORES


def rows_at(start, size, unit):
    return pl.ds(pl.multiple_of(start, unit), size)


MIB = 2**20


def limit(mib):
    return pltpu.CompilerParams(vmem_limit_bytes=min(60, mib) * MIB)


def work(us):
    return pl.CostEstimate(flops=int(us * 1e9), bytes_accessed=0, transcendentals=0)


def call(kernel, outs, *args, us=2.0, far=False):
    shapes = [jax.ShapeDtypeStruct(*o) for o in outs]
    held = sum(a.size * a.dtype.itemsize for a in (*args, *shapes))
    params = limit(8 + held * 5 // 4 // MIB)
    places = [pltpu.HBM(*o) for o in outs] if far else shapes
    results = pl.pallas_call(kernel, out_shape=places, compiler_params=params, cost_estimate=work(us))(*args)
    return [in_hbm(r) for r in results] if far else results


def in_hbm(x):
    return pltpu.with_memory_space_constraint(x, pltpu.HBM)


def norm_rows(r, gain, shift):
    centered = r - jnp.mean(r, axis=-1, keepdims=True)
    inv = lax.rsqrt(jnp.mean(centered * centered, axis=-1, keepdims=True) + 1e-05)
    z = centered * inv
    return z * gain + shift, z, inv


def norm_back(dh, z, inv, gain):
    dz = dh * gain
    return (dz - jnp.mean(dz, axis=-1, keepdims=True) - z * jnp.mean(dz * z, axis=-1, keepdims=True)) * inv


def lane_head(shape, keys):
    return lax.broadcasted_iota(jnp.int32, shape, 1) // keys


def per_head(x):
    head = lane_head(x.shape, HEAD)
    return jnp.concatenate([jnp.where(head == h, x, jnp.zeros_like(x)) for h in range(x.shape[1] // HEAD)], axis=0)


def own_heads(big, keys):
    count = big.shape[1] // HEAD
    head = lane_head((keys, big.shape[1]), HEAD)
    total = jnp.zeros((keys, big.shape[1]), F32)
    for h in range(count):
        total = total + jnp.where(head == h, big[h * keys : (h + 1) * keys], 0.0)
    return total


def head_probs(q, kbig, keys, causal):
    s = dot(q, kbig, NT) * 0.125
    head = lane_head(s.shape, keys)
    count = s.shape[1] // keys
    if causal:
        query = lax.broadcasted_iota(jnp.int32, s.shape, 0)
        key = lax.broadcasted_iota(jnp.int32, s.shape, 1) % keys
        s = jnp.where(query >= key, s, -1e30)
    peak = jnp.zeros_like(s)
    for h in range(count):
        m = jnp.max(jnp.where(head == h, s, -3e38), axis=1, keepdims=True)
        peak = jnp.where(head == h, m, peak)
    e = jnp.exp(s - peak)
    return e / head_sums(e, head, count)


def head_sums(x, head, count):
    total = jnp.zeros_like(x)
    for h in range(count):
        total = jnp.where(head == h, jnp.sum(jnp.where(head == h, x, 0.0), axis=1, keepdims=True), total)
    return total


def attend(q, k, v, causal):
    probs = head_probs(q, per_head(k), k.shape[0], causal)
    return dot(probs.astype(BF), per_head(v)).astype(BF)


def attend_back(g, q, k, v, causal):
    keys = k.shape[0]
    kbig, vbig = per_head(k), per_head(v)
    probs = head_probs(q, kbig, keys, causal)
    dp = dot(g, vbig, NT)
    head = lane_head(dp.shape, keys)
    ds = (probs * (dp - head_sums(dp * probs, head, dp.shape[1] // keys))).astype(BF)
    dq = dot(ds, kbig) * 0.125
    dk = own_heads(dot(ds, q, TN), keys) * 0.125
    dv = own_heads(dot(probs.astype(BF), g, TN), keys)
    return dq.astype(BF), dk.astype(BF), dv.astype(BF)


def pack_kernel(count, first, *refs):
    *rows_in, w_ref, o0, o1, o2, o3 = refs
    outs = (o0, o1, o2, o3)
    chip, _ = place()
    rows, quarter = w_ref.shape[1], w_ref.shape[2] // CHIPS
    for k in range(CHIPS):
        top = 0
        for x_ref in rows_in:
            x = x_ref[...]
            for b in range(CHIPS):
                outs[k][top : top + x.shape[0], :] = x[:, b * quarter : (b + 1) * quarter]
                top += x.shape[0]
        for j in range(count):
            outs[k][top : top + rows, :] = w_ref[first + j, :, rows_at((chip ^ k) * quarter, quarter, 128)]
            top += rows


def natural_columns(own, pair, w_out, top, count):
    chip, core = place()
    rows = w_out.shape[0] // TEAM
    quarter = own[0].shape[1]
    for k in range(CHIPS):
        for refs, c in ((own, core), (pair, 1 - core)):
            start = (chip ^ k) * (CORES * rows) + c * rows
            for j in range(count):
                w_out[rows_at(start, rows, 16), j * quarter : (j + 1) * quarter] = refs[k][
                    top + j * rows : top + (j + 1) * rows, :
                ]


def half_columns(parts, out, top, count):
    chip, _ = place()
    rows = (parts[0].shape[0] - top) // count
    quarter = parts[0].shape[1]
    for k in range(CHIPS):
        for j in range(count):
            out[chip ^ k, :, j * quarter : (j + 1) * quarter] = parts[k][top + j * rows : top + (j + 1) * rows, :]


def whole_columns(mine, pair, out):
    _, core = place()
    rows = mine.shape[1]
    for b in range(CHIPS):
        for part, c in ((mine, core), (pair, 1 - core)):
            out[rows_at(b * CORES * rows + c * rows, rows, 16), :] = part[b]


def pair_rows(own, pair):
    _, core = place()
    a, b = own[...], pair[...]
    return jnp.concatenate([jnp.where(core == 0, a, b), jnp.where(core == 0, b, a)], axis=0)


def self_kernel(*refs):
    own, pair, (o_own, o_pair, vec) = refs[:4], refs[4:8], refs[8:11]
    x_out, w_out, q_out, k_out, v_out, o_out, wo_out, mine_out = refs[11:19]
    send = refs[19:]
    chip, _ = place()
    quarter = own[0].shape[1]
    length = x_out.shape[0] // CHIPS
    natural_columns(own, pair, w_out, CHIPS * length, 3)
    for k in range(CHIPS):
        for b in range(CHIPS):
            x_out[k * length : (k + 1) * length, b * quarter : (b + 1) * quarter] = own[k][b * length : (b + 1) * length, :]
    for j in range(2):
        wo_out[j] = pair_rows(o_own.at[j], o_pair.at[j])
    lanes = rows_at(chip * quarter, quarter, 128)
    y = dot(x_out[...], w_out[...])
    q = (y[:, :quarter] + vec[0:1, lanes]).astype(BF)
    k = y[:, quarter : 2 * quarter].astype(BF)
    v = (y[:, 2 * quarter :] + vec[1:2, lanes]).astype(BF)
    q_out[...], k_out[...], v_out[...] = q, k, v
    for p in range(CHIPS):
        s = slice(p * length, (p + 1) * length)
        o_out[s, :] = attend(q[s], k[s], v[s], True)
    split_rows(dot(o_out[...], wo_out[0]), mine_out, send)


def half_kernel(*refs):
    half_columns(refs[:4], refs[4], 0, 3)


def memory_kernel(*refs):
    mem, own, pair, vec, (m_out, w_out, k_out, v_out) = refs[:4], refs[4:8], refs[8:12], refs[12], refs[13:]
    chip, _ = place()
    quarter = k_out.shape[1]
    natural_columns(own, pair, w_out, own[0].shape[0] - 3 * w_out.shape[0] // TEAM, 3)
    m_out[...] = stack_rows(mem)
    y = dot(m_out[...], w_out[:, quarter:])
    k_out[...] = y[:, :quarter].astype(BF)
    v_out[...] = (y[:, quarter:] + vec[4:5, rows_at(chip * quarter, quarter, 128)]).astype(BF)


def norm_kernel(rows, *refs):
    base, mine, r1, r2, r3, vec, h_out, low_out, z_out, inv_out = refs
    y = mine[...] + r1[...].astype(F32) + r2[...].astype(F32) + r3[...].astype(F32)
    r = base[...].astype(F32) + y + vec[rows[0] : rows[0] + 1, :]
    h, z, inv = norm_rows(r, vec[rows[1] : rows[1] + 1, :], vec[rows[2] : rows[2] + 1, :])
    h_out[...] = h
    low_out[...] = h.astype(BF)
    z_out[...] = z
    inv_out[...] = inv


def cross_kernel(*refs):
    parts, (wo, w_cols, keys, values, vec), (low_out, q_out, o_out, mine_out), send = refs[:4], refs[4:9], refs[9:13], refs[13:]
    chip, _ = place()
    quarter = keys.shape[1]
    length = parts[0].shape[0]
    memory = keys.shape[0] // CHIPS
    low = stack_rows(parts)
    low_out[...] = low
    q = (dot(low, w_cols[:, :quarter]) + vec[3:4, rows_at(chip * quarter, quarter, 128)]).astype(BF)
    q_out[...] = q
    for p in range(CHIPS):
        s, t = slice(p * length, (p + 1) * length), slice(p * memory, (p + 1) * memory)
        o_out[s, :] = attend(q[s], keys[t, :], values[t, :], False)
    split_rows(dot(o_out[...], wo[1]), mine_out, send)


def gelu_parts(u):
    phi = 0.5 * (1.0 + lax.erf(u * 0.7071067811865476))
    return phi


def up_half_kernel(*refs):
    half_columns(refs[:4], refs[4], 0, 1)


def ffn_kernel(*refs):
    parts, (up_mine, up_pair, down_own, down_pair, vec) = refs[:4], refs[4:9]
    low_out, u_out, a_out, up_out, down_out, mine_out = refs[9:15]
    send = refs[15:]
    chip, _ = place()
    whole_columns(up_mine, up_pair, up_out)
    down_out[...] = pair_rows(down_own, down_pair)
    low = stack_rows(parts)
    low_out[...] = low
    u = dot(low, up_out[...]) + vec[pl.ds(13 + chip, 1), :]
    u_out[...] = u
    a_out[...] = (u * gelu_parts(u)).astype(BF)
    split_rows(dot(a_out[...], down_out[...]), mine_out, send)


def stack_kernel(r0, r1, r2, r3, out, spread_out):
    n = r0.shape[0]
    for k, part in enumerate((r0, r1, r2, r3)):
        out[k * n : (k + 1) * n, :] = part[...]
        for slot in range(SLOTS):
            spread_out[slot, k * n : (k + 1) * n, :] = part[...]


def logits_kernel(length, h0_ref, h1_ref, ids_ref, own_ref, e_ref, l_ref, pay_ref, h_ref, m_ref, s_ref, p_ref):
    i = pl.program_id(0)
    half = h0_ref.shape[0]

    @pl.when(i == 0)
    def _():
        h_ref[:half, :] = h0_ref[...]
        h_ref[half:, :] = h1_ref[...]
        m_ref[...] = jnp.full_like(m_ref, -3e38)
        s_ref[...] = jnp.zeros_like(s_ref)
        p_ref[...] = jnp.zeros_like(p_ref)

    x = dot(e_ref[...], h_ref[...], NT)
    l_ref[...] = x
    entry = lax.broadcasted_iota(jnp.int32, x.shape, 0) + i * x.shape[0]
    peak = jnp.maximum(m_ref[0:1, :], jnp.max(x, axis=0, keepdims=True))
    total = s_ref[0:1, :] * jnp.exp(m_ref[0:1, :] - peak) + jnp.sum(jnp.exp(x - peak), axis=0, keepdims=True)
    pick = p_ref[0:1, :] + jnp.sum(jnp.where(entry == ids_ref[...], x, 0.0), axis=0, keepdims=True)
    m_ref[0:1, :], s_ref[0:1, :], p_ref[0:1, :] = peak, total, pick

    @pl.when(i == pl.num_programs(0) - 1)
    def _():
        pay_ref[...] = jnp.zeros_like(pay_ref)
        pay_ref[pay_ref.shape[0] - 8 : pay_ref.shape[0] - 7, :] = own_ref[...]
        norm = peak + jnp.log(total)
        lane = lax.broadcasted_iota(jnp.int32, (1, 2 * length), 1)
        chip, core = place()
        for n in range(2 * half // (2 * length)):
            s = slice(n * 2 * length, (n + 1) * 2 * length)
            d, rest = divmod(2 * n * length, half)
            first = rest // length
            team, k = first // CHIPS, first % CHIPS
            rows = (
                jnp.where(lane < length, norm[:, s], pltpu.roll(pick[:, s], length, 1)),
                jnp.where(lane < length, pltpu.roll(norm[:, s], length, 1), pick[:, s]),
            )
            for j in range(2):
                q = team * TEAM + (chip ^ (k + j)) * CORES + (core ^ d)
                pay_ref[pl.ds(q, 1), :] = rows[j]


def logits(held, pair, ids, own_row, embedding, length, questions):
    half, vocab, width = held.shape[0], embedding.shape[0], embedding.shape[1]
    tile = min(2 * VOCAB_TILE, vocab)
    stat = pltpu.VMEM((8, 2 * half), F32)
    whole = pl.BlockSpec(memory_space=pltpu.VMEM)
    return pl.pallas_call(
        functools.partial(logits_kernel, length),
        grid=(vocab // tile,),
        in_specs=[whole, whole, whole, whole, pl.BlockSpec((tile, width), lambda i: (i, 0))],
        out_specs=[
            pl.BlockSpec((tile, 2 * half), lambda i: (i, 0)),
            pl.BlockSpec((questions + 8, 2 * length), lambda i: (0, 0)),
        ],
        out_shape=[
            pltpu.HBM((vocab, 2 * half), F32),
            jax.ShapeDtypeStruct((questions + 8, 2 * length), F32),
        ],
        scratch_shapes=[pltpu.VMEM((2 * half, width), BF), stat, stat, stat],
        compiler_params=limit(14 + 24 * half * tile // MIB),
        cost_estimate=work(10),
    )(held, pair, ids, own_row, embedding)


def merge_kernel(length, all_ref, counts_ref, ids_ref, rows_out, own_out, logp_out, prior_out, n_ref, g_ref):
    n_slot, n_pb = n_ref.shape[0], n_ref.shape[1]
    chip, core = place()
    me, slot = lax.axis_index("pb"), lax.axis_index("slot")
    lane = lax.broadcasted_iota(jnp.int32, (1, 2 * length), 1)
    logps, priors = [], None
    for s in range(n_slot):
        blocks = [all_ref[s * n_pb + j, :n_pb, :] for j in range(n_pb)]
        peak = blocks[0]
        for b in blocks[1:]:
            peak = jnp.maximum(peak, b)
        total = jnp.zeros_like(peak)
        pick = jnp.zeros_like(peak)
        for b in blocks:
            total = total + jnp.exp(b - peak)
            pick = pick + b
        norm = peak + jnp.log(total)
        n_ref[s] = norm
        own = jnp.concatenate([all_ref[s * n_pb + j, n_pb : n_pb + 1, :] for j in range(n_pb)], axis=0)
        mask = own
        prior = pltpu.roll(own, length, 1)
        logp = pltpu.roll(pick, length, 1) - norm + prior
        logps.append(jnp.where(counts_ref[...] > s, logp, -1e30))
    top = logps[0]
    for p in logps[1:]:
        top = jnp.maximum(top, p)
    total = jnp.zeros_like(top)
    for p in logps:
        total = total + jnp.exp(p - top)
    merged = top + jnp.log(total)
    for s in range(n_slot):
        g_ref[s] = jnp.where(counts_ref[...] > s, -mask * jnp.exp(logps[s] - merged), 0.0)
    n_rows = n_ref.shape[1]
    row = lax.broadcasted_iota(jnp.int32, merged.shape, 0)
    logp_out[...] = jnp.sum(jnp.where(row == me, merged, 0.0), axis=0, keepdims=True)
    own_grad = jnp.where(lane < length, g_ref[slot, pl.ds(me, 1), :], 0.0)
    prior_out[...] = jnp.sum(own_grad, axis=1, keepdims=True)
    rows_out[...] = jnp.zeros_like(rows_out)
    half = rows_out.shape[3]
    for s in range(n_slot):
        for d in range(CORES):
            for n in range(half // (2 * length)):
                team, c = (2 * n) // CHIPS, (2 * n) % CHIPS
                q = [team * TEAM + (chip ^ (c + j)) * CORES + (core ^ d) for j in range(2)]
                t = slice(n * 2 * length, (n + 1) * 2 * length)
                for r, (first, second) in enumerate(
                    (
                        (n_ref[s, pl.ds(q[0], 1), :], n_ref[s, pl.ds(q[1], 1), :]),
                        (g_ref[s, pl.ds(q[0], 1), :], g_ref[s, pl.ds(q[1], 1), :]),
                        (ids_ref[pl.ds(q[0], 1), :], ids_ref[pl.ds(q[1], 1), :]),
                    )
                ):
                    rows_out[s, d, r : r + 1, t] = jnp.where(lane < length, first, pltpu.roll(second, length, 1))
    own_out[0] = rows_out[slot]


def merge(everyone, counts, ids, length, n_slot, n_pb, half):
    held = pltpu.VMEM((n_slot, n_pb, 2 * length), F32)
    return pl.pallas_call(
        functools.partial(merge_kernel, length),
        out_shape=[
            jax.ShapeDtypeStruct((n_slot, CORES, 8, half), F32),
            jax.ShapeDtypeStruct((1, CORES, 8, half), F32),
            jax.ShapeDtypeStruct((1, 2 * length), F32),
            jax.ShapeDtypeStruct((1, 1), F32),
        ],
        scratch_shapes=[held, held],
        compiler_params=limit(16 + 2 * everyone.size * 4 // MIB),
        cost_estimate=work(2),
    )(everyone, counts, ids)


def logit_gradient(x, rows, first):
    entry = (lax.broadcasted_iota(jnp.int32, x.shape, 0) + first).astype(F32)
    hit = jnp.where(entry == rows[2:3, :], 1.0, 0.0)
    return (rows[1:2, :] * (hit - jnp.exp(x - rows[0:1, :]))).astype(BF)


def state_grad_kernel(l_ref, rows_ref, e_ref, own_ref, pair_ref, d_ref, acc_ref):
    i = pl.program_id(0)
    half = own_ref.shape[0]

    @pl.when(i == 0)
    def _():
        acc_ref[...] = jnp.zeros_like(acc_ref)

    tile = l_ref.shape[0]
    d = [logit_gradient(l_ref[:, c * half : (c + 1) * half], rows_ref[0, c], i * tile) for c in range(CORES)]
    d_ref[...] = jnp.concatenate(d, axis=1)
    acc_ref[...] += dot(d_ref[...], e_ref[...], TN)

    @pl.when(i == pl.num_programs(0) - 1)
    def _():
        own_ref[...] = acc_ref[:half, :].astype(own_ref.dtype)
        pair_ref[...] = acc_ref[half:, :].astype(BF)


def state_grad(scores, rows, embedding, own_type):
    vocab, count = scores.shape
    width = embedding.shape[1]
    half = count // CORES
    tile = min(2 * VOCAB_TILE, vocab)
    last = pl.BlockSpec((half, width), lambda i: (0, 0))
    return pl.pallas_call(
        state_grad_kernel,
        grid=(vocab // tile,),
        in_specs=[
            pl.BlockSpec((tile, count), lambda i: (i, 0)),
            pl.BlockSpec((1,) + rows.shape[1:], lambda i: (0, 0, 0, 0)),
            pl.BlockSpec((tile, width), lambda i: (i, 0)),
        ],
        out_specs=[last, last, pl.BlockSpec((tile, count), lambda i: (i, 0))],
        out_shape=[
            jax.ShapeDtypeStruct((half, width), own_type),
            jax.ShapeDtypeStruct((half, width), BF),
            pltpu.HBM((vocab, count), BF),
        ],
        scratch_shapes=[pltpu.VMEM((count, width), F32)],
        compiler_params=limit(16 + 20 * half * tile // MIB + count * width * 4 // MIB),
        cost_estimate=work(11),
    )(in_hbm(scores), rows, embedding)


def own_embedding_kernel(d_ref, own_ref, pair_ref, *refs):
    half = own_ref.shape[0]
    refs[-1][...] = dot(d_ref[:, :half], own_ref[...]) + dot(d_ref[:, half:], pair_ref[...])


def own_embedding(d, own, pair, held, piece, count):
    vocab, tokens = d.shape
    tile = min(VOCAB_TILE, vocab // count)
    steps = vocab // count // tile
    ahead = [] if held is None else [held]
    whole = pl.BlockSpec(memory_space=pltpu.VMEM)
    shape = (vocab, own.shape[1])
    return pl.pallas_call(
        own_embedding_kernel,
        grid=(steps,),
        in_specs=[pl.BlockSpec((tile, tokens), lambda i: (piece * steps + i, 0)), whole, whole]
        + [pl.BlockSpec(memory_space=pl.ANY)] * len(ahead),
        out_specs=pl.BlockSpec((tile, shape[1]), lambda i: (piece * steps + i, 0)),
        out_shape=pltpu.HBM(shape, F32),
        input_output_aliases={3: 0} if ahead else {},
        compiler_params=limit(14),
        cost_estimate=work(1),
    )(d, own, pair, *ahead)


def embedding_kernel(base, rows_ref, own_ref, pair_ref, e_ref, held_ref, o_ref):
    first = base + pl.program_id(0) * e_ref.shape[0]
    e = e_ref[...]
    slot = lax.axis_index("slot")
    total = held_ref[...]
    for k in range(1, own_ref.shape[0]):
        n = slot ^ k
        for top in range(0, own_ref.shape[1], TOKENS // CORES):
            t = slice(top, top + TOKENS // CORES)
            h = jnp.concatenate([own_ref[n, t, :], pair_ref[n, t, :]], axis=0)
            rows = jnp.concatenate([rows_ref[n, 0, :, t], rows_ref[n, 1, :, t]], axis=1)
            total = total + dot(logit_gradient(dot(e, h, NT), rows, first), h)
    o_ref[...] = total


def embedding_piece(rows, states, embedding, held, first, size):
    width = embedding.shape[1]
    tile = min(VOCAB_TILE, size)
    steps = size // tile
    whole = pl.BlockSpec(memory_space=pltpu.VMEM)
    block = pl.BlockSpec((tile, width), lambda i: (first // tile + i, 0))
    return pl.pallas_call(
        functools.partial(embedding_kernel, first),
        grid=(steps,),
        in_specs=[whole, whole, whole, block, block],
        out_specs=block,
        out_shape=pltpu.HBM(embedding.shape, F32),
        input_output_aliases={4: 0},
        compiler_params=limit(24),
        cost_estimate=work(3 * size / 1024),
    )(rows, *states, embedding, held)


def add_kernel(mine, got, own_out, *send):
    length = own_out.shape[0]
    for k in range(CHIPS):
        s = slice(k * length, (k + 1) * length)
        y = mine[s, :] + got[s, :].astype(F32)
        if k == 0:
            own_out[...] = y
        else:
            send[k - 1][...] = y.astype(BF)


def norm_back_kernel(row, has_base, *refs):
    base = refs[0] if has_base else None
    mine, r1, r2, r3, z, inv, vec, dr_out, e_out, sums_out = refs[1 if has_base else 0 :]
    dh = mine[...] + r1[...].astype(F32) + r2[...].astype(F32) + r3[...].astype(F32)
    if has_base:
        dh = dh + base[...]
    dr = norm_back(dh, z[...], inv[...], vec[6 + row : 7 + row, :])
    e = dr.astype(BF)
    dr_out[...] = dr
    e_out[...] = e
    sums_out[...] = jnp.zeros_like(sums_out)
    sums_out[0:1, :] = jnp.sum(dh * z[...], axis=0, keepdims=True)
    sums_out[1:2, :] = jnp.sum(dh, axis=0, keepdims=True)
    sums_out[2:3, :] = jnp.sum(e.astype(F32), axis=0, keepdims=True)


def stack_rows(parts):
    return jnp.concatenate([p[...] for p in parts], axis=0)


def split_rows(y, mine_out, send):
    length = mine_out.shape[0]
    mine_out[...] = y[:length]
    for k in range(1, CHIPS):
        send[k - 1][...] = y[k * length : (k + 1) * length].astype(BF)


def column_sum(y):
    return jnp.sum(y.astype(F32), axis=0, keepdims=True)


def ffn_back_kernel(*refs):
    parts, (u_ref, up, down), (e_out, du_out, sum_out, mine_out), send = refs[:4], refs[4:7], refs[7:11], refs[11:]
    e = stack_rows(parts)
    e_out[...] = e
    da = dot(e, down[...], NT).astype(BF).astype(F32)
    u = u_ref[...]
    slope = gelu_parts(u) + u * (jnp.exp(-0.5 * u * u) * 0.3989422804014327)
    du = (da * slope).astype(BF)
    du_out[...] = du
    sum_out[...] = column_sum(du)
    split_rows(dot(du, up[...], NT), mine_out, send)


def pick_core(g, mine_out, other_out, top):
    _, core = place()
    lo, hi = g[:, :, 0], g[:, :, 1]
    n = lo.shape[1] * lo.shape[2]
    mine = jnp.where(core == 0, lo, hi).reshape(CHIPS, n, g.shape[-1])
    other = jnp.where(core == 0, hi, lo).reshape(CHIPS, n, g.shape[-1])
    mine_out[:, top : top + n, :] = mine.astype(BF)
    other_out[:, top : top + n, :] = other.astype(BF)


def place_columns(g, mine_out, other_out, top):
    unit = g.shape[0] // (CHIPS * CHIPS * CORES)
    pick_core(g.reshape(CHIPS, CHIPS, CORES, unit, g.shape[1]), mine_out, other_out, top)


def place_rows(g, mine_out, other_out, top):
    unit = g.shape[0] // (CHIPS * CORES)
    pick_core(g.reshape(CHIPS, 1, CORES, unit, g.shape[1]), mine_out, other_out, top)


def place_row_blocks(g, mine_out, other_out, top, lanes):
    unit = g.shape[0] // (CHIPS * CORES)
    for b in range(g.shape[1] // lanes):
        place_rows(g[:, b * lanes : (b + 1) * lanes], mine_out, other_out, top + b * unit)


def ffn_grads_kernel(low, du, a, e, mine_out, other_out):
    g = dot(low[...], du[...], TN)
    place_columns(g, mine_out, other_out, 0)
    g2 = dot(a[...], e[...], TN)
    place_rows(g2, mine_out, other_out, g.shape[0] // (CHIPS * CORES))


def cross_back_kernel(*refs):
    parts, (w_mine, w_cols, q_ref, k_ref, v_ref) = refs[:4], refs[4:9]
    (e_out, dq_out, dk_out, dv_out, mine_out), send = refs[9:14], refs[14:]
    quarter = q_ref.shape[1]
    length, memory = q_ref.shape[0] // CHIPS, k_ref.shape[0] // CHIPS
    e = stack_rows(parts)
    e_out[...] = e
    g = dot(e, w_mine[1], NT).astype(BF)
    for p in range(CHIPS):
        s, t = slice(p * length, (p + 1) * length), slice(p * memory, (p + 1) * memory)
        dq_out[s, :], dk_out[t, :], dv_out[t, :] = attend_back(g[s], q_ref[s, :], k_ref[t, :], v_ref[t, :], False)
    split_rows(dot(dq_out[...], w_cols[:, :quarter], NT), mine_out, send)


def cross_grads_kernel(low, dq, m, dk, dv, o, e, mine_out, other_out, sums_out):
    n = low.shape[1] // (CHIPS * CORES)
    for j, (a, g) in enumerate(((low, dq), (m, dk), (m, dv))):
        place_columns(dot(a[...], g[...], TN), mine_out, other_out, j * n)
    place_row_blocks(dot(o[...], e[...], TN), mine_out, other_out, 3 * n, dq.shape[1])
    sums_out[...] = jnp.zeros_like(sums_out)
    sums_out[0:1, :] = column_sum(dq[...])
    sums_out[1:2, :] = column_sum(dv[...])


def self_back_kernel(*refs):
    parts, (w_mine, q_ref, k_ref, v_ref), (e_out, d_out) = refs[:4], refs[4:8], refs[8:]
    quarter = q_ref.shape[1]
    length = q_ref.shape[0] // CHIPS
    e = stack_rows(parts)
    e_out[...] = e
    g = dot(e, w_mine[0], NT).astype(BF)
    for p in range(CHIPS):
        s = slice(p * length, (p + 1) * length)
        dq, dk, dv = attend_back(g[s], q_ref[s, :], k_ref[s, :], v_ref[s, :], True)
        d_out[s, :quarter] = dq
        d_out[s, quarter : 2 * quarter] = dk
        d_out[s, 2 * quarter :] = dv


SMALL = 16


def self_grads_kernel(x, d, o, e, c_sums, sum_in, one, two, three, mine_out, other_out):
    chip, core = place()
    quarter = d.shape[1] // 3
    n = x.shape[1] // (CHIPS * CORES)
    g = dot(x[...], d[...], TN)
    for j in range(3):
        place_columns(g[:, j * quarter : (j + 1) * quarter], mine_out, other_out, j * n)
    place_row_blocks(dot(o[...], e[...], TN), mine_out, other_out, 3 * n, quarter)

    def spread(row):
        zero = jnp.zeros_like(row)
        return jnp.concatenate([jnp.where(chip == b, row, zero) for b in range(CHIPS)], axis=1)

    rows = [
        spread(column_sum(d[:, :quarter])), spread(column_sum(d[:, 2 * quarter :])), one[2:3, :],
        spread(c_sums[0:1, :]), spread(c_sums[1:2, :]), two[2:3, :], one[0:1, :], two[0:1, :], three[0:1, :],
        one[1:2, :], two[1:2, :], three[1:2, :], three[2:3, :],
    ]
    v = jnp.concatenate(rows + [jnp.zeros((SMALL - len(rows), x.shape[1]), F32)], axis=0)
    unit = x.shape[1] // (CHIPS * CHIPS * CORES)
    wide = sum_in.shape[1] // (CHIPS * CORES)
    last = sum_in[...]
    top = 4 * n
    for out in (mine_out, other_out):
        out[:, top:, :] = jnp.zeros((CHIPS, 2 * SMALL, quarter), BF)
    for s in range(CHIPS):
        halves, ends = [], []
        for c in range(CORES):
            parts = [v[:, ((s * CHIPS + b) * CORES + c) * unit :][:, :unit] for b in range(CHIPS)]
            halves.append(jnp.concatenate(parts, axis=1))
            ends.append(last[:, (s * CORES + c) * wide :][:, :wide])
        for out, swap in ((mine_out, False), (other_out, True)):
            first = (core == 0) != swap
            out[s, top : top + SMALL, : CHIPS * unit] = jnp.where(first, halves[0], halves[1]).astype(BF)
            out[s, top + SMALL : top + SMALL + 1, :wide] = jnp.where(first, ends[0], ends[1]).astype(BF)


def input_back_kernel(d, w_self, dk, dv, w_cross, mine_out, *send):
    quarter = dk.shape[1]
    length, memory = d.shape[0] // CHIPS, dk.shape[0] // CHIPS
    y = dot(d[...], w_self[...], NT)
    m = dot(dk[...], w_cross[:, quarter : 2 * quarter], NT) + dot(dv[...], w_cross[:, 2 * quarter :], NT)
    for k, out in enumerate((mine_out, *send)):
        out[:length, :] = y[k * length : (k + 1) * length].astype(out.dtype)
        out[length:, :] = m[k * memory : (k + 1) * memory].astype(out.dtype)


def input_total_kernel(base, mine, r1, r2, r3, source_out, memory_out):
    length = base.shape[0]
    y = mine[...] + r1[...].astype(F32) + r2[...].astype(F32) + r3[...].astype(F32)
    source_out[...] = base[...] + y[:length]
    memory_out[...] = y[length:]


def core_sum_kernel(mine, got, out):
    for n in range(SLOTS):
        out[n] = (mine[n].astype(F32) + got[n].astype(F32)).astype(BF)


def column_pieces_kernel(count, got, *outs):
    *pieces, rest = outs
    chip, _ = place()
    unit = pieces[0].shape[0] // count
    y = sum(got[n].astype(F32) for n in range(SLOTS))
    top = count * CHIPS * unit
    rest[...] = y[top:].astype(BF)
    hold = y[:top].astype(BF).reshape(count, CHIPS, unit, y.shape[1])
    for k in range(CHIPS):
        for j in range(count):
            block = jnp.zeros((unit, y.shape[1]), BF)
            for b in range(CHIPS):
                block = jnp.where((chip ^ k) == b, hold[j, b], block)
            pieces[k][j * unit : (j + 1) * unit, :] = block


def attn_pieces_kernel(s_got, c_got, *outs):
    *pieces, rest = outs
    chip, _ = place()
    s = sum(s_got[n].astype(F32) for n in range(SLOTS)).astype(BF)
    c = sum(c_got[n].astype(F32) for n in range(SLOTS)).astype(BF)
    top = 3 * c.shape[0] // 4
    unit = top // (3 * CHIPS)
    both = [y[:top].reshape(3, CHIPS, unit, y.shape[1]) for y in (s, c)]
    for k in range(CHIPS):
        for m, y in enumerate(both):
            for j in range(3):
                block = jnp.zeros((unit, y.shape[3]), BF)
                for b in range(CHIPS):
                    block = jnp.where((chip ^ k) == b, y[j, b], block)
                pieces[k][(3 * m + j) * unit : (3 * m + j + 1) * unit, :] = block
        pieces[k][6 * unit :, :] = s[c.shape[0] : c.shape[0] + SMALL]
    n = c.shape[0] - top
    rest[:n, :] = s[top : top + n]
    rest[n : 2 * n, :] = c[top:]
    rest[2 * n :, :] = s[c.shape[0] + SMALL :]


def attn_out_kernel(p0, p1, p2, p3, out, bias_out, gain_out, shift_out, last_out):
    chip, _ = place()
    unit, quarter = out.shape[1], p0.shape[1]
    parts = (p0, p1, p2, p3)
    for k, p in enumerate(parts):
        lanes = rows_at((chip ^ k) * quarter, quarter, 128)
        for j in range(6):
            out[j, :, lanes] = p[j * unit : (j + 1) * unit, :].astype(F32)
    total = sum(p[6 * unit :, : CHIPS * unit].astype(F32) for p in parts)
    mine = jnp.zeros((SMALL, unit), F32)
    for b in range(CHIPS):
        mine = jnp.where(chip == b, total[:, b * unit : (b + 1) * unit], mine)
    columns = jnp.transpose(jnp.concatenate([mine, jnp.zeros((SMALL, 128 - unit), F32)], axis=1))
    bias_out[...] = columns[:unit, 0:6]
    gain_out[...] = columns[:unit, 6:9]
    shift_out[...] = columns[:unit, 9:12]
    last_out[...] = mine[12:13, :]


def rows_out_kernel(owned, f_owned, out, down_out, in_out):
    unit, quarter = out.shape[1], owned.shape[1]
    n = CHIPS * unit
    for m in range(2):
        for b in range(CHIPS):
            out[m, :, b * quarter : (b + 1) * quarter] = owned[m * n + b * unit : m * n + (b + 1) * unit, :].astype(F32)
    down_out[...] = f_owned[...].astype(F32)
    in_out[...] = owned[2 * n : 2 * n + 1, : in_out.shape[1]].astype(F32)


def up_out_kernel(p0, p1, p2, p3, out):
    chip, _ = place()
    quarter = p0.shape[1]
    for k, p in enumerate((p0, p1, p2, p3)):
        out[:, rows_at((chip ^ k) * quarter, quarter, 128)] = p[...].astype(F32)


def shards(
    inputs, memory, attn_weight, attn_out, ffn_in, ffn_out, attn_bias, norm_gain, norm_bias,
    bias_in, bias_out, embedding, targets, slot_counts, pad_mask, log_prior,
):
    n_pb, n_slot = lax.axis_size("pb"), lax.axis_size("slot")
    n_all = n_pb * n_slot
    teams = n_pb // TEAM
    me = lax.axis_index("pb")
    length, width = inputs.shape[2], inputs.shape[3]
    passage = memory.shape[2]
    quarter = width // CHIPS
    unit = width // (TEAM * n_slot)
    vocab_rows = embedding.shape[0]
    embedding = in_hbm(embedding)

    def team_rows(w):
        if teams == 1:
            return w
        w = lax.all_gather(w, "pb", axis=0, tiled=True)
        n = w.shape[0] // TEAM
        return lax.dynamic_slice_in_dim(w, (me % TEAM) * n, n)

    x, m = inputs[0, 0], memory[0, 0]
    attn_w = jnp.moveaxis(team_rows(attn_weight), 1, 0)
    out_w = jnp.moveaxis(team_rows(attn_out), 1, 0)
    up_w = team_rows(ffn_in)
    down_w = team_rows(ffn_out)
    rows = attn_w.shape[1]
    ff = up_w.shape[1] // CHIPS
    vec = jnp.concatenate(
        [attn_bias.T, norm_gain.T, norm_bias.T, bias_out[None], bias_in.reshape(CHIPS, -1)], axis=0
    )
    ids = (targets - me * vocab_rows).astype(jnp.int32)
    own_row = jnp.concatenate([pad_mask.astype(F32), jnp.broadcast_to(log_prior, (1, length))], axis=1)

    block = (length, width)
    every = (CHIPS * length, width)
    cols = (CHIPS * length, quarter)
    m_cols = (CHIPS * passage, quarter)
    sends = [(block, BF)] * 3

    def give(send):
        return [from_chip(send[k - 1], k) for k in range(1, CHIPS)]

    def give_far(send):
        return [in_hbm(r) for r in give(send)]

    far_call = functools.partial(call, far=True)

    first = call(functools.partial(pack_kernel, 6, 0), [((CHIPS * length + 6 * rows, quarter), BF)] * CHIPS, x, attn_w)
    got_first = [first[0]] + give(first[1:])
    got_first[1], vec = tie(got_first[1], vec)
    pair_first = [from_core(g) for g in got_first]
    out_pair = from_core(out_w)
    down_pair = from_core(down_w)
    third = list(call(functools.partial(pack_kernel, 1, 0), [((rows, ff), BF)] * CHIPS, up_w[None]))
    m_send, pair_first[3] = tie(m, pair_first[3])
    got_memory = [m, from_chip(m_send, 1), from_chip(m_send, 2)]

    x_all, w_self, queries, keys, values, mixed, w_out, mine, *send = call(
        self_kernel,
        [(every, BF), ((width, 3 * quarter), BF)] + [(cols, BF)] * 4 + [((2, quarter, width), BF), (block, F32)]
        + sends,
        *got_first, *pair_first, out_w, out_pair, vec,
    )
    got = give(send)
    got_memory[1], got_memory[2], *got = tie(got_memory[1], got_memory[2], *got)
    norm_outs = [(block, F32), (block, BF), (block, F32), ((length, 1), F32)]
    hidden_one, low_one, z_one, inv_one = call(
        functools.partial(norm_kernel, (2, 6, 9)), norm_outs, x, mine, *got, vec, us=1
    )
    got_low = [low_one] + others(low_one)
    m_send, got_memory[1] = tie(m, got_memory[1])
    got_memory.append(from_chip(m_send, 3))
    m_all, w_cross, cross_keys, cross_values = call(
        memory_kernel, [((CHIPS * passage, width), BF), ((width, 3 * quarter), BF)] + [(m_cols, BF)] * 2,
        *got_memory, *got_first, *pair_first, vec,
    )
    third[1], third[2], *got_low = tie(third[1], third[2], *got_low)
    got_third = [third[0], from_chip(third[1], 1), from_chip(third[2], 2)]
    low_one_all, cross_queries, cross_mixed, mine, *send = call(
        cross_kernel, [(every, BF), (cols, BF), (cols, BF), (block, F32)] + sends,
        *got_low, w_out, w_cross, cross_keys, cross_values, vec,
    )
    got = give(send)
    got_third[1], got_third[2], *got = tie(got_third[1], got_third[2], *got)
    hidden_two, low_two, z_two, inv_two = call(
        functools.partial(norm_kernel, (5, 7, 10)), norm_outs, hidden_one, mine, *got, vec, us=1
    )
    got_low = [low_two] + others(low_two)
    third[3], got_third[1] = tie(third[3], got_third[1])
    got_third.append(from_chip(third[3], 3))
    (up_half,) = call(up_half_kernel, [((CHIPS, rows, ff), BF)], *got_third)
    up_half_pair = from_core(up_half)
    low_two_all, upward, active, w_up, w_down, mine, *send = call(
        ffn_kernel,
        [(every, BF), ((CHIPS * length, ff), F32), ((CHIPS * length, ff), BF), ((width, ff), BF)]
        + [((ff, width), BF), (block, F32)]
        + sends,
        *got_low, up_half, up_half_pair, down_w, down_pair, vec,
    )
    got = give(send)
    _, final_low, z_three, inv_three = call(
        functools.partial(norm_kernel, (12, 8, 11)), norm_outs, hidden_two, mine, *got, vec, us=1
    )

    held, spread_held = call(
        stack_kernel, [(every, BF), ((n_slot,) + every, BF)], final_low, *others(final_low), us=1
    )
    pair = from_core(held)

    def all_teams(h):
        return lax.all_gather(h, "pb", axis_index_groups=same_place_groups(), axis=0, tiled=True) if teams > 1 else h

    half = teams * CHIPS * length
    chip, core = place()
    order = [
        t * TEAM + (chip ^ k) * CORES + (core ^ d) for d in range(CORES) for t in range(teams) for k in range(CHIPS)
    ]
    ids_row = jnp.concatenate([lax.dynamic_slice_in_dim(ids, q, 1) for q in order], axis=1)
    states = [all_teams(held), all_teams(pair)]
    scores, payload = logits(*states, ids_row, own_row, embedding, length, n_pb)
    everyone = lax.all_to_all(
        jnp.broadcast_to(payload[None], (n_all,) + payload.shape), ("slot", "pb"), 0, 0, tiled=True
    )
    ids_wide = jnp.pad(ids.astype(F32), ((0, 0), (0, length)))
    spread_held, everyone = tie(spread_held, everyone)
    all_held = across_slots(spread_held)
    token_rows, own_rows, token_logprob, prior_grad = merge(
        everyone, slot_counts.astype(jnp.int32)[:, None], ids_wide, length, n_slot, n_pb, half
    )
    def home(partial):
        if teams == 1:
            return partial
        return lax.psum_scatter(partial, "pb", axis_index_groups=same_place_groups(), scatter_dimension=0, tiled=True)

    own_part, for_pair, own_logits = state_grad(scores, own_rows, embedding, F32)
    own_logits = in_hbm(own_logits)
    own_part, got_pair = home(own_part), from_core(home(for_pair))
    mine, *send = call(add_kernel, [(block, F32)] + sends, own_part, got_pair, us=1)
    got = give(send)
    own_logits, send[0] = tie(own_logits, send[0])
    own_terms = own_embedding(own_logits, *states, None, 0, 2)
    own_terms, *got = tie(own_terms, *got)

    eighth = vocab_rows // 8
    parts = (1, 1, 1, 2, 2, 1)
    made = []

    def piece(*wait):
        n = len(made) - 1
        rows_in, *wait = tie(token_rows, *wait)
        first = sum(parts[:n]) * eighth
        made.append(embedding_piece(rows_in, states, embedding, made[-1], first, parts[n] * eighth))
        return wait

    def pieces(count, *wait):
        for _ in range(count):
            wait = piece(*wait)
        return list(wait)

    def then(*values):
        *values, made[-1] = tie(*values, made[-1])
        return values

    def settle(g):
        if teams == 1:
            return g
        g = lax.psum(g, "pb", axis_index_groups=same_place_groups())
        g = lax.all_gather(g, "pb", axis_index_groups=team_groups(), axis=0, tiled=True)
        n = g.shape[0] // n_pb
        return lax.dynamic_slice_in_dim(g, me * n, n)

    def to_owner(g):
        pairs = []
        for s in range(n_slot):
            for i in range(n_pb):
                t, b, c = i // TEAM, (i % TEAM) // CORES, i % CORES
                pairs.append((s * n_pb + i, b * n_pb + t * TEAM + s * CORES + c))
        return lax.ppermute(g, ("slot", "pb"), pairs)

    def column_pieces(count, got, n, cols):
        rest = got.shape[1] - count * CHIPS * n
        *piece, rest = call(
            functools.partial(column_pieces_kernel, count),
            [((count * n, cols), BF)] * CHIPS + [((rest, cols), BF)], got,
        )
        return [piece[0]] + give_far(piece[1:]), rest

    x_all, w_self, queries, keys, values, mixed, w_out, m_all, w_cross, cross_keys, cross_values = (
        in_hbm(v)
        for v in (x_all, w_self, queries, keys, values, mixed, w_out, m_all, w_cross, cross_keys, cross_values)
    )
    low_one_all, cross_queries, cross_mixed, low_two_all, upward, active, w_up, w_down = (
        in_hbm(v) for v in (low_one_all, cross_queries, cross_mixed, low_two_all, upward, active, w_up, w_down)
    )
    z_one, z_two, z_three = in_hbm(z_one), in_hbm(z_two), in_hbm(z_three)
    grads = [(block, F32), (block, BF), ((8, width), F32)]
    dr_three, e_three, sums_three = call(
        functools.partial(norm_back_kernel, 2, False), grads, mine, *got, z_three, inv_three, vec, us=1
    )
    got_e = others(e_three)
    own_logits, e_three = tie(own_logits, e_three)
    own_terms = own_embedding(own_logits, *states, own_terms, 1, 2)
    own_terms, *got_e = tie(own_terms, *got_e)
    made.append(own_terms)
    e_all, du, sum_in, mine, *send = call(
        ffn_back_kernel,
        [(every, BF), ((CHIPS * length, ff), BF), ((1, ff), F32), (block, F32)] + sends,
        e_three, *got_e, upward, w_up, w_down,
    )
    got = give_far(send)
    f_shape = (n_slot, CHIPS * unit + ff // TEAM, width)
    du, send[0] = tie(du, send[0])
    f_mine, f_other = call(ffn_grads_kernel, [(f_shape, BF)] * 2, low_two_all, du, active, e_all, us=3)
    f_other, all_held, *got = tie(f_other, all_held, *got)
    all_pair = from_core(all_held)
    dr_two, e_two, sums_two = far_call(
        functools.partial(norm_back_kernel, 1, True), grads, dr_three, mine, *got, z_two, inv_two, vec, us=1
    )
    got_e = give_far([e_two] * 3)
    f_got = from_core(f_other)
    f_got, all_pair, e_two = tie(f_got, all_pair, e_two)
    states = [jnp.stack([all_teams(h[n]) for n in range(n_slot)]) if teams > 1 else h for h in (all_held, all_pair)]
    (f_total,) = far_call(core_sum_kernel, [(f_shape, BF)], f_mine, f_got)
    f_got = across_slots(f_total)
    e_all_two, dqc, dkc, dvc, mine, *send = far_call(
        cross_back_kernel,
        [(every, BF), (cols, BF), (m_cols, BF), (m_cols, BF), (block, F32)] + sends,
        e_two, *got_e, w_out, w_cross, cross_queries, cross_keys, cross_values, us=5,
    )
    got = give_far(send)
    dqc, send[0] = tie(dqc, send[0])
    g_shape = (n_slot, 4 * CHIPS * unit, quarter)
    c_mine, c_other, c_sums = call(
        cross_grads_kernel, [(g_shape, BF)] * 2 + [((8, quarter), F32)],
        low_one_all, dqc, m_all, dkc, dvc, cross_mixed, e_all_two,
    )
    c_got = from_core(c_other)
    (c_mine,) = piece(c_mine)
    got = then(*got)
    dr_one, e_one, sums_one = far_call(
        functools.partial(norm_back_kernel, 0, True), grads, dr_two, mine, *got, z_one, inv_one, vec, us=1
    )
    got_e = give_far([e_one] * 3)
    c_got, e_one = tie(c_got, e_one)
    (c_total,) = far_call(core_sum_kernel, [(g_shape, BF)], c_mine, c_got)
    (c_total,) = piece(c_total)
    f_got, *got_e = then(f_got, *got_e)
    e_all_one, d_self = far_call(
        self_back_kernel, [(every, BF), ((CHIPS * length, 3 * quarter), BF)], e_one, *got_e, w_out, queries, keys, values, us=4
    )
    c_total, d_self = tie(c_total, d_self)
    c_got = across_slots(c_total)
    s_shape = (n_slot, g_shape[1] + 2 * SMALL, quarter)
    s_mine, s_other = far_call(
        self_grads_kernel, [(s_shape, BF)] * 2, x_all, d_self, mixed, e_all_one, c_sums, sum_in, sums_one, sums_two, sums_three
    )
    s_got = from_core(s_other)
    f_got, s_mine = tie(f_got, s_mine)
    f_pieces, f_rest = column_pieces(1, f_got, unit, width)
    f_owned = to_owner(f_rest)
    d_self, f_rest = tie(d_self, f_rest)
    both = (length + passage, width)
    mine, *send = far_call(input_back_kernel, [(both, F32)] + [(both, BF)] * 3, d_self, w_self, dkc, dvc, w_cross, us=3)
    s_got, send[0] = tie(s_got, send[0])
    (s_total,) = far_call(core_sum_kernel, [(s_shape, BF)], s_mine, s_got)
    (s_total,) = pieces(1, s_total)
    c_got, *f_pieces = then(c_got, *f_pieces)
    s_total, send[0], c_got = tie(s_total, send[0], c_got)
    s_got = across_slots(s_total)
    got = give_far(send)
    (out_up,) = call(up_out_kernel, [((unit, up_w.shape[1]), F32)], *f_pieces, us=1)
    (out_up,) = pieces(len(parts) + 1 - len(made), out_up)
    s_got, *got = then(s_got, *got)
    *piece_parts, rest = call(
        attn_pieces_kernel,
        [((6 * unit + SMALL, quarter), BF)] * CHIPS + [((2 * CHIPS * unit + SMALL, quarter), BF)],
        s_got, c_got,
    )
    last = give(piece_parts[1:])
    owned = to_owner(rest)
    grad_source, grad_passage = call(
        input_total_kernel, [(block, F32), ((passage, width), F32)], dr_one, mine, *got, us=1
    )
    owned, grad_source, *last = tie(owned, grad_source, *last)
    out_attn, *vectors = call(
        attn_out_kernel,
        [((6, unit, width), F32), ((unit, 6), F32), ((unit, 3), F32), ((unit, 3), F32), ((1, unit), F32)],
        piece_parts[0], *last, us=1,
    )
    outs, out_down, sum_in_out = call(
        rows_out_kernel, [((2, unit, width), F32), (f_rest.shape, F32), ((1, ff // TEAM), F32)], owned, f_owned, us=1
    )
    out_attn = settle(jnp.moveaxis(out_attn, 0, 1))
    out_outputs = settle(jnp.moveaxis(outs, 0, 1))
    out_up, out_down = settle(out_up), settle(out_down)
    vectors = [settle(v) for v in (*vectors[:3], sum_in_out[0], vectors[3][0])]
    return (
        token_logprob[:, :length],
        grad_source[None, None],
        grad_passage[None, None],
        prior_grad,
        out_attn,
        out_outputs,
        out_up,
        out_down,
        vectors[0],
        vectors[1],
        vectors[2],
        vectors[3],
        vectors[4],
        made[-1],
    )


def solution(mesh):
    placed = (
        P("pb", "slot", None, None),
        P("pb", "slot", None, None),
        P("pb", None, None),
        P("pb", None, None),
        P("pb", None),
        P("pb", None),
        P(),
        P(),
        P(),
        P(),
        P(),
        P("pb", None),
        P(),
        P(),
        P("pb", None),
        P("pb", "slot"),
    )
    both = ("slot", "pb")
    return jax.shard_map(
        shards,
        mesh=mesh,
        in_specs=placed,
        out_specs=(
            P("pb", None),
            P("pb", "slot", None, None),
            P("pb", "slot", None, None),
            P("pb", "slot"),
            P(both, None, None),
            P(both, None, None),
            P(both, None),
            P(both, None),
            P(both, None),
            P(both, None),
            P(both, None),
            P(both),
            P(both),
            P("pb", None),
        ),
        check_vma=False,
    )
```

```python
import functools

import jax
import jax.numpy as jnp
from jax import lax
from jax.experimental import pallas as pl
from jax.experimental.pallas import tpu as pltpu
from jax.sharding import PartitionSpec as P

HEAD = 64
CHIPS = 4
CORES = 2
TEAM = CHIPS * CORES
SLOTS = 4
BF = jnp.bfloat16
F32 = jnp.float32
TOKENS = 512
VOCAB_TILE = 512


def from_chip(x, k):
    pairs = []
    for i in range(lax.axis_size("pb")):
        place = i % TEAM
        pairs.append((i, i - place + ((place // CORES) ^ k) * CORES + place % CORES))
    return lax.ppermute(x, "pb", pairs)


def from_core(x):
    return lax.ppermute(x, "pb", [(i, i ^ 1) for i in range(lax.axis_size("pb"))])


def across_slot(x, k):
    return lax.ppermute(x, "slot", [(i, i ^ k) for i in range(lax.axis_size("slot"))])


def same_place_groups():
    size = lax.axis_size("pb")
    return [[g * TEAM + j for g in range(size // TEAM)] for j in range(TEAM)]


def team_groups():
    size = lax.axis_size("pb")
    return [[g * TEAM + j for j in range(TEAM)] for g in range(size // TEAM)]


def others(x):
    return [from_chip(x, k) for k in range(1, CHIPS)]


def tie(*values):
    return list(lax.optimization_barrier(values))


def across_slots(x):
    return lax.all_to_all(x, "slot", 0, 0, tiled=True)


def at(x, index):
    return lax.dynamic_index_in_dim(x, index, 0, False)


NN = (((1,), (0,)), ((), ()))
NT = (((1,), (1,)), ((), ()))
TN = (((0,), (0,)), ((), ()))


def dot(a, b, dims=NN):
    return lax.dot_general(a, b, dims, preferred_element_type=F32)


def place():
    j = lax.axis_index("pb") % TEAM
    return j // CORES, j % CORES


def rows_at(start, size, unit):
    return pl.ds(pl.multiple_of(start, unit), size)


MIB = 2**20


def limit(mib):
    return pltpu.CompilerParams(vmem_limit_bytes=min(60, mib) * MIB)


def work(us):
    return pl.CostEstimate(flops=int(us * 1e9), bytes_accessed=0, transcendentals=0)


def call(kernel, outs, *args, us=2.0, far=False, scratch=()):
    shapes = [jax.ShapeDtypeStruct(*o) for o in outs]
    held = sum(a.size * a.dtype.itemsize for a in (*args, *shapes))
    params = limit(8 + held * 5 // 4 // MIB)
    places = [pltpu.HBM(*o) for o in outs] if far else shapes
    results = pl.pallas_call(
        kernel, out_shape=places, scratch_shapes=scratch, compiler_params=params, cost_estimate=work(us)
    )(*args)
    return [in_hbm(r) for r in results] if far else results


def in_hbm(x):
    return pltpu.with_memory_space_constraint(x, pltpu.HBM)


def norm_rows(r, gain, shift):
    centered = r - jnp.mean(r, axis=-1, keepdims=True)
    inv = lax.rsqrt(jnp.mean(centered * centered, axis=-1, keepdims=True) + 1e-05)
    z = centered * inv
    return z * gain + shift, z, inv


def norm_back(dh, z, inv, gain):
    dz = dh * gain
    return (dz - jnp.mean(dz, axis=-1, keepdims=True) - z * jnp.mean(dz * z, axis=-1, keepdims=True)) * inv


def lane_head(shape, keys):
    return lax.broadcasted_iota(jnp.int32, shape, 1) // keys


def per_head(x):
    head = lane_head(x.shape, HEAD)
    return jnp.concatenate([jnp.where(head == h, x, jnp.zeros_like(x)) for h in range(x.shape[1] // HEAD)], axis=0)


def own_heads(big, keys):
    count = big.shape[1] // HEAD
    head = lane_head((keys, big.shape[1]), HEAD)
    total = jnp.zeros((keys, big.shape[1]), F32)
    for h in range(count):
        total = total + jnp.where(head == h, big[h * keys : (h + 1) * keys], 0.0)
    return total


def head_probs(q, kbig, keys, causal):
    s = dot(q, kbig, NT) * 0.125
    head = lane_head(s.shape, keys)
    count = s.shape[1] // keys
    if causal:
        query = lax.broadcasted_iota(jnp.int32, s.shape, 0)
        key = lax.broadcasted_iota(jnp.int32, s.shape, 1) % keys
        s = jnp.where(query >= key, s, -1e30)
    peak = jnp.zeros_like(s)
    for h in range(count):
        m = jnp.max(jnp.where(head == h, s, -3e38), axis=1, keepdims=True)
        peak = jnp.where(head == h, m, peak)
    e = jnp.exp(s - peak)
    return e / head_sums(e, head, count)


def head_sums(x, head, count):
    total = jnp.zeros_like(x)
    for h in range(count):
        total = jnp.where(head == h, jnp.sum(jnp.where(head == h, x, 0.0), axis=1, keepdims=True), total)
    return total


def attend(q, k, v, causal):
    probs = head_probs(q, per_head(k), k.shape[0], causal)
    return dot(probs.astype(BF), per_head(v)).astype(BF)


def attend_back(g, q, k, v, causal):
    keys = k.shape[0]
    kbig, vbig = per_head(k), per_head(v)
    probs = head_probs(q, kbig, keys, causal)
    dp = dot(g, vbig, NT)
    head = lane_head(dp.shape, keys)
    ds = (probs * (dp - head_sums(dp * probs, head, dp.shape[1] // keys))).astype(BF)
    dq = dot(ds, kbig) * 0.125
    dk = own_heads(dot(ds, q, TN), keys) * 0.125
    dv = own_heads(dot(probs.astype(BF), g, TN), keys)
    return dq.astype(BF), dk.astype(BF), dv.astype(BF)


def pack_kernel(count, first, *refs):
    *rows_in, w_ref, o0, o1, o2, o3 = refs
    outs = (o0, o1, o2, o3)
    chip, _ = place()
    rows, quarter = w_ref.shape[1], w_ref.shape[2] // CHIPS
    for k in range(CHIPS):
        top = 0
        for x_ref in rows_in:
            x = x_ref[...]
            for b in range(CHIPS):
                outs[k][top : top + x.shape[0], :] = x[:, b * quarter : (b + 1) * quarter]
                top += x.shape[0]
        for j in range(count):
            outs[k][top : top + rows, :] = w_ref[first + j, :, rows_at((chip ^ k) * quarter, quarter, 128)]
            top += rows


def natural_columns(own, pair, w_out, top, count):
    chip, core = place()
    rows = w_out.shape[0] // TEAM
    quarter = own[0].shape[1]
    for k in range(CHIPS):
        for refs, c in ((own, core), (pair, 1 - core)):
            start = (chip ^ k) * (CORES * rows) + c * rows
            for j in range(count):
                w_out[rows_at(start, rows, 16), j * quarter : (j + 1) * quarter] = refs[k][
                    top + j * rows : top + (j + 1) * rows, :
                ]


def half_columns(parts, out, top, count):
    chip, _ = place()
    rows = (parts[0].shape[0] - top) // count
    quarter = parts[0].shape[1]
    for k in range(CHIPS):
        for j in range(count):
            out[chip ^ k, :, j * quarter : (j + 1) * quarter] = parts[k][top + j * rows : top + (j + 1) * rows, :]


def whole_columns(mine, pair, out):
    _, core = place()
    rows = mine.shape[1]
    for b in range(CHIPS):
        for part, c in ((mine, core), (pair, 1 - core)):
            out[rows_at(b * CORES * rows + c * rows, rows, 16), :] = part[b]


def pair_rows(own, pair):
    _, core = place()
    a, b = own[...], pair[...]
    return jnp.concatenate([jnp.where(core == 0, a, b), jnp.where(core == 0, b, a)], axis=0)


def self_kernel(*refs):
    own, pair, (o_own, o_pair, vec) = refs[:4], refs[4:8], refs[8:11]
    x_out, w_out, q_out, k_out, v_out, o_out, wo_out, mine_out = refs[11:19]
    send = refs[19:]
    chip, _ = place()
    quarter = own[0].shape[1]
    length = x_out.shape[0] // CHIPS
    natural_columns(own, pair, w_out, CHIPS * length, 3)
    for k in range(CHIPS):
        for b in range(CHIPS):
            x_out[k * length : (k + 1) * length, b * quarter : (b + 1) * quarter] = own[k][b * length : (b + 1) * length, :]
    for j in range(2):
        wo_out[j] = pair_rows(o_own.at[j], o_pair.at[j])
    lanes = rows_at(chip * quarter, quarter, 128)
    y = dot(x_out[...], w_out[...])
    q = (y[:, :quarter] + vec[0:1, lanes]).astype(BF)
    k = y[:, quarter : 2 * quarter].astype(BF)
    v = (y[:, 2 * quarter :] + vec[1:2, lanes]).astype(BF)
    q_out[...], k_out[...], v_out[...] = q, k, v

    def pair(i, carry):
        for j in range(2):
            s = rows_at((2 * i + j) * length, length, 16)
            o_out[s, :] = attend(q_out[s, :], k_out[s, :], v_out[s, :], True)
        return carry

    lax.fori_loop(0, CHIPS // 2, pair, 0)
    split_rows(dot(o_out[...], wo_out[0]), mine_out, send)


def half_kernel(*refs):
    half_columns(refs[:4], refs[4], 0, 3)


def memory_kernel(*refs):
    mem, own, pair, vec, (m_out, w_out, k_out, v_out) = refs[:4], refs[4:8], refs[8:12], refs[12], refs[13:]
    chip, _ = place()
    quarter = k_out.shape[1]
    natural_columns(own, pair, w_out, own[0].shape[0] - 3 * w_out.shape[0] // TEAM, 3)
    m_out[...] = stack_rows(mem)
    y = dot(m_out[...], w_out[:, quarter:])
    k_out[...] = y[:, :quarter].astype(BF)
    v_out[...] = (y[:, quarter:] + vec[4:5, rows_at(chip * quarter, quarter, 128)]).astype(BF)


def norm_kernel(rows, *refs):
    base, mine, r1, r2, r3, vec, h_out, low_out, z_out, inv_out = refs
    y = mine[...] + r1[...].astype(F32) + r2[...].astype(F32) + r3[...].astype(F32)
    r = base[...].astype(F32) + y + vec[rows[0] : rows[0] + 1, :]
    h, z, inv = norm_rows(r, vec[rows[1] : rows[1] + 1, :], vec[rows[2] : rows[2] + 1, :])
    h_out[...] = h
    low_out[...] = h.astype(BF)
    z_out[...] = z
    inv_out[...] = inv


def cross_kernel(*refs):
    parts, (wo, w_cols, keys, values, vec), (low_out, q_out, o_out, mine_out), send = refs[:4], refs[4:9], refs[9:13], refs[13:]
    chip, _ = place()
    quarter = keys.shape[1]
    length = parts[0].shape[0]
    memory = keys.shape[0] // CHIPS
    low = stack_rows(parts)
    low_out[...] = low
    q = (dot(low, w_cols[:, :quarter]) + vec[3:4, rows_at(chip * quarter, quarter, 128)]).astype(BF)
    q_out[...] = q

    def pair(i, carry):
        for j in range(2):
            s, t = rows_at((2 * i + j) * length, length, 16), rows_at((2 * i + j) * memory, memory, 16)
            o_out[s, :] = attend(q_out[s, :], keys[t, :], values[t, :], False)
        return carry

    lax.fori_loop(0, CHIPS // 2, pair, 0)
    split_rows(dot(o_out[...], wo[1]), mine_out, send)


def gelu_parts(u):
    phi = 0.5 * (1.0 + lax.erf(u * 0.7071067811865476))
    return phi


def up_half_kernel(*refs):
    half_columns(refs[:4], refs[4], 0, 1)


def ffn_kernel(*refs):
    parts, (up_mine, up_pair, down_own, down_pair, vec) = refs[:4], refs[4:9]
    low_out, u_out, a_out, up_out, down_out, mine_out = refs[9:15]
    send = refs[15:]
    chip, _ = place()
    whole_columns(up_mine, up_pair, up_out)
    down_out[...] = pair_rows(down_own, down_pair)
    low = stack_rows(parts)
    low_out[...] = low
    u = dot(low, up_out[...]) + vec[pl.ds(13 + chip, 1), :]
    u_out[...] = u
    a_out[...] = (u * gelu_parts(u)).astype(BF)
    split_rows(dot(a_out[...], down_out[...]), mine_out, send)


def stack_kernel(r0, r1, r2, r3, out, spread_out):
    n = r0.shape[0]
    for k, part in enumerate((r0, r1, r2, r3)):
        out[k * n : (k + 1) * n, :] = part[...]
        for slot in range(SLOTS):
            spread_out[slot, k * n : (k + 1) * n, :] = part[...]


def logits_kernel(length, h0_ref, h1_ref, ids_ref, own_ref, e_ref, l_ref, pay_ref, h_ref, m_ref, s_ref, p_ref):
    i = pl.program_id(0)
    half = h0_ref.shape[0]

    @pl.when(i == 0)
    def _():
        h_ref[:half, :] = h0_ref[...]
        h_ref[half:, :] = h1_ref[...]
        m_ref[...] = jnp.full_like(m_ref, -3e38)
        s_ref[...] = jnp.zeros_like(s_ref)
        p_ref[...] = jnp.zeros_like(p_ref)

    x = dot(e_ref[...], h_ref[...], NT)
    l_ref[...] = x
    entry = lax.broadcasted_iota(jnp.int32, x.shape, 0) + i * x.shape[0]
    peak = jnp.maximum(m_ref[0:1, :], jnp.max(x, axis=0, keepdims=True))
    total = s_ref[0:1, :] * jnp.exp(m_ref[0:1, :] - peak) + jnp.sum(jnp.exp(x - peak), axis=0, keepdims=True)
    pick = p_ref[0:1, :] + jnp.sum(jnp.where(entry == ids_ref[...], x, 0.0), axis=0, keepdims=True)
    m_ref[0:1, :], s_ref[0:1, :], p_ref[0:1, :] = peak, total, pick

    @pl.when(i == pl.num_programs(0) - 1)
    def _():
        pay_ref[...] = jnp.zeros_like(pay_ref)
        pay_ref[pay_ref.shape[0] - 8 : pay_ref.shape[0] - 7, :] = own_ref[...]
        norm = peak + jnp.log(total)
        lane = lax.broadcasted_iota(jnp.int32, (1, 2 * length), 1)
        chip, core = place()
        for n in range(2 * half // (2 * length)):
            s = slice(n * 2 * length, (n + 1) * 2 * length)
            d, rest = divmod(2 * n * length, half)
            first = rest // length
            team, k = first // CHIPS, first % CHIPS
            rows = (
                jnp.where(lane < length, norm[:, s], pltpu.roll(pick[:, s], length, 1)),
                jnp.where(lane < length, pltpu.roll(norm[:, s], length, 1), pick[:, s]),
            )
            for j in range(2):
                q = team * TEAM + (chip ^ (k + j)) * CORES + (core ^ d)
                pay_ref[pl.ds(q, 1), :] = rows[j]


def logits(held, pair, ids, own_row, embedding, length, questions):
    half, vocab, width = held.shape[0], embedding.shape[0], embedding.shape[1]
    tile = min(2 * VOCAB_TILE, vocab)
    stat = pltpu.VMEM((8, 2 * half), F32)
    whole = pl.BlockSpec(memory_space=pltpu.VMEM)
    return pl.pallas_call(
        functools.partial(logits_kernel, length),
        grid=(vocab // tile,),
        in_specs=[whole, whole, whole, whole, pl.BlockSpec((tile, width), lambda i: (i, 0))],
        out_specs=[
            pl.BlockSpec((tile, 2 * half), lambda i: (i, 0)),
            pl.BlockSpec((questions + 8, 2 * length), lambda i: (0, 0)),
        ],
        out_shape=[
            pltpu.HBM((vocab, 2 * half), F32),
            jax.ShapeDtypeStruct((questions + 8, 2 * length), F32),
        ],
        scratch_shapes=[pltpu.VMEM((2 * half, width), BF), stat, stat, stat],
        compiler_params=limit(14 + 24 * half * tile // MIB),
        cost_estimate=work(10),
    )(held, pair, ids, own_row, embedding)


def merge_kernel(length, all_ref, counts_ref, ids_ref, rows_out, own_out, logp_out, prior_out, n_ref, g_ref):
    n_slot, n_pb = n_ref.shape[0], n_ref.shape[1]
    chip, core = place()
    me, slot = lax.axis_index("pb"), lax.axis_index("slot")
    lane = lax.broadcasted_iota(jnp.int32, (1, 2 * length), 1)
    logps, priors = [], None
    for s in range(n_slot):
        blocks = [all_ref[s * n_pb + j, :n_pb, :] for j in range(n_pb)]
        peak = blocks[0]
        for b in blocks[1:]:
            peak = jnp.maximum(peak, b)
        total = jnp.zeros_like(peak)
        pick = jnp.zeros_like(peak)
        for b in blocks:
            total = total + jnp.exp(b - peak)
            pick = pick + b
        norm = peak + jnp.log(total)
        n_ref[s] = norm
        own = jnp.concatenate([all_ref[s * n_pb + j, n_pb : n_pb + 1, :] for j in range(n_pb)], axis=0)
        mask = own
        prior = pltpu.roll(own, length, 1)
        logp = pltpu.roll(pick, length, 1) - norm + prior
        logps.append(jnp.where(counts_ref[...] > s, logp, -1e30))
    top = logps[0]
    for p in logps[1:]:
        top = jnp.maximum(top, p)
    total = jnp.zeros_like(top)
    for p in logps:
        total = total + jnp.exp(p - top)
    merged = top + jnp.log(total)
    for s in range(n_slot):
        g_ref[s] = jnp.where(counts_ref[...] > s, -mask * jnp.exp(logps[s] - merged), 0.0)
    n_rows = n_ref.shape[1]
    row = lax.broadcasted_iota(jnp.int32, merged.shape, 0)
    logp_out[...] = jnp.sum(jnp.where(row == me, merged, 0.0), axis=0, keepdims=True)
    own_grad = jnp.where(lane < length, g_ref[slot, pl.ds(me, 1), :], 0.0)
    prior_out[...] = jnp.sum(own_grad, axis=1, keepdims=True)
    rows_out[...] = jnp.zeros_like(rows_out)
    half = rows_out.shape[3]
    for s in range(n_slot):
        for d in range(CORES):
            for n in range(half // (2 * length)):
                team, c = (2 * n) // CHIPS, (2 * n) % CHIPS
                q = [team * TEAM + (chip ^ (c + j)) * CORES + (core ^ d) for j in range(2)]
                t = slice(n * 2 * length, (n + 1) * 2 * length)
                for r, (first, second) in enumerate(
                    (
                        (n_ref[s, pl.ds(q[0], 1), :], n_ref[s, pl.ds(q[1], 1), :]),
                        (g_ref[s, pl.ds(q[0], 1), :], g_ref[s, pl.ds(q[1], 1), :]),
                        (ids_ref[pl.ds(q[0], 1), :], ids_ref[pl.ds(q[1], 1), :]),
                    )
                ):
                    rows_out[s, d, r : r + 1, t] = jnp.where(lane < length, first, pltpu.roll(second, length, 1))
    own_out[0] = rows_out[slot]


def merge(everyone, counts, ids, length, n_slot, n_pb, half):
    held = pltpu.VMEM((n_slot, n_pb, 2 * length), F32)
    return pl.pallas_call(
        functools.partial(merge_kernel, length),
        out_shape=[
            jax.ShapeDtypeStruct((n_slot, CORES, 8, half), F32),
            jax.ShapeDtypeStruct((1, CORES, 8, half), F32),
            jax.ShapeDtypeStruct((1, 2 * length), F32),
            jax.ShapeDtypeStruct((1, 1), F32),
        ],
        scratch_shapes=[held, held],
        compiler_params=limit(16 + 2 * everyone.size * 4 // MIB),
        cost_estimate=work(2),
    )(everyone, counts, ids)


def logit_gradient(x, rows, first):
    entry = (lax.broadcasted_iota(jnp.int32, x.shape, 0) + first).astype(F32)
    hit = jnp.where(entry == rows[2:3, :], 1.0, 0.0)
    return (rows[1:2, :] * (hit - jnp.exp(x - rows[0:1, :]))).astype(BF)


def state_grad_kernel(l_ref, rows_ref, e_ref, own_ref, pair_ref, d_ref, acc_ref):
    i = pl.program_id(0)
    half = own_ref.shape[0]

    @pl.when(i == 0)
    def _():
        acc_ref[...] = jnp.zeros_like(acc_ref)

    tile = l_ref.shape[0]
    d = [logit_gradient(l_ref[:, c * half : (c + 1) * half], rows_ref[0, c], i * tile) for c in range(CORES)]
    d_ref[...] = jnp.concatenate(d, axis=1)
    acc_ref[...] += dot(d_ref[...], e_ref[...], TN)

    @pl.when(i == pl.num_programs(0) - 1)
    def _():
        own_ref[...] = acc_ref[:half, :].astype(own_ref.dtype)
        pair_ref[...] = acc_ref[half:, :].astype(BF)


def state_grad(scores, rows, embedding, own_type):
    vocab, count = scores.shape
    width = embedding.shape[1]
    half = count // CORES
    tile = min(2 * VOCAB_TILE, vocab)
    last = pl.BlockSpec((half, width), lambda i: (0, 0))
    return pl.pallas_call(
        state_grad_kernel,
        grid=(vocab // tile,),
        in_specs=[
            pl.BlockSpec((tile, count), lambda i: (i, 0)),
            pl.BlockSpec((1,) + rows.shape[1:], lambda i: (0, 0, 0, 0)),
            pl.BlockSpec((tile, width), lambda i: (i, 0)),
        ],
        out_specs=[last, last, pl.BlockSpec((tile, count), lambda i: (i, 0))],
        out_shape=[
            jax.ShapeDtypeStruct((half, width), own_type),
            jax.ShapeDtypeStruct((half, width), BF),
            pltpu.HBM((vocab, count), BF),
        ],
        scratch_shapes=[pltpu.VMEM((count, width), F32)],
        compiler_params=limit(16 + 20 * half * tile // MIB + count * width * 4 // MIB),
        cost_estimate=work(11),
    )(in_hbm(scores), rows, embedding)


def own_embedding_kernel(d_ref, own_ref, pair_ref, *refs):
    half = own_ref.shape[0]
    refs[-1][...] = dot(d_ref[:, :half], own_ref[...]) + dot(d_ref[:, half:], pair_ref[...])


def own_embedding(d, own, pair, held, piece, count):
    vocab, tokens = d.shape
    tile = min(VOCAB_TILE, vocab // count)
    steps = vocab // count // tile
    ahead = [] if held is None else [held]
    whole = pl.BlockSpec(memory_space=pltpu.VMEM)
    shape = (vocab, own.shape[1])
    return pl.pallas_call(
        own_embedding_kernel,
        grid=(steps,),
        in_specs=[pl.BlockSpec((tile, tokens), lambda i: (piece * steps + i, 0)), whole, whole]
        + [pl.BlockSpec(memory_space=pl.ANY)] * len(ahead),
        out_specs=pl.BlockSpec((tile, shape[1]), lambda i: (piece * steps + i, 0)),
        out_shape=pltpu.HBM(shape, F32),
        input_output_aliases={3: 0} if ahead else {},
        compiler_params=limit(14),
        cost_estimate=work(1),
    )(d, own, pair, *ahead)


def embedding_kernel(base, rows_ref, own_ref, pair_ref, e_ref, held_ref, o_ref):
    first = base + pl.program_id(0) * e_ref.shape[0]
    slot = lax.axis_index("slot")
    o_ref[...] = held_ref[...]

    def other(k, carry):
        n = slot ^ k
        for top in range(0, own_ref.shape[1], TOKENS // CORES):
            t = slice(top, top + TOKENS // CORES)
            h = jnp.concatenate([own_ref[n, t, :], pair_ref[n, t, :]], axis=0)
            rows = jnp.concatenate([rows_ref[n, 0, :, t], rows_ref[n, 1, :, t]], axis=1)
            o_ref[...] += dot(logit_gradient(dot(e_ref[...], h, NT), rows, first), h)
        return carry

    lax.fori_loop(1, own_ref.shape[0], other, 0)


def embedding_piece(rows, states, embedding, held, first, size):
    width = embedding.shape[1]
    tile = min(VOCAB_TILE, size)
    steps = size // tile
    whole = pl.BlockSpec(memory_space=pltpu.VMEM)
    block = pl.BlockSpec((tile, width), lambda i: (first // tile + i, 0))
    return pl.pallas_call(
        functools.partial(embedding_kernel, first),
        grid=(steps,),
        in_specs=[whole, whole, whole, block, block],
        out_specs=block,
        out_shape=pltpu.HBM(embedding.shape, F32),
        input_output_aliases={4: 0},
        compiler_params=limit(24),
        cost_estimate=work(3 * size / 1024),
    )(rows, *states, embedding, held)


def add_kernel(mine, got, own_out, *send):
    length = own_out.shape[0]
    for k in range(CHIPS):
        s = slice(k * length, (k + 1) * length)
        y = mine[s, :] + got[s, :].astype(F32)
        if k == 0:
            own_out[...] = y
        else:
            send[k - 1][...] = y.astype(BF)


def norm_back_kernel(row, has_base, *refs):
    base = refs[0] if has_base else None
    mine, r1, r2, r3, z, inv, vec, dr_out, e_out, sums_out = refs[1 if has_base else 0 :]
    dh = mine[...] + r1[...].astype(F32) + r2[...].astype(F32) + r3[...].astype(F32)
    if has_base:
        dh = dh + base[...]
    dr = norm_back(dh, z[...], inv[...], vec[6 + row : 7 + row, :])
    e = dr.astype(BF)
    dr_out[...] = dr
    e_out[...] = e
    sums_out[...] = jnp.zeros_like(sums_out)
    sums_out[0:1, :] = jnp.sum(dh * z[...], axis=0, keepdims=True)
    sums_out[1:2, :] = jnp.sum(dh, axis=0, keepdims=True)
    sums_out[2:3, :] = jnp.sum(e.astype(F32), axis=0, keepdims=True)


def stack_rows(parts):
    return jnp.concatenate([p[...] for p in parts], axis=0)


def split_rows(y, mine_out, send):
    length = mine_out.shape[0]
    mine_out[...] = y[:length]
    for k in range(1, CHIPS):
        send[k - 1][...] = y[k * length : (k + 1) * length].astype(BF)


def column_sum(y):
    return jnp.sum(y.astype(F32), axis=0, keepdims=True)


def ffn_back_kernel(*refs):
    parts, (u_ref, up, down), (e_out, du_out, sum_out, mine_out), send = refs[:4], refs[4:7], refs[7:11], refs[11:]
    e = stack_rows(parts)
    e_out[...] = e
    da = dot(e, down[...], NT).astype(BF).astype(F32)
    u = u_ref[...]
    slope = gelu_parts(u) + u * (jnp.exp(-0.5 * u * u) * 0.3989422804014327)
    du = (da * slope).astype(BF)
    du_out[...] = du
    sum_out[...] = column_sum(du)
    split_rows(dot(du, up[...], NT), mine_out, send)


def pick_core(g, mine_out, other_out, top):
    _, core = place()
    lo, hi = g[:, :, 0], g[:, :, 1]
    n = lo.shape[1] * lo.shape[2]
    mine = jnp.where(core == 0, lo, hi).reshape(CHIPS, n, g.shape[-1])
    other = jnp.where(core == 0, hi, lo).reshape(CHIPS, n, g.shape[-1])
    mine_out[:, top : top + n, :] = mine.astype(BF)
    other_out[:, top : top + n, :] = other.astype(BF)


def place_columns(g, mine_out, other_out, top):
    unit = g.shape[0] // (CHIPS * CHIPS * CORES)
    pick_core(g.reshape(CHIPS, CHIPS, CORES, unit, g.shape[1]), mine_out, other_out, top)


def place_rows(g, mine_out, other_out, top):
    unit = g.shape[0] // (CHIPS * CORES)
    pick_core(g.reshape(CHIPS, 1, CORES, unit, g.shape[1]), mine_out, other_out, top)


def place_row_blocks(g, mine_out, other_out, top, lanes):
    unit = g.shape[0] // (CHIPS * CORES)
    for b in range(g.shape[1] // lanes):
        place_rows(g[:, b * lanes : (b + 1) * lanes], mine_out, other_out, top + b * unit)


def ffn_grads_kernel(low, du, a, e, mine_out, other_out):
    g = dot(low[...], du[...], TN)
    place_columns(g, mine_out, other_out, 0)
    g2 = dot(a[...], e[...], TN)
    place_rows(g2, mine_out, other_out, g.shape[0] // (CHIPS * CORES))


def cross_back_kernel(*refs):
    parts, (w_mine, w_cols, q_ref, k_ref, v_ref) = refs[:4], refs[4:9]
    (e_out, dq_out, dk_out, dv_out, mine_out), send, g_ref = refs[9:14], refs[14:-1], refs[-1]
    quarter = q_ref.shape[1]
    length, memory = q_ref.shape[0] // CHIPS, k_ref.shape[0] // CHIPS
    e = stack_rows(parts)
    e_out[...] = e
    g = dot(e, w_mine[1], NT).astype(BF)
    g_ref[...] = g

    def pair(i, carry):
        for j in range(2):
            s, t = rows_at((2 * i + j) * length, length, 16), rows_at((2 * i + j) * memory, memory, 16)
            dq_out[s, :], dk_out[t, :], dv_out[t, :] = attend_back(
                g_ref[s, :], q_ref[s, :], k_ref[t, :], v_ref[t, :], False
            )
        return carry

    lax.fori_loop(0, CHIPS // 2, pair, 0)
    split_rows(dot(dq_out[...], w_cols[:, :quarter], NT), mine_out, send)


def cross_grads_kernel(low, dq, m, dk, dv, o, e, mine_out, other_out, sums_out):
    n = low.shape[1] // (CHIPS * CORES)
    for j, (a, g) in enumerate(((low, dq), (m, dk), (m, dv))):
        place_columns(dot(a[...], g[...], TN), mine_out, other_out, j * n)
    place_row_blocks(dot(o[...], e[...], TN), mine_out, other_out, 3 * n, dq.shape[1])
    sums_out[...] = jnp.zeros_like(sums_out)
    sums_out[0:1, :] = column_sum(dq[...])
    sums_out[1:2, :] = column_sum(dv[...])


def self_back_kernel(*refs):
    parts, (w_mine, q_ref, k_ref, v_ref), (e_out, d_out, g_ref) = refs[:4], refs[4:8], refs[8:]
    quarter = q_ref.shape[1]
    length = q_ref.shape[0] // CHIPS
    e = stack_rows(parts)
    e_out[...] = e
    g = dot(e, w_mine[0], NT).astype(BF)
    g_ref[...] = g

    def pair(i, carry):
        for j in range(2):
            s = rows_at((2 * i + j) * length, length, 16)
            dq, dk, dv = attend_back(g_ref[s, :], q_ref[s, :], k_ref[s, :], v_ref[s, :], True)
            d_out[s, :quarter] = dq
            d_out[s, quarter : 2 * quarter] = dk
            d_out[s, 2 * quarter :] = dv
        return carry

    lax.fori_loop(0, CHIPS // 2, pair, 0)


SMALL = 16


def self_grads_kernel(x, d, o, e, c_sums, sum_in, one, two, three, mine_out, other_out):
    chip, core = place()
    quarter = d.shape[1] // 3
    n = x.shape[1] // (CHIPS * CORES)
    g = dot(x[...], d[...], TN)
    for j in range(3):
        place_columns(g[:, j * quarter : (j + 1) * quarter], mine_out, other_out, j * n)
    place_row_blocks(dot(o[...], e[...], TN), mine_out, other_out, 3 * n, quarter)

    def spread(row):
        zero = jnp.zeros_like(row)
        return jnp.concatenate([jnp.where(chip == b, row, zero) for b in range(CHIPS)], axis=1)

    rows = [
        spread(column_sum(d[:, :quarter])), spread(column_sum(d[:, 2 * quarter :])), one[2:3, :],
        spread(c_sums[0:1, :]), spread(c_sums[1:2, :]), two[2:3, :], one[0:1, :], two[0:1, :], three[0:1, :],
        one[1:2, :], two[1:2, :], three[1:2, :], three[2:3, :],
    ]
    v = jnp.concatenate(rows + [jnp.zeros((SMALL - len(rows), x.shape[1]), F32)], axis=0)
    unit = x.shape[1] // (CHIPS * CHIPS * CORES)
    wide = sum_in.shape[1] // (CHIPS * CORES)
    last = sum_in[...]
    top = 4 * n
    for out in (mine_out, other_out):
        out[:, top:, :] = jnp.zeros((CHIPS, 2 * SMALL, quarter), BF)
    for s in range(CHIPS):
        halves, ends = [], []
        for c in range(CORES):
            parts = [v[:, ((s * CHIPS + b) * CORES + c) * unit :][:, :unit] for b in range(CHIPS)]
            halves.append(jnp.concatenate(parts, axis=1))
            ends.append(last[:, (s * CORES + c) * wide :][:, :wide])
        for out, swap in ((mine_out, False), (other_out, True)):
            first = (core == 0) != swap
            out[s, top : top + SMALL, : CHIPS * unit] = jnp.where(first, halves[0], halves[1]).astype(BF)
            out[s, top + SMALL : top + SMALL + 1, :wide] = jnp.where(first, ends[0], ends[1]).astype(BF)


def input_back_kernel(d, w_self, dk, dv, w_cross, mine_out, *send):
    quarter = dk.shape[1]
    length, memory = d.shape[0] // CHIPS, dk.shape[0] // CHIPS
    y = dot(d[...], w_self[...], NT)
    m = dot(dk[...], w_cross[:, quarter : 2 * quarter], NT) + dot(dv[...], w_cross[:, 2 * quarter :], NT)
    for k, out in enumerate((mine_out, *send)):
        out[:length, :] = y[k * length : (k + 1) * length].astype(out.dtype)
        out[length:, :] = m[k * memory : (k + 1) * memory].astype(out.dtype)


def input_total_kernel(base, mine, r1, r2, r3, source_out, memory_out):
    length = base.shape[0]
    y = mine[...] + r1[...].astype(F32) + r2[...].astype(F32) + r3[...].astype(F32)
    source_out[...] = base[...] + y[:length]
    memory_out[...] = y[length:]


def core_sum_kernel(mine, got, out):
    for n in range(SLOTS):
        out[n] = (mine[n].astype(F32) + got[n].astype(F32)).astype(BF)


def column_pieces_kernel(count, got, *outs):
    *pieces, rest = outs
    chip, _ = place()
    unit = pieces[0].shape[0] // count
    y = sum(got[n].astype(F32) for n in range(SLOTS))
    top = count * CHIPS * unit
    rest[...] = y[top:].astype(BF)
    hold = y[:top].astype(BF).reshape(count, CHIPS, unit, y.shape[1])
    for k in range(CHIPS):
        for j in range(count):
            block = jnp.zeros((unit, y.shape[1]), BF)
            for b in range(CHIPS):
                block = jnp.where((chip ^ k) == b, hold[j, b], block)
            pieces[k][j * unit : (j + 1) * unit, :] = block


def attn_pieces_kernel(s_got, c_got, *outs):
    *pieces, rest = outs
    chip, _ = place()
    s = sum(s_got[n].astype(F32) for n in range(SLOTS)).astype(BF)
    c = sum(c_got[n].astype(F32) for n in range(SLOTS)).astype(BF)
    top = 3 * c.shape[0] // 4
    unit = top // (3 * CHIPS)
    both = [y[:top].reshape(3, CHIPS, unit, y.shape[1]) for y in (s, c)]
    for k in range(CHIPS):
        for m, y in enumerate(both):
            for j in range(3):
                block = jnp.zeros((unit, y.shape[3]), BF)
                for b in range(CHIPS):
                    block = jnp.where((chip ^ k) == b, y[j, b], block)
                pieces[k][(3 * m + j) * unit : (3 * m + j + 1) * unit, :] = block
        pieces[k][6 * unit :, :] = s[c.shape[0] : c.shape[0] + SMALL]
    n = c.shape[0] - top
    rest[:n, :] = s[top : top + n]
    rest[n : 2 * n, :] = c[top:]
    rest[2 * n :, :] = s[c.shape[0] + SMALL :]


def attn_out_kernel(p0, p1, p2, p3, out, bias_out, gain_out, shift_out, last_out):
    chip, _ = place()
    unit, quarter = out.shape[1], p0.shape[1]
    parts = (p0, p1, p2, p3)
    for k, p in enumerate(parts):
        lanes = rows_at((chip ^ k) * quarter, quarter, 128)
        for j in range(6):
            out[j, :, lanes] = p[j * unit : (j + 1) * unit, :].astype(F32)
    total = sum(p[6 * unit :, : CHIPS * unit].astype(F32) for p in parts)
    mine = jnp.zeros((SMALL, unit), F32)
    for b in range(CHIPS):
        mine = jnp.where(chip == b, total[:, b * unit : (b + 1) * unit], mine)
    columns = jnp.transpose(jnp.concatenate([mine, jnp.zeros((SMALL, 128 - unit), F32)], axis=1))
    bias_out[...] = columns[:unit, 0:6]
    gain_out[...] = columns[:unit, 6:9]
    shift_out[...] = columns[:unit, 9:12]
    last_out[...] = mine[12:13, :]


def rows_out_kernel(owned, f_owned, out, down_out, in_out):
    unit, quarter = out.shape[1], owned.shape[1]
    n = CHIPS * unit
    for m in range(2):
        for b in range(CHIPS):
            out[m, :, b * quarter : (b + 1) * quarter] = owned[m * n + b * unit : m * n + (b + 1) * unit, :].astype(F32)
    down_out[...] = f_owned[...].astype(F32)
    in_out[...] = owned[2 * n : 2 * n + 1, : in_out.shape[1]].astype(F32)


def up_out_kernel(p0, p1, p2, p3, out):
    chip, _ = place()
    quarter = p0.shape[1]
    for k, p in enumerate((p0, p1, p2, p3)):
        out[:, rows_at((chip ^ k) * quarter, quarter, 128)] = p[...].astype(F32)


def shards(
    inputs, memory, attn_weight, attn_out, ffn_in, ffn_out, attn_bias, norm_gain, norm_bias,
    bias_in, bias_out, embedding, targets, slot_counts, pad_mask, log_prior,
):
    n_pb, n_slot = lax.axis_size("pb"), lax.axis_size("slot")
    n_all = n_pb * n_slot
    teams = n_pb // TEAM
    me = lax.axis_index("pb")
    length, width = inputs.shape[2], inputs.shape[3]
    passage = memory.shape[2]
    quarter = width // CHIPS
    unit = width // (TEAM * n_slot)
    vocab_rows = embedding.shape[0]
    embedding = in_hbm(embedding)

    def team_rows(w):
        if teams == 1:
            return w
        w = lax.all_gather(w, "pb", axis=0, tiled=True)
        n = w.shape[0] // TEAM
        return lax.dynamic_slice_in_dim(w, (me % TEAM) * n, n)

    x, m = inputs[0, 0], memory[0, 0]
    attn_w = jnp.moveaxis(team_rows(attn_weight), 1, 0)
    out_w = jnp.moveaxis(team_rows(attn_out), 1, 0)
    up_w = team_rows(ffn_in)
    down_w = team_rows(ffn_out)
    rows = attn_w.shape[1]
    ff = up_w.shape[1] // CHIPS
    vec = jnp.concatenate(
        [attn_bias.T, norm_gain.T, norm_bias.T, bias_out[None], bias_in.reshape(CHIPS, -1)], axis=0
    )
    ids = (targets - me * vocab_rows).astype(jnp.int32)
    own_row = jnp.concatenate([pad_mask.astype(F32), jnp.broadcast_to(log_prior, (1, length))], axis=1)

    block = (length, width)
    every = (CHIPS * length, width)
    cols = (CHIPS * length, quarter)
    m_cols = (CHIPS * passage, quarter)
    sends = [(block, BF)] * 3

    def give(send):
        return [from_chip(send[k - 1], k) for k in range(1, CHIPS)]

    def give_far(send):
        return [in_hbm(r) for r in give(send)]

    far_call = functools.partial(call, far=True)

    first = call(functools.partial(pack_kernel, 6, 0), [((CHIPS * length + 6 * rows, quarter), BF)] * CHIPS, x, attn_w)
    got_first = [first[0]] + give(first[1:])
    got_first[1], vec = tie(got_first[1], vec)
    pair_first = [from_core(g) for g in got_first]
    out_pair = from_core(out_w)
    down_pair = from_core(down_w)
    third = list(call(functools.partial(pack_kernel, 1, 0), [((rows, ff), BF)] * CHIPS, up_w[None]))
    m_send, pair_first[3] = tie(m, pair_first[3])
    got_memory = [m, from_chip(m_send, 1), from_chip(m_send, 2)]

    x_all, w_self, queries, keys, values, mixed, w_out, mine, *send = call(
        self_kernel,
        [(every, BF), ((width, 3 * quarter), BF)] + [(cols, BF)] * 4 + [((2, quarter, width), BF), (block, F32)]
        + sends,
        *got_first, *pair_first, out_w, out_pair, vec,
    )
    got = give(send)
    got_memory[1], got_memory[2], *got = tie(got_memory[1], got_memory[2], *got)
    norm_outs = [(block, F32), (block, BF), (block, F32), ((length, 1), F32)]
    hidden_one, low_one, z_one, inv_one = call(
        functools.partial(norm_kernel, (2, 6, 9)), norm_outs, x, mine, *got, vec, us=1
    )
    got_low = [low_one] + others(low_one)
    m_send, got_memory[1] = tie(m, got_memory[1])
    got_memory.append(from_chip(m_send, 3))
    m_all, w_cross, cross_keys, cross_values = call(
        memory_kernel, [((CHIPS * passage, width), BF), ((width, 3 * quarter), BF)] + [(m_cols, BF)] * 2,
        *got_memory, *got_first, *pair_first, vec,
    )
    third[1], third[2], *got_low = tie(third[1], third[2], *got_low)
    got_third = [third[0], from_chip(third[1], 1), from_chip(third[2], 2)]
    low_one_all, cross_queries, cross_mixed, mine, *send = call(
        cross_kernel, [(every, BF), (cols, BF), (cols, BF), (block, F32)] + sends,
        *got_low, w_out, w_cross, cross_keys, cross_values, vec,
    )
    got = give(send)
    got_third[1], got_third[2], *got = tie(got_third[1], got_third[2], *got)
    hidden_two, low_two, z_two, inv_two = call(
        functools.partial(norm_kernel, (5, 7, 10)), norm_outs, hidden_one, mine, *got, vec, us=1
    )
    got_low = [low_two] + others(low_two)
    third[3], got_third[1] = tie(third[3], got_third[1])
    got_third.append(from_chip(third[3], 3))
    (up_half,) = call(up_half_kernel, [((CHIPS, rows, ff), BF)], *got_third)
    up_half_pair = from_core(up_half)
    low_two_all, upward, active, w_up, w_down, mine, *send = call(
        ffn_kernel,
        [(every, BF), ((CHIPS * length, ff), F32), ((CHIPS * length, ff), BF), ((width, ff), BF)]
        + [((ff, width), BF), (block, F32)]
        + sends,
        *got_low, up_half, up_half_pair, down_w, down_pair, vec,
    )
    got = give(send)
    _, final_low, z_three, inv_three = call(
        functools.partial(norm_kernel, (12, 8, 11)), norm_outs, hidden_two, mine, *got, vec, us=1
    )

    held, spread_held = call(
        stack_kernel, [(every, BF), ((n_slot,) + every, BF)], final_low, *others(final_low), us=1
    )
    pair = from_core(held)

    def all_teams(h):
        return lax.all_gather(h, "pb", axis_index_groups=same_place_groups(), axis=0, tiled=True) if teams > 1 else h

    half = teams * CHIPS * length
    chip, core = place()
    order = [
        t * TEAM + (chip ^ k) * CORES + (core ^ d) for d in range(CORES) for t in range(teams) for k in range(CHIPS)
    ]
    ids_row = jnp.concatenate([lax.dynamic_slice_in_dim(ids, q, 1) for q in order], axis=1)
    states = [all_teams(held), all_teams(pair)]
    scores, payload = logits(*states, ids_row, own_row, embedding, length, n_pb)
    everyone = lax.all_to_all(
        jnp.broadcast_to(payload[None], (n_all,) + payload.shape), ("slot", "pb"), 0, 0, tiled=True
    )
    ids_wide = jnp.pad(ids.astype(F32), ((0, 0), (0, length)))
    spread_held, everyone = tie(spread_held, everyone)
    all_held = across_slots(spread_held)
    token_rows, own_rows, token_logprob, prior_grad = merge(
        everyone, slot_counts.astype(jnp.int32)[:, None], ids_wide, length, n_slot, n_pb, half
    )
    def home(partial):
        if teams == 1:
            return partial
        return lax.psum_scatter(partial, "pb", axis_index_groups=same_place_groups(), scatter_dimension=0, tiled=True)

    own_part, for_pair, own_logits = state_grad(scores, own_rows, embedding, F32)
    own_logits = in_hbm(own_logits)
    own_part, got_pair = home(own_part), from_core(home(for_pair))
    mine, *send = call(add_kernel, [(block, F32)] + sends, own_part, got_pair, us=1)
    got = give(send)
    own_logits, send[0] = tie(own_logits, send[0])
    own_terms = own_embedding(own_logits, *states, None, 0, 2)
    own_terms, *got = tie(own_terms, *got)

    eighth = vocab_rows // 8
    parts = (1, 1, 1, 5)
    made = []

    def piece(*wait):
        n = len(made) - 1
        rows_in, *wait = tie(token_rows, *wait)
        first = sum(parts[:n]) * eighth
        made.append(embedding_piece(rows_in, states, embedding, made[-1], first, parts[n] * eighth))
        return wait

    def pieces(count, *wait):
        for _ in range(count):
            wait = piece(*wait)
        return list(wait)

    def then(*values):
        *values, made[-1] = tie(*values, made[-1])
        return values

    def settle(g):
        if teams == 1:
            return g
        g = lax.psum(g, "pb", axis_index_groups=same_place_groups())
        g = lax.all_gather(g, "pb", axis_index_groups=team_groups(), axis=0, tiled=True)
        n = g.shape[0] // n_pb
        return lax.dynamic_slice_in_dim(g, me * n, n)

    def to_owner(g):
        pairs = []
        for s in range(n_slot):
            for i in range(n_pb):
                t, b, c = i // TEAM, (i % TEAM) // CORES, i % CORES
                pairs.append((s * n_pb + i, b * n_pb + t * TEAM + s * CORES + c))
        return lax.ppermute(g, ("slot", "pb"), pairs)

    def column_pieces(count, got, n, cols):
        rest = got.shape[1] - count * CHIPS * n
        *piece, rest = call(
            functools.partial(column_pieces_kernel, count),
            [((count * n, cols), BF)] * CHIPS + [((rest, cols), BF)], got,
        )
        return [piece[0]] + give_far(piece[1:]), rest

    x_all, w_self, queries, keys, values, mixed, w_out, m_all, w_cross, cross_keys, cross_values = (
        in_hbm(v)
        for v in (x_all, w_self, queries, keys, values, mixed, w_out, m_all, w_cross, cross_keys, cross_values)
    )
    low_one_all, cross_queries, cross_mixed, low_two_all, upward, active, w_up, w_down = (
        in_hbm(v) for v in (low_one_all, cross_queries, cross_mixed, low_two_all, upward, active, w_up, w_down)
    )
    z_one, z_two, z_three = in_hbm(z_one), in_hbm(z_two), in_hbm(z_three)
    grads = [(block, F32), (block, BF), ((8, width), F32)]
    dr_three, e_three, sums_three = call(
        functools.partial(norm_back_kernel, 2, False), grads, mine, *got, z_three, inv_three, vec, us=1
    )
    got_e = others(e_three)
    own_logits, e_three = tie(own_logits, e_three)
    own_terms = own_embedding(own_logits, *states, own_terms, 1, 2)
    own_terms, *got_e = tie(own_terms, *got_e)
    made.append(own_terms)
    e_all, du, sum_in, mine, *send = call(
        ffn_back_kernel,
        [(every, BF), ((CHIPS * length, ff), BF), ((1, ff), F32), (block, F32)] + sends,
        e_three, *got_e, upward, w_up, w_down,
    )
    got = give_far(send)
    f_shape = (n_slot, CHIPS * unit + ff // TEAM, width)
    du, send[0] = tie(du, send[0])
    f_mine, f_other = call(ffn_grads_kernel, [(f_shape, BF)] * 2, low_two_all, du, active, e_all, us=3)
    f_other, all_held, *got = tie(f_other, all_held, *got)
    all_pair = from_core(all_held)
    dr_two, e_two, sums_two = far_call(
        functools.partial(norm_back_kernel, 1, True), grads, dr_three, mine, *got, z_two, inv_two, vec, us=1
    )
    got_e = give_far([e_two] * 3)
    f_got = from_core(f_other)
    f_got, all_pair, e_two = tie(f_got, all_pair, e_two)
    states = [jnp.stack([all_teams(h[n]) for n in range(n_slot)]) if teams > 1 else h for h in (all_held, all_pair)]
    (f_total,) = far_call(core_sum_kernel, [(f_shape, BF)], f_mine, f_got)
    f_got = across_slots(f_total)
    e_all_two, dqc, dkc, dvc, mine, *send = far_call(
        cross_back_kernel,
        [(every, BF), (cols, BF), (m_cols, BF), (m_cols, BF), (block, F32)] + sends,
        e_two, *got_e, w_out, w_cross, cross_queries, cross_keys, cross_values, us=5,
        scratch=[pltpu.VMEM(cols, BF)],
    )
    got = give_far(send)
    dqc, send[0] = tie(dqc, send[0])
    g_shape = (n_slot, 4 * CHIPS * unit, quarter)
    c_mine, c_other, c_sums = call(
        cross_grads_kernel, [(g_shape, BF)] * 2 + [((8, quarter), F32)],
        low_one_all, dqc, m_all, dkc, dvc, cross_mixed, e_all_two,
    )
    c_got = from_core(c_other)
    (c_mine,) = piece(c_mine)
    got = then(*got)
    dr_one, e_one, sums_one = far_call(
        functools.partial(norm_back_kernel, 0, True), grads, dr_two, mine, *got, z_one, inv_one, vec, us=1
    )
    got_e = give_far([e_one] * 3)
    c_got, e_one = tie(c_got, e_one)
    (c_total,) = far_call(core_sum_kernel, [(g_shape, BF)], c_mine, c_got)
    (c_total,) = piece(c_total)
    f_got, *got_e = then(f_got, *got_e)
    e_all_one, d_self = far_call(
        self_back_kernel, [(every, BF), ((CHIPS * length, 3 * quarter), BF)], e_one, *got_e, w_out, queries, keys, values, us=4,
        scratch=[pltpu.VMEM(cols, BF)],
    )
    c_total, d_self = tie(c_total, d_self)
    c_got = across_slots(c_total)
    s_shape = (n_slot, g_shape[1] + 2 * SMALL, quarter)
    s_mine, s_other = far_call(
        self_grads_kernel, [(s_shape, BF)] * 2, x_all, d_self, mixed, e_all_one, c_sums, sum_in, sums_one, sums_two, sums_three
    )
    s_got = from_core(s_other)
    f_got, s_mine = tie(f_got, s_mine)
    f_pieces, f_rest = column_pieces(1, f_got, unit, width)
    f_owned = to_owner(f_rest)
    d_self, f_rest = tie(d_self, f_rest)
    both = (length + passage, width)
    mine, *send = far_call(input_back_kernel, [(both, F32)] + [(both, BF)] * 3, d_self, w_self, dkc, dvc, w_cross, us=3)
    s_got, send[0] = tie(s_got, send[0])
    (s_total,) = far_call(core_sum_kernel, [(s_shape, BF)], s_mine, s_got)
    (s_total,) = pieces(1, s_total)
    c_got, *f_pieces = then(c_got, *f_pieces)
    s_total, send[0], c_got = tie(s_total, send[0], c_got)
    s_got = across_slots(s_total)
    got = give_far(send)
    (out_up,) = call(up_out_kernel, [((unit, up_w.shape[1]), F32)], *f_pieces, us=1)
    (out_up,) = pieces(len(parts) + 1 - len(made), out_up)
    s_got, *got = then(s_got, *got)
    *piece_parts, rest = call(
        attn_pieces_kernel,
        [((6 * unit + SMALL, quarter), BF)] * CHIPS + [((2 * CHIPS * unit + SMALL, quarter), BF)],
        s_got, c_got,
    )
    last = give(piece_parts[1:])
    owned = to_owner(rest)
    grad_source, grad_passage = call(
        input_total_kernel, [(block, F32), ((passage, width), F32)], dr_one, mine, *got, us=1
    )
    owned, grad_source, *last = tie(owned, grad_source, *last)
    out_attn, *vectors = call(
        attn_out_kernel,
        [((6, unit, width), F32), ((unit, 6), F32), ((unit, 3), F32), ((unit, 3), F32), ((1, unit), F32)],
        piece_parts[0], *last, us=1,
    )
    outs, out_down, sum_in_out = call(
        rows_out_kernel, [((2, unit, width), F32), (f_rest.shape, F32), ((1, ff // TEAM), F32)], owned, f_owned, us=1
    )
    out_attn = settle(jnp.moveaxis(out_attn, 0, 1))
    out_outputs = settle(jnp.moveaxis(outs, 0, 1))
    out_up, out_down = settle(out_up), settle(out_down)
    vectors = [settle(v) for v in (*vectors[:3], sum_in_out[0], vectors[3][0])]
    return (
        token_logprob[:, :length],
        grad_source[None, None],
        grad_passage[None, None],
        prior_grad,
        out_attn,
        out_outputs,
        out_up,
        out_down,
        vectors[0],
        vectors[1],
        vectors[2],
        vectors[3],
        vectors[4],
        made[-1],
    )


def solution(mesh):
    placed = (
        P("pb", "slot", None, None),
        P("pb", "slot", None, None),
        P("pb", None, None),
        P("pb", None, None),
        P("pb", None),
        P("pb", None),
        P(),
        P(),
        P(),
        P(),
        P(),
        P("pb", None),
        P(),
        P(),
        P("pb", None),
        P("pb", "slot"),
    )
    both = ("slot", "pb")
    return jax.shard_map(
        shards,
        mesh=mesh,
        in_specs=placed,
        out_specs=(
            P("pb", None),
            P("pb", "slot", None, None),
            P("pb", "slot", None, None),
            P("pb", "slot"),
            P(both, None, None),
            P(both, None, None),
            P(both, None),
            P(both, None),
            P(both, None),
            P(both, None),
            P(both, None),
            P(both),
            P(both),
            P("pb", None),
        ),
        check_vma=False,
    )
```

```python
import functools

import jax
import jax.numpy as jnp
from jax import lax
from jax.experimental import pallas as pl
from jax.experimental.pallas import tpu as pltpu
from jax.sharding import PartitionSpec as P

HEAD = 64
CHIPS = 4
CORES = 2
TEAM = CHIPS * CORES
SLOTS = 4
BF = jnp.bfloat16
F32 = jnp.float32
TOKENS = 512
VOCAB_TILE = 512


def from_chip(x, k):
    pairs = []
    for i in range(lax.axis_size("pb")):
        place = i % TEAM
        pairs.append((i, i - place + ((place // CORES) ^ k) * CORES + place % CORES))
    return lax.ppermute(x, "pb", pairs)


def from_core(x):
    return lax.ppermute(x, "pb", [(i, i ^ 1) for i in range(lax.axis_size("pb"))])


def across_slot(x, k):
    return lax.ppermute(x, "slot", [(i, i ^ k) for i in range(lax.axis_size("slot"))])


def same_place_groups():
    size = lax.axis_size("pb")
    return [[g * TEAM + j for g in range(size // TEAM)] for j in range(TEAM)]


def team_groups():
    size = lax.axis_size("pb")
    return [[g * TEAM + j for j in range(TEAM)] for g in range(size // TEAM)]


def others(x):
    return [from_chip(x, k) for k in range(1, CHIPS)]


def tie(*values):
    return list(lax.optimization_barrier(values))


def across_slots(x):
    return lax.all_to_all(x, "slot", 0, 0, tiled=True)


def at(x, index):
    return lax.dynamic_index_in_dim(x, index, 0, False)


NN = (((1,), (0,)), ((), ()))
NT = (((1,), (1,)), ((), ()))
TN = (((0,), (0,)), ((), ()))


def dot(a, b, dims=NN):
    return lax.dot_general(a, b, dims, preferred_element_type=F32)


def place():
    j = lax.axis_index("pb") % TEAM
    return j // CORES, j % CORES


def rows_at(start, size, unit):
    return pl.ds(pl.multiple_of(start, unit), size)


MIB = 2**20


def limit(mib):
    return pltpu.CompilerParams(vmem_limit_bytes=min(60, mib) * MIB)


def work(us):
    return pl.CostEstimate(flops=int(us * 1e9), bytes_accessed=0, transcendentals=0)


def call(kernel, outs, *args, us=2.0, far=(), scratch=()):
    shapes = [jax.ShapeDtypeStruct(*o) for o in outs]
    held = sum(a.size * a.dtype.itemsize for a in (*args, *shapes))
    params = limit(8 + held * 5 // 4 // MIB)
    far = range(len(outs)) if far is True else far
    places = [pltpu.HBM(*o) if n in far else s for n, (o, s) in enumerate(zip(outs, shapes))]
    results = pl.pallas_call(
        kernel, out_shape=places, scratch_shapes=scratch, compiler_params=params, cost_estimate=work(us)
    )(*args)
    return [in_hbm(r) if n in far else r for n, r in enumerate(results)]


def in_hbm(x):
    return pltpu.with_memory_space_constraint(x, pltpu.HBM)


def norm_rows(r, gain, shift):
    centered = r - jnp.mean(r, axis=-1, keepdims=True)
    inv = lax.rsqrt(jnp.mean(centered * centered, axis=-1, keepdims=True) + 1e-05)
    z = centered * inv
    return z * gain + shift, z, inv


def norm_back(dh, z, inv, gain):
    dz = dh * gain
    return (dz - jnp.mean(dz, axis=-1, keepdims=True) - z * jnp.mean(dz * z, axis=-1, keepdims=True)) * inv


def lane_head(shape, keys):
    return lax.broadcasted_iota(jnp.int32, shape, 1) // keys


def per_head(x):
    head = lane_head(x.shape, HEAD)
    return jnp.concatenate([jnp.where(head == h, x, jnp.zeros_like(x)) for h in range(x.shape[1] // HEAD)], axis=0)


def own_heads(big, keys):
    count = big.shape[1] // HEAD
    head = lane_head((keys, big.shape[1]), HEAD)
    total = jnp.zeros((keys, big.shape[1]), F32)
    for h in range(count):
        total = total + jnp.where(head == h, big[h * keys : (h + 1) * keys], 0.0)
    return total


def head_probs(q, kbig, keys, causal):
    s = dot(q, kbig, NT) * 0.125
    head = lane_head(s.shape, keys)
    count = s.shape[1] // keys
    if causal:
        query = lax.broadcasted_iota(jnp.int32, s.shape, 0)
        key = lax.broadcasted_iota(jnp.int32, s.shape, 1) % keys
        s = jnp.where(query >= key, s, -1e30)
    peak = jnp.zeros_like(s)
    for h in range(count):
        m = jnp.max(jnp.where(head == h, s, -3e38), axis=1, keepdims=True)
        peak = jnp.where(head == h, m, peak)
    e = jnp.exp(s - peak)
    return e / head_sums(e, head, count)


def head_sums(x, head, count):
    total = jnp.zeros_like(x)
    for h in range(count):
        total = jnp.where(head == h, jnp.sum(jnp.where(head == h, x, 0.0), axis=1, keepdims=True), total)
    return total


def attend(q, k, v, causal):
    probs = head_probs(q, per_head(k), k.shape[0], causal)
    return dot(probs.astype(BF), per_head(v)).astype(BF)


def attend_back(g, q, k, v, causal):
    keys = k.shape[0]
    kbig, vbig = per_head(k), per_head(v)
    probs = head_probs(q, kbig, keys, causal)
    dp = dot(g, vbig, NT)
    head = lane_head(dp.shape, keys)
    ds = (probs * (dp - head_sums(dp * probs, head, dp.shape[1] // keys))).astype(BF)
    dq = dot(ds, kbig) * 0.125
    dk = own_heads(dot(ds, q, TN), keys) * 0.125
    dv = own_heads(dot(probs.astype(BF), g, TN), keys)
    return dq.astype(BF), dk.astype(BF), dv.astype(BF)


def pack_kernel(count, first, *refs):
    *rows_in, w_ref, o0, o1, o2, o3 = refs
    outs = (o0, o1, o2, o3)
    chip, _ = place()
    rows, quarter = w_ref.shape[1], w_ref.shape[2] // CHIPS
    for k in range(CHIPS):
        top = 0
        for x_ref in rows_in:
            x = x_ref[...]
            for b in range(CHIPS):
                outs[k][top : top + x.shape[0], :] = x[:, b * quarter : (b + 1) * quarter]
                top += x.shape[0]
        for j in range(count):
            outs[k][top : top + rows, :] = w_ref[first + j, :, rows_at((chip ^ k) * quarter, quarter, 128)]
            top += rows


def natural_columns(own, pair, w_out, top, count):
    chip, core = place()
    rows = w_out.shape[0] // TEAM
    quarter = own[0].shape[1]
    for k in range(CHIPS):
        for refs, c in ((own, core), (pair, 1 - core)):
            start = (chip ^ k) * (CORES * rows) + c * rows
            for j in range(count):
                w_out[rows_at(start, rows, 16), j * quarter : (j + 1) * quarter] = refs[k][
                    top + j * rows : top + (j + 1) * rows, :
                ]


def half_columns(parts, out, top, count):
    chip, _ = place()
    rows = (parts[0].shape[0] - top) // count
    quarter = parts[0].shape[1]
    for k in range(CHIPS):
        for j in range(count):
            out[chip ^ k, :, j * quarter : (j + 1) * quarter] = parts[k][top + j * rows : top + (j + 1) * rows, :]


def whole_columns(mine, pair, out):
    _, core = place()
    rows = mine.shape[1]
    for b in range(CHIPS):
        for part, c in ((mine, core), (pair, 1 - core)):
            out[rows_at(b * CORES * rows + c * rows, rows, 16), :] = part[b]


def pair_rows(own, pair):
    _, core = place()
    a, b = own[...], pair[...]
    return jnp.concatenate([jnp.where(core == 0, a, b), jnp.where(core == 0, b, a)], axis=0)


def self_kernel(*refs):
    own, pair, (o_own, o_pair, vec) = refs[:4], refs[4:8], refs[8:11]
    x_out, w_out, q_out, k_out, v_out, o_out, wo_out, mine_out = refs[11:19]
    send = refs[19:]
    chip, _ = place()
    quarter = own[0].shape[1]
    length = x_out.shape[0] // CHIPS
    natural_columns(own, pair, w_out, CHIPS * length, 3)
    for k in range(CHIPS):
        for b in range(CHIPS):
            x_out[k * length : (k + 1) * length, b * quarter : (b + 1) * quarter] = own[k][b * length : (b + 1) * length, :]
    for j in range(2):
        wo_out[j] = pair_rows(o_own.at[j], o_pair.at[j])
    lanes = rows_at(chip * quarter, quarter, 128)
    y = dot(x_out[...], w_out[...])
    q = (y[:, :quarter] + vec[0:1, lanes]).astype(BF)
    k = y[:, quarter : 2 * quarter].astype(BF)
    v = (y[:, 2 * quarter :] + vec[1:2, lanes]).astype(BF)
    q_out[...], k_out[...], v_out[...] = q, k, v

    def pair(i, carry):
        for j in range(2):
            s = rows_at((2 * i + j) * length, length, 16)
            o_out[s, :] = attend(q_out[s, :], k_out[s, :], v_out[s, :], True)
        return carry

    lax.fori_loop(0, CHIPS // 2, pair, 0)
    split_rows(dot(o_out[...], wo_out[0]), mine_out, send)


def half_kernel(*refs):
    half_columns(refs[:4], refs[4], 0, 3)


def memory_kernel(*refs):
    mem, own, pair, vec, (m_out, w_out, k_out, v_out) = refs[:4], refs[4:8], refs[8:12], refs[12], refs[13:]
    chip, _ = place()
    quarter = k_out.shape[1]
    natural_columns(own, pair, w_out, own[0].shape[0] - 3 * w_out.shape[0] // TEAM, 3)
    m_out[...] = stack_rows(mem)
    y = dot(m_out[...], w_out[:, quarter:])
    k_out[...] = y[:, :quarter].astype(BF)
    v_out[...] = (y[:, quarter:] + vec[4:5, rows_at(chip * quarter, quarter, 128)]).astype(BF)


def norm_kernel(rows, *refs):
    base, mine, r1, r2, r3, vec, h_out, low_out, z_out, inv_out = refs
    y = mine[...] + r1[...].astype(F32) + r2[...].astype(F32) + r3[...].astype(F32)
    r = base[...].astype(F32) + y + vec[rows[0] : rows[0] + 1, :]
    h, z, inv = norm_rows(r, vec[rows[1] : rows[1] + 1, :], vec[rows[2] : rows[2] + 1, :])
    h_out[...] = h
    low_out[...] = h.astype(BF)
    z_out[...] = z
    inv_out[...] = inv


def cross_kernel(*refs):
    parts, (wo, w_cols, keys, values, vec), (low_out, q_out, o_out, mine_out), send = refs[:4], refs[4:9], refs[9:13], refs[13:]
    chip, _ = place()
    quarter = keys.shape[1]
    length = parts[0].shape[0]
    memory = keys.shape[0] // CHIPS
    low = stack_rows(parts)
    low_out[...] = low
    q = (dot(low, w_cols[:, :quarter]) + vec[3:4, rows_at(chip * quarter, quarter, 128)]).astype(BF)
    q_out[...] = q

    def pair(i, carry):
        for j in range(2):
            s, t = rows_at((2 * i + j) * length, length, 16), rows_at((2 * i + j) * memory, memory, 16)
            o_out[s, :] = attend(q_out[s, :], keys[t, :], values[t, :], False)
        return carry

    lax.fori_loop(0, CHIPS // 2, pair, 0)
    split_rows(dot(o_out[...], wo[1]), mine_out, send)


def gelu_parts(u):
    phi = 0.5 * (1.0 + lax.erf(u * 0.7071067811865476))
    return phi


def up_half_kernel(*refs):
    half_columns(refs[:4], refs[4], 0, 1)


def ffn_kernel(*refs):
    parts, (up_mine, up_pair, down_own, down_pair, vec) = refs[:4], refs[4:9]
    low_out, u_out, a_out, up_out, down_out, mine_out = refs[9:15]
    send = refs[15:]
    chip, _ = place()
    whole_columns(up_mine, up_pair, up_out)
    down_out[...] = pair_rows(down_own, down_pair)
    low = stack_rows(parts)
    low_out[...] = low
    u = dot(low, up_out[...]) + vec[pl.ds(13 + chip, 1), :]
    u_out[...] = u
    a_out[...] = (u * gelu_parts(u)).astype(BF)
    split_rows(dot(a_out[...], down_out[...]), mine_out, send)


def stack_kernel(r0, r1, r2, r3, out, spread_out):
    n = r0.shape[0]
    for k, part in enumerate((r0, r1, r2, r3)):
        out[k * n : (k + 1) * n, :] = part[...]
        for slot in range(SLOTS):
            spread_out[slot, k * n : (k + 1) * n, :] = part[...]


def logits_kernel(length, h0_ref, h1_ref, ids_ref, own_ref, e_ref, l_ref, pay_ref, h_ref, m_ref, s_ref, p_ref):
    i = pl.program_id(0)
    half = h0_ref.shape[0]

    @pl.when(i == 0)
    def _():
        h_ref[:half, :] = h0_ref[...]
        h_ref[half:, :] = h1_ref[...]
        m_ref[...] = jnp.full_like(m_ref, -3e38)
        s_ref[...] = jnp.zeros_like(s_ref)
        p_ref[...] = jnp.zeros_like(p_ref)

    x = dot(e_ref[...], h_ref[...], NT)
    l_ref[...] = x
    entry = lax.broadcasted_iota(jnp.int32, x.shape, 0) + i * x.shape[0]
    peak = jnp.maximum(m_ref[0:1, :], jnp.max(x, axis=0, keepdims=True))
    total = s_ref[0:1, :] * jnp.exp(m_ref[0:1, :] - peak) + jnp.sum(jnp.exp(x - peak), axis=0, keepdims=True)
    pick = p_ref[0:1, :] + jnp.sum(jnp.where(entry == ids_ref[...], x, 0.0), axis=0, keepdims=True)
    m_ref[0:1, :], s_ref[0:1, :], p_ref[0:1, :] = peak, total, pick

    @pl.when(i == pl.num_programs(0) - 1)
    def _():
        pay_ref[...] = jnp.zeros_like(pay_ref)
        pay_ref[pay_ref.shape[0] - 8 : pay_ref.shape[0] - 7, :] = own_ref[...]
        norm = peak + jnp.log(total)
        lane = lax.broadcasted_iota(jnp.int32, (1, 2 * length), 1)
        chip, core = place()
        for n in range(2 * half // (2 * length)):
            s = slice(n * 2 * length, (n + 1) * 2 * length)
            d, rest = divmod(2 * n * length, half)
            first = rest // length
            team, k = first // CHIPS, first % CHIPS
            rows = (
                jnp.where(lane < length, norm[:, s], pltpu.roll(pick[:, s], length, 1)),
                jnp.where(lane < length, pltpu.roll(norm[:, s], length, 1), pick[:, s]),
            )
            for j in range(2):
                q = team * TEAM + (chip ^ (k + j)) * CORES + (core ^ d)
                pay_ref[pl.ds(q, 1), :] = rows[j]


def logits(held, pair, ids, own_row, embedding, length, questions):
    half, vocab, width = held.shape[0], embedding.shape[0], embedding.shape[1]
    tile = min(2 * VOCAB_TILE, vocab)
    stat = pltpu.VMEM((8, 2 * half), F32)
    whole = pl.BlockSpec(memory_space=pltpu.VMEM)
    return pl.pallas_call(
        functools.partial(logits_kernel, length),
        grid=(vocab // tile,),
        in_specs=[whole, whole, whole, whole, pl.BlockSpec((tile, width), lambda i: (i, 0))],
        out_specs=[
            pl.BlockSpec((tile, 2 * half), lambda i: (i, 0)),
            pl.BlockSpec((questions + 8, 2 * length), lambda i: (0, 0)),
        ],
        out_shape=[
            pltpu.HBM((vocab, 2 * half), F32),
            jax.ShapeDtypeStruct((questions + 8, 2 * length), F32),
        ],
        scratch_shapes=[pltpu.VMEM((2 * half, width), BF), stat, stat, stat],
        compiler_params=limit(14 + 24 * half * tile // MIB),
        cost_estimate=work(10),
    )(held, pair, ids, own_row, embedding)


def merge_kernel(length, all_ref, counts_ref, ids_ref, rows_out, own_out, logp_out, prior_out, n_ref, g_ref):
    n_slot, n_pb = n_ref.shape[0], n_ref.shape[1]
    chip, core = place()
    me, slot = lax.axis_index("pb"), lax.axis_index("slot")
    lane = lax.broadcasted_iota(jnp.int32, (1, 2 * length), 1)
    logps, priors = [], None
    for s in range(n_slot):
        blocks = [all_ref[s * n_pb + j, :n_pb, :] for j in range(n_pb)]
        peak = blocks[0]
        for b in blocks[1:]:
            peak = jnp.maximum(peak, b)
        total = jnp.zeros_like(peak)
        pick = jnp.zeros_like(peak)
        for b in blocks:
            total = total + jnp.exp(b - peak)
            pick = pick + b
        norm = peak + jnp.log(total)
        n_ref[s] = norm
        own = jnp.concatenate([all_ref[s * n_pb + j, n_pb : n_pb + 1, :] for j in range(n_pb)], axis=0)
        mask = own
        prior = pltpu.roll(own, length, 1)
        logp = pltpu.roll(pick, length, 1) - norm + prior
        logps.append(jnp.where(counts_ref[...] > s, logp, -1e30))
    top = logps[0]
    for p in logps[1:]:
        top = jnp.maximum(top, p)
    total = jnp.zeros_like(top)
    for p in logps:
        total = total + jnp.exp(p - top)
    merged = top + jnp.log(total)
    for s in range(n_slot):
        g_ref[s] = jnp.where(counts_ref[...] > s, -mask * jnp.exp(logps[s] - merged), 0.0)
    n_rows = n_ref.shape[1]
    row = lax.broadcasted_iota(jnp.int32, merged.shape, 0)
    logp_out[...] = jnp.sum(jnp.where(row == me, merged, 0.0), axis=0, keepdims=True)
    own_grad = jnp.where(lane < length, g_ref[slot, pl.ds(me, 1), :], 0.0)
    prior_out[...] = jnp.sum(own_grad, axis=1, keepdims=True)
    rows_out[...] = jnp.zeros_like(rows_out)
    half = rows_out.shape[3]
    for s in range(n_slot):
        for d in range(CORES):
            for n in range(half // (2 * length)):
                team, c = (2 * n) // CHIPS, (2 * n) % CHIPS
                q = [team * TEAM + (chip ^ (c + j)) * CORES + (core ^ d) for j in range(2)]
                t = slice(n * 2 * length, (n + 1) * 2 * length)
                for r, (first, second) in enumerate(
                    (
                        (n_ref[s, pl.ds(q[0], 1), :], n_ref[s, pl.ds(q[1], 1), :]),
                        (g_ref[s, pl.ds(q[0], 1), :], g_ref[s, pl.ds(q[1], 1), :]),
                        (ids_ref[pl.ds(q[0], 1), :], ids_ref[pl.ds(q[1], 1), :]),
                    )
                ):
                    rows_out[s, d, r : r + 1, t] = jnp.where(lane < length, first, pltpu.roll(second, length, 1))
    own_out[0] = rows_out[slot]


def merge(everyone, counts, ids, length, n_slot, n_pb, half):
    held = pltpu.VMEM((n_slot, n_pb, 2 * length), F32)
    return pl.pallas_call(
        functools.partial(merge_kernel, length),
        out_shape=[
            jax.ShapeDtypeStruct((n_slot, CORES, 8, half), F32),
            jax.ShapeDtypeStruct((1, CORES, 8, half), F32),
            jax.ShapeDtypeStruct((1, 2 * length), F32),
            jax.ShapeDtypeStruct((1, 1), F32),
        ],
        scratch_shapes=[held, held],
        compiler_params=limit(16 + 2 * everyone.size * 4 // MIB),
        cost_estimate=work(2),
    )(everyone, counts, ids)


def logit_gradient(x, rows, first):
    entry = (lax.broadcasted_iota(jnp.int32, x.shape, 0) + first).astype(F32)
    hit = jnp.where(entry == rows[2:3, :], 1.0, 0.0)
    return (rows[1:2, :] * (hit - jnp.exp(x - rows[0:1, :]))).astype(BF)


def state_grad_kernel(l_ref, rows_ref, e_ref, own_ref, pair_ref, d_ref, acc_ref):
    i = pl.program_id(0)
    half = own_ref.shape[0]

    @pl.when(i == 0)
    def _():
        acc_ref[...] = jnp.zeros_like(acc_ref)

    tile = l_ref.shape[0]
    d = [logit_gradient(l_ref[:, c * half : (c + 1) * half], rows_ref[0, c], i * tile) for c in range(CORES)]
    d_ref[...] = jnp.concatenate(d, axis=1)
    acc_ref[...] += dot(d_ref[...], e_ref[...], TN)

    @pl.when(i == pl.num_programs(0) - 1)
    def _():
        own_ref[...] = acc_ref[:half, :].astype(own_ref.dtype)
        pair_ref[...] = acc_ref[half:, :].astype(BF)


def state_grad(scores, rows, embedding, own_type):
    vocab, count = scores.shape
    width = embedding.shape[1]
    half = count // CORES
    tile = min(2 * VOCAB_TILE, vocab)
    last = pl.BlockSpec((half, width), lambda i: (0, 0))
    return pl.pallas_call(
        state_grad_kernel,
        grid=(vocab // tile,),
        in_specs=[
            pl.BlockSpec((tile, count), lambda i: (i, 0)),
            pl.BlockSpec((1,) + rows.shape[1:], lambda i: (0, 0, 0, 0)),
            pl.BlockSpec((tile, width), lambda i: (i, 0)),
        ],
        out_specs=[last, last, pl.BlockSpec((tile, count), lambda i: (i, 0))],
        out_shape=[
            jax.ShapeDtypeStruct((half, width), own_type),
            jax.ShapeDtypeStruct((half, width), BF),
            pltpu.HBM((vocab, count), BF),
        ],
        scratch_shapes=[pltpu.VMEM((count, width), F32)],
        compiler_params=limit(16 + 20 * half * tile // MIB + count * width * 4 // MIB),
        cost_estimate=work(11),
    )(in_hbm(scores), rows, embedding)


def own_embedding_kernel(d_ref, own_ref, pair_ref, *refs):
    half = own_ref.shape[0]
    refs[-1][...] = dot(d_ref[:, :half], own_ref[...]) + dot(d_ref[:, half:], pair_ref[...])


def own_embedding(d, own, pair, held, piece, count):
    vocab, tokens = d.shape
    tile = min(VOCAB_TILE, vocab // count)
    steps = vocab // count // tile
    ahead = [] if held is None else [held]
    whole = pl.BlockSpec(memory_space=pltpu.VMEM)
    shape = (vocab, own.shape[1])
    return pl.pallas_call(
        own_embedding_kernel,
        grid=(steps,),
        in_specs=[pl.BlockSpec((tile, tokens), lambda i: (piece * steps + i, 0)), whole, whole]
        + [pl.BlockSpec(memory_space=pl.ANY)] * len(ahead),
        out_specs=pl.BlockSpec((tile, shape[1]), lambda i: (piece * steps + i, 0)),
        out_shape=pltpu.HBM(shape, F32),
        input_output_aliases={3: 0} if ahead else {},
        compiler_params=limit(14),
        cost_estimate=work(1),
    )(d, own, pair, *ahead)


def embedding_kernel(base, rows_ref, own_ref, pair_ref, e_ref, held_ref, o_ref):
    first = base + pl.program_id(0) * e_ref.shape[0]
    slot = lax.axis_index("slot")
    o_ref[...] = held_ref[...]

    def other(k, carry):
        n = slot ^ k
        for top in range(0, own_ref.shape[1], TOKENS // CORES):
            t = slice(top, top + TOKENS // CORES)
            h = jnp.concatenate([own_ref[n, t, :], pair_ref[n, t, :]], axis=0)
            rows = jnp.concatenate([rows_ref[n, 0, :, t], rows_ref[n, 1, :, t]], axis=1)
            o_ref[...] += dot(logit_gradient(dot(e_ref[...], h, NT), rows, first), h)
        return carry

    lax.fori_loop(1, own_ref.shape[0], other, 0)


def embedding_piece(rows, states, embedding, held, first, size):
    width = embedding.shape[1]
    tile = min(VOCAB_TILE, size)
    steps = size // tile
    whole = pl.BlockSpec(memory_space=pltpu.VMEM)
    block = pl.BlockSpec((tile, width), lambda i: (first // tile + i, 0))
    return pl.pallas_call(
        functools.partial(embedding_kernel, first),
        grid=(steps,),
        in_specs=[whole, whole, whole, block, block],
        out_specs=block,
        out_shape=pltpu.HBM(embedding.shape, F32),
        input_output_aliases={4: 0},
        compiler_params=limit(24),
        cost_estimate=work(3 * size / 1024),
    )(rows, *states, embedding, held)


def add_kernel(mine, got, own_out, *send):
    length = own_out.shape[0]
    for k in range(CHIPS):
        s = slice(k * length, (k + 1) * length)
        y = mine[s, :] + got[s, :].astype(F32)
        if k == 0:
            own_out[...] = y
        else:
            send[k - 1][...] = y.astype(BF)


def norm_back_kernel(row, has_base, *refs):
    base = refs[0] if has_base else None
    mine, r1, r2, r3, z, inv, vec, dr_out, e_out, sums_out = refs[1 if has_base else 0 :]
    dh = mine[...] + r1[...].astype(F32) + r2[...].astype(F32) + r3[...].astype(F32)
    if has_base:
        dh = dh + base[...]
    dr = norm_back(dh, z[...], inv[...], vec[6 + row : 7 + row, :])
    e = dr.astype(BF)
    dr_out[...] = dr
    e_out[...] = e
    sums_out[...] = jnp.zeros_like(sums_out)
    sums_out[0:1, :] = jnp.sum(dh * z[...], axis=0, keepdims=True)
    sums_out[1:2, :] = jnp.sum(dh, axis=0, keepdims=True)
    sums_out[2:3, :] = jnp.sum(e.astype(F32), axis=0, keepdims=True)


def stack_rows(parts):
    return jnp.concatenate([p[...] for p in parts], axis=0)


def split_rows(y, mine_out, send):
    length = mine_out.shape[0]
    mine_out[...] = y[:length]
    for k in range(1, CHIPS):
        send[k - 1][...] = y[k * length : (k + 1) * length].astype(BF)


def column_sum(y):
    return jnp.sum(y.astype(F32), axis=0, keepdims=True)


def ffn_back_kernel(*refs):
    parts, (u_ref, up, down), (e_out, du_out, sum_out, mine_out), send = refs[:4], refs[4:7], refs[7:11], refs[11:]
    e = stack_rows(parts)
    e_out[...] = e
    da = dot(e, down[...], NT).astype(BF).astype(F32)
    u = u_ref[...]
    slope = gelu_parts(u) + u * (jnp.exp(-0.5 * u * u) * 0.3989422804014327)
    du = (da * slope).astype(BF)
    du_out[...] = du
    sum_out[...] = column_sum(du)
    split_rows(dot(du, up[...], NT), mine_out, send)


def pick_core(g, mine_out, other_out, top):
    _, core = place()
    lo, hi = g[:, :, 0], g[:, :, 1]
    n = lo.shape[1] * lo.shape[2]
    mine = jnp.where(core == 0, lo, hi).reshape(CHIPS, n, g.shape[-1])
    other = jnp.where(core == 0, hi, lo).reshape(CHIPS, n, g.shape[-1])
    mine_out[:, top : top + n, :] = mine.astype(BF)
    other_out[:, top : top + n, :] = other.astype(BF)


def place_columns(g, mine_out, other_out, top):
    unit = g.shape[0] // (CHIPS * CHIPS * CORES)
    pick_core(g.reshape(CHIPS, CHIPS, CORES, unit, g.shape[1]), mine_out, other_out, top)


def place_rows(g, mine_out, other_out, top):
    unit = g.shape[0] // (CHIPS * CORES)
    pick_core(g.reshape(CHIPS, 1, CORES, unit, g.shape[1]), mine_out, other_out, top)


def place_row_blocks(g, mine_out, other_out, top, lanes):
    unit = g.shape[0] // (CHIPS * CORES)
    for b in range(g.shape[1] // lanes):
        place_rows(g[:, b * lanes : (b + 1) * lanes], mine_out, other_out, top + b * unit)


def ffn_grads_kernel(low, du, a, e, mine_out, other_out):
    g = dot(low[...], du[...], TN)
    place_columns(g, mine_out, other_out, 0)
    g2 = dot(a[...], e[...], TN)
    place_rows(g2, mine_out, other_out, g.shape[0] // (CHIPS * CORES))


def cross_back_kernel(*refs):
    parts, (w_mine, w_cols, q_ref, k_ref, v_ref) = refs[:4], refs[4:9]
    (e_out, dq_out, dk_out, dv_out, mine_out), send, g_ref = refs[9:14], refs[14:-1], refs[-1]
    quarter = q_ref.shape[1]
    length, memory = q_ref.shape[0] // CHIPS, k_ref.shape[0] // CHIPS
    e = stack_rows(parts)
    e_out[...] = e
    g = dot(e, w_mine[1], NT).astype(BF)
    g_ref[...] = g

    def pair(i, carry):
        for j in range(2):
            s, t = rows_at((2 * i + j) * length, length, 16), rows_at((2 * i + j) * memory, memory, 16)
            dq_out[s, :], dk_out[t, :], dv_out[t, :] = attend_back(
                g_ref[s, :], q_ref[s, :], k_ref[t, :], v_ref[t, :], False
            )
        return carry

    lax.fori_loop(0, CHIPS // 2, pair, 0)
    split_rows(dot(dq_out[...], w_cols[:, :quarter], NT), mine_out, send)


def cross_grads_kernel(low, dq, m, dk, dv, o, e, mine_out, other_out, sums_out):
    n = low.shape[1] // (CHIPS * CORES)
    for j, (a, g) in enumerate(((low, dq), (m, dk), (m, dv))):
        place_columns(dot(a[...], g[...], TN), mine_out, other_out, j * n)
    place_row_blocks(dot(o[...], e[...], TN), mine_out, other_out, 3 * n, dq.shape[1])
    sums_out[...] = jnp.zeros_like(sums_out)
    sums_out[0:1, :] = column_sum(dq[...])
    sums_out[1:2, :] = column_sum(dv[...])


def self_back_kernel(*refs):
    parts, (w_mine, q_ref, k_ref, v_ref), (e_out, d_out, g_ref) = refs[:4], refs[4:8], refs[8:]
    quarter = q_ref.shape[1]
    length = q_ref.shape[0] // CHIPS
    e = stack_rows(parts)
    e_out[...] = e
    g = dot(e, w_mine[0], NT).astype(BF)
    g_ref[...] = g

    def pair(i, carry):
        for j in range(2):
            s = rows_at((2 * i + j) * length, length, 16)
            dq, dk, dv = attend_back(g_ref[s, :], q_ref[s, :], k_ref[s, :], v_ref[s, :], True)
            d_out[s, :quarter] = dq
            d_out[s, quarter : 2 * quarter] = dk
            d_out[s, 2 * quarter :] = dv
        return carry

    lax.fori_loop(0, CHIPS // 2, pair, 0)


SMALL = 16


def self_grads_kernel(x, d, o, e, c_sums, sum_in, one, two, three, mine_out, other_out):
    chip, core = place()
    quarter = d.shape[1] // 3
    n = x.shape[1] // (CHIPS * CORES)
    g = dot(x[...], d[...], TN)
    for j in range(3):
        place_columns(g[:, j * quarter : (j + 1) * quarter], mine_out, other_out, j * n)
    place_row_blocks(dot(o[...], e[...], TN), mine_out, other_out, 3 * n, quarter)

    def spread(row):
        zero = jnp.zeros_like(row)
        return jnp.concatenate([jnp.where(chip == b, row, zero) for b in range(CHIPS)], axis=1)

    rows = [
        spread(column_sum(d[:, :quarter])), spread(column_sum(d[:, 2 * quarter :])), one[2:3, :],
        spread(c_sums[0:1, :]), spread(c_sums[1:2, :]), two[2:3, :], one[0:1, :], two[0:1, :], three[0:1, :],
        one[1:2, :], two[1:2, :], three[1:2, :], three[2:3, :],
    ]
    v = jnp.concatenate(rows + [jnp.zeros((SMALL - len(rows), x.shape[1]), F32)], axis=0)
    unit = x.shape[1] // (CHIPS * CHIPS * CORES)
    wide = sum_in.shape[1] // (CHIPS * CORES)
    last = sum_in[...]
    top = 4 * n
    for out in (mine_out, other_out):
        out[:, top:, :] = jnp.zeros((CHIPS, 2 * SMALL, quarter), BF)
    for s in range(CHIPS):
        halves, ends = [], []
        for c in range(CORES):
            parts = [v[:, ((s * CHIPS + b) * CORES + c) * unit :][:, :unit] for b in range(CHIPS)]
            halves.append(jnp.concatenate(parts, axis=1))
            ends.append(last[:, (s * CORES + c) * wide :][:, :wide])
        for out, swap in ((mine_out, False), (other_out, True)):
            first = (core == 0) != swap
            out[s, top : top + SMALL, : CHIPS * unit] = jnp.where(first, halves[0], halves[1]).astype(BF)
            out[s, top + SMALL : top + SMALL + 1, :wide] = jnp.where(first, ends[0], ends[1]).astype(BF)


def input_back_kernel(d, w_self, dk, dv, w_cross, f_got, mine_out, rest_out, *send):
    chip, _ = place()
    quarter = dk.shape[1]
    length, memory = d.shape[0] // CHIPS, dk.shape[0] // CHIPS
    y = dot(d[...], w_self[...], NT)
    m = dot(dk[...], w_cross[:, quarter : 2 * quarter], NT) + dot(dv[...], w_cross[:, 2 * quarter :], NT)
    f = sum(f_got[n].astype(F32) for n in range(SLOTS)).astype(BF)
    both = length + memory
    unit = (send[0].shape[0] - both)
    rest_out[...] = f[CHIPS * unit :]
    mine_out[:length, :] = y[:length]
    mine_out[length:, :] = m[:memory]
    for k, out in enumerate(send):
        if k:
            out[:length, :] = y[k * length : (k + 1) * length].astype(BF)
            out[length:both, :] = m[k * memory : (k + 1) * memory].astype(BF)
        block = jnp.zeros((unit, f.shape[1]), BF)
        for b in range(CHIPS):
            block = jnp.where((chip ^ k) == b, f[b * unit : (b + 1) * unit], block)
        out[both:, :] = block


def input_total_kernel(base, mine, own, r1, r2, r3, source_out, memory_out, up_out):
    chip, _ = place()
    length = base.shape[0]
    both = mine.shape[0]
    width = base.shape[1]
    y = mine[...]
    for k, r in enumerate((own, r1, r2, r3)):
        if k:
            y = y + r[:both, :].astype(F32)
        up_out[:, rows_at((chip ^ k) * width, width, 128)] = r[both:, :].astype(F32)
    source_out[...] = base[...] + y[:length]
    memory_out[...] = y[length:]


def core_sum_kernel(mine, got, out):
    for n in range(SLOTS):
        out[n] = (mine[n].astype(F32) + got[n].astype(F32)).astype(BF)


def attn_pieces_kernel(s_got, c_got, *outs):
    *pieces, rest = outs
    chip, _ = place()
    s = sum(s_got[n].astype(F32) for n in range(SLOTS)).astype(BF)
    c = sum(c_got[n].astype(F32) for n in range(SLOTS)).astype(BF)
    top = 3 * c.shape[0] // 4
    unit = top // (3 * CHIPS)
    both = [y[:top].reshape(3, CHIPS, unit, y.shape[1]) for y in (s, c)]
    for k in range(CHIPS):
        for m, y in enumerate(both):
            for j in range(3):
                block = jnp.zeros((unit, y.shape[3]), BF)
                for b in range(CHIPS):
                    block = jnp.where((chip ^ k) == b, y[j, b], block)
                pieces[k][(3 * m + j) * unit : (3 * m + j + 1) * unit, :] = block
        pieces[k][6 * unit :, :] = s[c.shape[0] : c.shape[0] + SMALL]
    n = c.shape[0] - top
    rest[:n, :] = s[top : top + n]
    rest[n : 2 * n, :] = c[top:]
    rest[2 * n :, :] = s[c.shape[0] + SMALL :]


def attn_out_kernel(p0, p1, p2, p3, out, bias_out, gain_out, shift_out, last_out):
    chip, _ = place()
    unit, quarter = out.shape[1], p0.shape[1]
    parts = (p0, p1, p2, p3)
    for k, p in enumerate(parts):
        lanes = rows_at((chip ^ k) * quarter, quarter, 128)
        for j in range(6):
            out[j, :, lanes] = p[j * unit : (j + 1) * unit, :].astype(F32)
    total = sum(p[6 * unit :, : CHIPS * unit].astype(F32) for p in parts)
    mine = jnp.zeros((SMALL, unit), F32)
    for b in range(CHIPS):
        mine = jnp.where(chip == b, total[:, b * unit : (b + 1) * unit], mine)
    bias_out[...] = mine[0:6]
    gain_out[...] = mine[6:9]
    shift_out[...] = mine[9:12]
    last_out[...] = mine[12:13]


def rows_out_kernel(owned, f_owned, out, down_out, in_out):
    unit, quarter = out.shape[1], owned.shape[1]
    n = CHIPS * unit
    for m in range(2):
        for b in range(CHIPS):
            out[m, :, b * quarter : (b + 1) * quarter] = owned[m * n + b * unit : m * n + (b + 1) * unit, :].astype(F32)
    down_out[...] = f_owned[...].astype(F32)
    in_out[...] = owned[2 * n : 2 * n + 1, : in_out.shape[1]].astype(F32)


def shards(
    inputs, memory, attn_weight, attn_out, ffn_in, ffn_out, attn_bias, norm_gain, norm_bias,
    bias_in, bias_out, embedding, targets, slot_counts, pad_mask, log_prior,
):
    n_pb, n_slot = lax.axis_size("pb"), lax.axis_size("slot")
    n_all = n_pb * n_slot
    teams = n_pb // TEAM
    me = lax.axis_index("pb")
    length, width = inputs.shape[2], inputs.shape[3]
    passage = memory.shape[2]
    quarter = width // CHIPS
    unit = width // (TEAM * n_slot)
    vocab_rows = embedding.shape[0]
    embedding = in_hbm(embedding)

    def team_rows(w):
        if teams == 1:
            return w
        w = lax.all_gather(w, "pb", axis=0, tiled=True)
        n = w.shape[0] // TEAM
        return lax.dynamic_slice_in_dim(w, (me % TEAM) * n, n)

    x, m = inputs[0, 0], memory[0, 0]
    attn_w = jnp.moveaxis(team_rows(attn_weight), 1, 0)
    out_w = jnp.moveaxis(team_rows(attn_out), 1, 0)
    up_w = team_rows(ffn_in)
    down_w = team_rows(ffn_out)
    rows = attn_w.shape[1]
    ff = up_w.shape[1] // CHIPS
    vec = jnp.concatenate(
        [attn_bias.T, norm_gain.T, norm_bias.T, bias_out[None], bias_in.reshape(CHIPS, -1)], axis=0
    )
    ids = (targets - me * vocab_rows).astype(jnp.int32)
    own_row = jnp.concatenate([pad_mask.astype(F32), jnp.broadcast_to(log_prior, (1, length))], axis=1)

    block = (length, width)
    every = (CHIPS * length, width)
    cols = (CHIPS * length, quarter)
    m_cols = (CHIPS * passage, quarter)
    sends = [(block, BF)] * 3

    def give(send):
        return [from_chip(send[k - 1], k) for k in range(1, CHIPS)]

    def give_far(send):
        return [in_hbm(r) for r in give(send)]

    far_call = functools.partial(call, far=True)

    first = call(functools.partial(pack_kernel, 6, 0), [((CHIPS * length + 6 * rows, quarter), BF)] * CHIPS, x, attn_w)
    got_first = [first[0]] + give(first[1:])
    got_first[1], vec = tie(got_first[1], vec)
    pair_first = [from_core(g) for g in got_first]
    out_pair = from_core(out_w)
    down_pair = from_core(down_w)
    third = list(call(functools.partial(pack_kernel, 1, 0), [((rows, ff), BF)] * CHIPS, up_w[None]))
    m_send, pair_first[3] = tie(m, pair_first[3])
    got_memory = [m, from_chip(m_send, 1), from_chip(m_send, 2)]

    x_all, w_self, queries, keys, values, mixed, w_out, mine, *send = call(
        self_kernel,
        [(every, BF), ((width, 3 * quarter), BF)] + [(cols, BF)] * 4 + [((2, quarter, width), BF), (block, F32)]
        + sends,
        *got_first, *pair_first, out_w, out_pair, vec,
    )
    got = give(send)
    got_memory[1], got_memory[2], *got = tie(got_memory[1], got_memory[2], *got)
    norm_outs = [(block, F32), (block, BF), (block, F32), ((length, 1), F32)]
    hidden_one, low_one, z_one, inv_one = call(
        functools.partial(norm_kernel, (2, 6, 9)), norm_outs, x, mine, *got, vec, us=1
    )
    got_low = [low_one] + others(low_one)
    m_send, got_memory[1] = tie(m, got_memory[1])
    got_memory.append(from_chip(m_send, 3))
    m_all, w_cross, cross_keys, cross_values = call(
        memory_kernel, [((CHIPS * passage, width), BF), ((width, 3 * quarter), BF)] + [(m_cols, BF)] * 2,
        *got_memory, *got_first, *pair_first, vec,
    )
    third[1], third[2], *got_low = tie(third[1], third[2], *got_low)
    got_third = [third[0], from_chip(third[1], 1), from_chip(third[2], 2)]
    low_one_all, cross_queries, cross_mixed, mine, *send = call(
        cross_kernel, [(every, BF), (cols, BF), (cols, BF), (block, F32)] + sends,
        *got_low, w_out, w_cross, cross_keys, cross_values, vec,
    )
    got = give(send)
    got_third[1], got_third[2], *got = tie(got_third[1], got_third[2], *got)
    hidden_two, low_two, z_two, inv_two = call(
        functools.partial(norm_kernel, (5, 7, 10)), norm_outs, hidden_one, mine, *got, vec, us=1
    )
    got_low = [low_two] + others(low_two)
    third[3], got_third[1] = tie(third[3], got_third[1])
    got_third.append(from_chip(third[3], 3))
    got_third[3], *got_low = tie(got_third[3], *got_low)
    (up_half,) = call(up_half_kernel, [((CHIPS, rows, ff), BF)], *got_third)
    up_half_pair = from_core(up_half)
    low_two_all, upward, active, w_up, w_down, mine, *send = call(
        ffn_kernel,
        [(every, BF), ((CHIPS * length, ff), F32), ((CHIPS * length, ff), BF), ((width, ff), BF)]
        + [((ff, width), BF), (block, F32)]
        + sends,
        *got_low, up_half, up_half_pair, down_w, down_pair, vec,
    )
    got = give(send)
    _, final_low, z_three, inv_three = call(
        functools.partial(norm_kernel, (12, 8, 11)), norm_outs, hidden_two, mine, *got, vec, us=1
    )

    held, spread_held = call(
        stack_kernel, [(every, BF), ((n_slot,) + every, BF)], final_low, *others(final_low), us=1, far=(1,) if teams == 1 else ()
    )
    pair = from_core(held)

    def all_teams(h):
        return lax.all_gather(h, "pb", axis_index_groups=same_place_groups(), axis=0, tiled=True) if teams > 1 else h

    half = teams * CHIPS * length
    chip, core = place()
    order = [
        t * TEAM + (chip ^ k) * CORES + (core ^ d) for d in range(CORES) for t in range(teams) for k in range(CHIPS)
    ]
    ids_row = jnp.concatenate([lax.dynamic_slice_in_dim(ids, q, 1) for q in order], axis=1)
    states = [all_teams(held), all_teams(pair)]
    scores, payload = logits(*states, ids_row, own_row, embedding, length, n_pb)
    everyone = lax.all_to_all(
        jnp.broadcast_to(payload[None], (n_all,) + payload.shape), ("slot", "pb"), 0, 0, tiled=True
    )
    ids_wide = jnp.pad(ids.astype(F32), ((0, 0), (0, length)))
    spread_held, everyone = tie(spread_held, everyone)
    all_held = across_slots(spread_held)
    token_rows, own_rows, token_logprob, prior_grad = merge(
        everyone, slot_counts.astype(jnp.int32)[:, None], ids_wide, length, n_slot, n_pb, half
    )
    def home(partial):
        if teams == 1:
            return partial
        return lax.psum_scatter(partial, "pb", axis_index_groups=same_place_groups(), scatter_dimension=0, tiled=True)

    own_part, for_pair, own_logits = state_grad(scores, own_rows, embedding, F32)
    own_logits = in_hbm(own_logits)
    own_part, got_pair = home(own_part), from_core(home(for_pair))
    mine, *send = call(add_kernel, [(block, F32)] + sends, own_part, got_pair, us=1)
    got = give(send)
    own_logits, send[0] = tie(own_logits, send[0])
    own_terms = own_embedding(own_logits, *states, None, 0, 2)
    own_terms, *got = tie(own_terms, *got)

    eighth = vocab_rows // 8
    parts = (1, 1, 1, 5)
    made = []

    def piece(*wait):
        n = len(made) - 1
        rows_in, *wait = tie(token_rows, *wait)
        first = sum(parts[:n]) * eighth
        made.append(embedding_piece(rows_in, states, embedding, made[-1], first, parts[n] * eighth))
        return wait

    def pieces(count, *wait):
        for _ in range(count):
            wait = piece(*wait)
        return list(wait)

    def then(*values):
        *values, made[-1] = tie(*values, made[-1])
        return values

    def settle(g):
        if teams == 1:
            return g
        g = lax.psum(g, "pb", axis_index_groups=same_place_groups())
        g = lax.all_gather(g, "pb", axis_index_groups=team_groups(), axis=0, tiled=True)
        n = g.shape[0] // n_pb
        return lax.dynamic_slice_in_dim(g, me * n, n)

    def to_owner(g):
        pairs = []
        for s in range(n_slot):
            for i in range(n_pb):
                t, b, c = i // TEAM, (i % TEAM) // CORES, i % CORES
                pairs.append((s * n_pb + i, b * n_pb + t * TEAM + s * CORES + c))
        return lax.ppermute(g, ("slot", "pb"), pairs)

    x_all, w_self, queries, keys, values, mixed, w_out, m_all, w_cross, cross_keys, cross_values = (
        in_hbm(v)
        for v in (x_all, w_self, queries, keys, values, mixed, w_out, m_all, w_cross, cross_keys, cross_values)
    )
    low_one_all, cross_queries, cross_mixed, low_two_all, upward, active, w_up, w_down = (
        in_hbm(v) for v in (low_one_all, cross_queries, cross_mixed, low_two_all, upward, active, w_up, w_down)
    )
    z_one, z_two, z_three = in_hbm(z_one), in_hbm(z_two), in_hbm(z_three)
    grads = [(block, F32), (block, BF), ((8, width), F32)]
    dr_three, e_three, sums_three = call(
        functools.partial(norm_back_kernel, 2, False), grads, mine, *got, z_three, inv_three, vec, us=1
    )
    got_e = others(e_three)
    own_logits, e_three = tie(own_logits, e_three)
    own_terms = own_embedding(own_logits, *states, own_terms, 1, 2)
    own_terms, *got_e = tie(own_terms, *got_e)
    made.append(own_terms)
    e_all, du, sum_in, mine, *send = call(
        ffn_back_kernel,
        [(every, BF), ((CHIPS * length, ff), BF), ((1, ff), F32), (block, F32)] + sends,
        e_three, *got_e, upward, w_up, w_down,
    )
    got = give(send)
    f_shape = (n_slot, CHIPS * unit + ff // TEAM, width)
    du, send[0] = tie(du, send[0])
    f_mine, f_other = far_call(ffn_grads_kernel, [(f_shape, BF)] * 2, low_two_all, du, active, e_all, us=3)
    f_other, all_held, *got = tie(f_other, all_held, *got)
    all_pair = from_core(all_held)
    dr_two, e_two, sums_two = far_call(
        functools.partial(norm_back_kernel, 1, True), grads, dr_three, mine, *got, z_two, inv_two, vec, us=1
    )
    got_e = give_far([e_two] * 3)
    f_got = from_core(f_other)
    f_got, all_pair, got_e[2] = tie(f_got, all_pair, got_e[2])
    states = [jnp.stack([all_teams(h[n]) for n in range(n_slot)]) if teams > 1 else h for h in (all_held, all_pair)]
    (f_total,) = far_call(core_sum_kernel, [(f_shape, BF)], f_mine, f_got)
    f_got = across_slots(f_total)
    e_all_two, dqc, dkc, dvc, mine, *send = far_call(
        cross_back_kernel,
        [(every, BF), (cols, BF), (m_cols, BF), (m_cols, BF), (block, F32)] + sends,
        e_two, *got_e, w_out, w_cross, cross_queries, cross_keys, cross_values, us=5,
        scratch=[pltpu.VMEM(cols, BF)],
    )
    got = give(send)
    dqc, send[0] = tie(dqc, send[0])
    g_shape = (n_slot, 4 * CHIPS * unit, quarter)
    c_mine, c_other, c_sums = call(
        cross_grads_kernel, [(g_shape, BF)] * 2 + [((8, quarter), F32)],
        low_one_all, dqc, m_all, dkc, dvc, cross_mixed, e_all_two,
    )
    c_got = from_core(c_other)
    (c_mine,) = piece(c_mine)
    got = then(*got)
    dr_one, e_one, sums_one = far_call(
        functools.partial(norm_back_kernel, 0, True), grads, dr_two, mine, *got, z_one, inv_one, vec, us=1
    )
    got_e = give([e_one] * 3)
    c_got, e_one = tie(c_got, e_one)
    (c_total,) = far_call(core_sum_kernel, [(g_shape, BF)], c_mine, c_got)
    (c_total,) = piece(c_total)
    got_e = then(*got_e)
    e_all_one, d_self = far_call(
        self_back_kernel, [(every, BF), ((CHIPS * length, 3 * quarter), BF)], e_one, *got_e, w_out, queries, keys, values, us=4,
        scratch=[pltpu.VMEM(cols, BF)],
    )
    c_total, d_self, f_got = tie(c_total, d_self, f_got)
    c_got = across_slots(c_total)
    s_shape = (n_slot, g_shape[1] + 2 * SMALL, quarter)
    s_mine, s_other = far_call(
        self_grads_kernel, [(s_shape, BF)] * 2, x_all, d_self, mixed, e_all_one, c_sums, sum_in, sums_one, sums_two, sums_three
    )
    s_got = from_core(s_other)
    f_got, s_mine = tie(f_got, s_mine)
    both = (length + passage, width)
    f_rest = (f_shape[1] - CHIPS * unit, width)
    mine, f_rest, *send = far_call(
        input_back_kernel, [(both, F32), (f_rest, BF)] + [((both[0] + unit, width), BF)] * CHIPS,
        d_self, w_self, dkc, dvc, w_cross, f_got, us=3,
    )
    f_owned = to_owner(f_rest)
    s_got, send[0] = tie(s_got, send[0])
    (s_total,) = far_call(core_sum_kernel, [(s_shape, BF)], s_mine, s_got)
    (s_total,) = pieces(1, s_total)
    (c_got,) = then(c_got)
    s_total, send[0], c_got = tie(s_total, send[0], c_got)
    s_got = across_slots(s_total)
    got = give(send[1:])
    (send[0],) = pieces(len(parts) + 1 - len(made), send[0])
    s_got, *got = then(s_got, *got)
    *piece_parts, rest = call(
        attn_pieces_kernel,
        [((6 * unit + SMALL, quarter), BF)] * CHIPS + [((2 * CHIPS * unit + SMALL, quarter), BF)],
        s_got, c_got,
    )
    last = give(piece_parts[1:])
    owned = to_owner(rest)
    grad_source, grad_passage, out_up = call(
        input_total_kernel, [(block, F32), ((passage, width), F32), ((unit, up_w.shape[1]), F32)],
        dr_one, mine, send[0], *got, us=1,
    )
    owned, grad_source, *last = tie(owned, grad_source, *last)
    out_attn, *vectors = call(
        attn_out_kernel,
        [((6, unit, width), F32), ((6, unit), F32), ((3, unit), F32), ((3, unit), F32), ((1, unit), F32)],
        piece_parts[0], *last, us=1,
    )
    outs, out_down, sum_in_out = call(
        rows_out_kernel, [((2, unit, width), F32), (f_rest.shape, F32), ((1, ff // TEAM), F32)], owned, f_owned, us=1
    )
    out_attn = settle(jnp.moveaxis(out_attn, 0, 1))
    out_outputs = settle(jnp.moveaxis(outs, 0, 1))
    out_up, out_down = settle(out_up), settle(out_down)
    vectors = [settle(v) for v in (vectors[0].T, vectors[1].T, vectors[2].T, sum_in_out[0], vectors[3][0])]
    return (
        token_logprob[:, :length],
        grad_source[None, None],
        grad_passage[None, None],
        prior_grad,
        out_attn,
        out_outputs,
        out_up,
        out_down,
        vectors[0],
        vectors[1],
        vectors[2],
        vectors[3],
        vectors[4],
        made[-1],
    )


def solution(mesh):
    placed = (
        P("pb", "slot", None, None),
        P("pb", "slot", None, None),
        P("pb", None, None),
        P("pb", None, None),
        P("pb", None),
        P("pb", None),
        P(),
        P(),
        P(),
        P(),
        P(),
        P("pb", None),
        P(),
        P(),
        P("pb", None),
        P("pb", "slot"),
    )
    both = ("slot", "pb")
    return jax.shard_map(
        shards,
        mesh=mesh,
        in_specs=placed,
        out_specs=(
            P("pb", None),
            P("pb", "slot", None, None),
            P("pb", "slot", None, None),
            P("pb", "slot"),
            P(both, None, None),
            P(both, None, None),
            P(both, None),
            P(both, None),
            P(both, None),
            P(both, None),
            P(both, None),
            P(both),
            P(both),
            P("pb", None),
        ),
        check_vma=False,
    )
```

```python
import functools

import jax
import jax.numpy as jnp
from jax import lax
from jax.experimental import pallas as pl
from jax.experimental.pallas import tpu as pltpu
from jax.sharding import PartitionSpec as P

HEAD = 64
CHIPS = 4
CORES = 2
TEAM = CHIPS * CORES
SLOTS = 4
BF = jnp.bfloat16
F32 = jnp.float32
TOKENS = 512
VOCAB_TILE = 512


def from_chip(x, k):
    pairs = []
    for i in range(lax.axis_size("pb")):
        place = i % TEAM
        pairs.append((i, i - place + ((place // CORES) ^ k) * CORES + place % CORES))
    return lax.ppermute(x, "pb", pairs)


def from_core(x):
    return lax.ppermute(x, "pb", [(i, i ^ 1) for i in range(lax.axis_size("pb"))])


def across_slot(x, k):
    return lax.ppermute(x, "slot", [(i, i ^ k) for i in range(lax.axis_size("slot"))])


def same_place_groups():
    size = lax.axis_size("pb")
    return [[g * TEAM + j for g in range(size // TEAM)] for j in range(TEAM)]


def team_groups():
    size = lax.axis_size("pb")
    return [[g * TEAM + j for j in range(TEAM)] for g in range(size // TEAM)]


def others(x):
    return [from_chip(x, k) for k in range(1, CHIPS)]


def tie(*values):
    return list(lax.optimization_barrier(values))


def across_slots(x):
    return lax.all_to_all(x, "slot", 0, 0, tiled=True)


def at(x, index):
    return lax.dynamic_index_in_dim(x, index, 0, False)


NN = (((1,), (0,)), ((), ()))
NT = (((1,), (1,)), ((), ()))
TN = (((0,), (0,)), ((), ()))


def dot(a, b, dims=NN):
    return lax.dot_general(a, b, dims, preferred_element_type=F32)


def place():
    j = lax.axis_index("pb") % TEAM
    return j // CORES, j % CORES


def rows_at(start, size, unit):
    return pl.ds(pl.multiple_of(start, unit), size)


MIB = 2**20


def limit(mib):
    return pltpu.CompilerParams(vmem_limit_bytes=min(60, mib) * MIB)


def work(us):
    return pl.CostEstimate(flops=int(us * 1e9), bytes_accessed=0, transcendentals=0)


def call(kernel, outs, *args, us=2.0, far=(), scratch=()):
    shapes = [jax.ShapeDtypeStruct(*o) for o in outs]
    held = sum(a.size * a.dtype.itemsize for a in (*args, *shapes))
    params = limit(8 + held * 5 // 4 // MIB)
    far = range(len(outs)) if far is True else far
    places = [pltpu.HBM(*o) if n in far else s for n, (o, s) in enumerate(zip(outs, shapes))]
    results = pl.pallas_call(
        kernel, out_shape=places, scratch_shapes=scratch, compiler_params=params, cost_estimate=work(us)
    )(*args)
    return [in_hbm(r) if n in far else r for n, r in enumerate(results)]


def in_hbm(x):
    return pltpu.with_memory_space_constraint(x, pltpu.HBM)


def norm_rows(r, gain, shift):
    centered = r - jnp.mean(r, axis=-1, keepdims=True)
    inv = lax.rsqrt(jnp.mean(centered * centered, axis=-1, keepdims=True) + 1e-05)
    z = centered * inv
    return z * gain + shift, z, inv


def norm_back(dh, z, inv, gain):
    dz = dh * gain
    return (dz - jnp.mean(dz, axis=-1, keepdims=True) - z * jnp.mean(dz * z, axis=-1, keepdims=True)) * inv


def lane_head(shape, keys):
    return lax.broadcasted_iota(jnp.int32, shape, 1) // keys


def per_head(x):
    head = lane_head(x.shape, HEAD)
    return jnp.concatenate([jnp.where(head == h, x, jnp.zeros_like(x)) for h in range(x.shape[1] // HEAD)], axis=0)


def own_heads(big, keys):
    count = big.shape[1] // HEAD
    head = lane_head((keys, big.shape[1]), HEAD)
    total = jnp.zeros((keys, big.shape[1]), F32)
    for h in range(count):
        total = total + jnp.where(head == h, big[h * keys : (h + 1) * keys], 0.0)
    return total


def head_probs(q, kbig, keys, causal):
    s = dot(q, kbig, NT) * 0.125
    head = lane_head(s.shape, keys)
    count = s.shape[1] // keys
    if causal:
        query = lax.broadcasted_iota(jnp.int32, s.shape, 0)
        key = lax.broadcasted_iota(jnp.int32, s.shape, 1) % keys
        s = jnp.where(query >= key, s, -1e30)
    peak = jnp.zeros_like(s)
    for h in range(count):
        m = jnp.max(jnp.where(head == h, s, -3e38), axis=1, keepdims=True)
        peak = jnp.where(head == h, m, peak)
    e = jnp.exp(s - peak)
    return e / head_sums(e, head, count)


def head_sums(x, head, count):
    total = jnp.zeros_like(x)
    for h in range(count):
        total = jnp.where(head == h, jnp.sum(jnp.where(head == h, x, 0.0), axis=1, keepdims=True), total)
    return total


def attend(q, k, v, causal):
    probs = head_probs(q, per_head(k), k.shape[0], causal)
    return dot(probs.astype(BF), per_head(v)).astype(BF)


def attend_back(g, q, k, v, causal):
    keys = k.shape[0]
    kbig, vbig = per_head(k), per_head(v)
    probs = head_probs(q, kbig, keys, causal)
    dp = dot(g, vbig, NT)
    head = lane_head(dp.shape, keys)
    ds = (probs * (dp - head_sums(dp * probs, head, dp.shape[1] // keys))).astype(BF)
    dq = dot(ds, kbig) * 0.125
    dk = own_heads(dot(ds, q, TN), keys) * 0.125
    dv = own_heads(dot(probs.astype(BF), g, TN), keys)
    return dq.astype(BF), dk.astype(BF), dv.astype(BF)


def pack_kernel(count, first, *refs):
    *rows_in, w_ref, o0, o1, o2, o3 = refs
    outs = (o0, o1, o2, o3)
    chip, _ = place()
    rows, quarter = w_ref.shape[1], w_ref.shape[2] // CHIPS
    for k in range(CHIPS):
        top = 0
        for x_ref in rows_in:
            x = x_ref[...]
            for b in range(CHIPS):
                outs[k][top : top + x.shape[0], :] = x[:, b * quarter : (b + 1) * quarter]
                top += x.shape[0]
        for j in range(count):
            outs[k][top : top + rows, :] = w_ref[first + j, :, rows_at((chip ^ k) * quarter, quarter, 128)]
            top += rows


def natural_columns(own, pair, w_out, top, count):
    chip, core = place()
    rows = w_out.shape[0] // TEAM
    quarter = own[0].shape[1]
    for k in range(CHIPS):
        for refs, c in ((own, core), (pair, 1 - core)):
            start = (chip ^ k) * (CORES * rows) + c * rows
            for j in range(count):
                w_out[rows_at(start, rows, 16), j * quarter : (j + 1) * quarter] = refs[k][
                    top + j * rows : top + (j + 1) * rows, :
                ]


def half_columns(parts, out, top, count):
    chip, _ = place()
    rows = (parts[0].shape[0] - top) // count
    quarter = parts[0].shape[1]
    for k in range(CHIPS):
        for j in range(count):
            out[chip ^ k, :, j * quarter : (j + 1) * quarter] = parts[k][top + j * rows : top + (j + 1) * rows, :]


def whole_columns(mine, pair, out):
    _, core = place()
    rows = mine.shape[1]
    for b in range(CHIPS):
        for part, c in ((mine, core), (pair, 1 - core)):
            out[rows_at(b * CORES * rows + c * rows, rows, 16), :] = part[b]


def pair_rows(own, pair):
    _, core = place()
    a, b = own[...], pair[...]
    return jnp.concatenate([jnp.where(core == 0, a, b), jnp.where(core == 0, b, a)], axis=0)


def self_kernel(*refs):
    own, pair, (o_own, o_pair, vec) = refs[:4], refs[4:8], refs[8:11]
    x_out, w_out, q_out, k_out, v_out, o_out, wo_out, mine_out = refs[11:19]
    send = refs[19:]
    chip, _ = place()
    quarter = own[0].shape[1]
    length = x_out.shape[0] // CHIPS
    natural_columns(own, pair, w_out, CHIPS * length, 3)
    for k in range(CHIPS):
        for b in range(CHIPS):
            x_out[k * length : (k + 1) * length, b * quarter : (b + 1) * quarter] = own[k][b * length : (b + 1) * length, :]
    for j in range(2):
        wo_out[j] = pair_rows(o_own.at[j], o_pair.at[j])
    lanes = rows_at(chip * quarter, quarter, 128)
    y = dot(x_out[...], w_out[...])
    q = (y[:, :quarter] + vec[0:1, lanes]).astype(BF)
    k = y[:, quarter : 2 * quarter].astype(BF)
    v = (y[:, 2 * quarter :] + vec[1:2, lanes]).astype(BF)
    q_out[...], k_out[...], v_out[...] = q, k, v

    def pair(i, carry):
        for j in range(2):
            s = rows_at((2 * i + j) * length, length, 16)
            o_out[s, :] = attend(q_out[s, :], k_out[s, :], v_out[s, :], True)
        return carry

    lax.fori_loop(0, CHIPS // 2, pair, 0)
    split_rows(dot(o_out[...], wo_out[0]), mine_out, send)


def half_kernel(*refs):
    half_columns(refs[:4], refs[4], 0, 3)


def memory_kernel(*refs):
    mem, own, pair, vec, (m_out, w_out, k_out, v_out) = refs[:4], refs[4:8], refs[8:12], refs[12], refs[13:]
    chip, _ = place()
    quarter = k_out.shape[1]
    natural_columns(own, pair, w_out, own[0].shape[0] - 3 * w_out.shape[0] // TEAM, 3)
    m_out[...] = stack_rows(mem)
    y = dot(m_out[...], w_out[:, quarter:])
    k_out[...] = y[:, :quarter].astype(BF)
    v_out[...] = (y[:, quarter:] + vec[4:5, rows_at(chip * quarter, quarter, 128)]).astype(BF)


def norm_kernel(rows, *refs):
    base, mine, r1, r2, r3, vec, h_out, low_out, z_out, inv_out = refs
    y = mine[...] + r1[...].astype(F32) + r2[...].astype(F32) + r3[...].astype(F32)
    r = base[...].astype(F32) + y + vec[rows[0] : rows[0] + 1, :]
    h, z, inv = norm_rows(r, vec[rows[1] : rows[1] + 1, :], vec[rows[2] : rows[2] + 1, :])
    h_out[...] = h
    low_out[...] = h.astype(BF)
    z_out[...] = z
    inv_out[...] = inv


def cross_kernel(*refs):
    parts, (wo, w_cols, keys, values, vec), (low_out, q_out, o_out, mine_out), send = refs[:4], refs[4:9], refs[9:13], refs[13:]
    chip, _ = place()
    quarter = keys.shape[1]
    length = parts[0].shape[0]
    memory = keys.shape[0] // CHIPS
    low = stack_rows(parts)
    low_out[...] = low
    q = (dot(low, w_cols[:, :quarter]) + vec[3:4, rows_at(chip * quarter, quarter, 128)]).astype(BF)
    q_out[...] = q

    def pair(i, carry):
        for j in range(2):
            s, t = rows_at((2 * i + j) * length, length, 16), rows_at((2 * i + j) * memory, memory, 16)
            o_out[s, :] = attend(q_out[s, :], keys[t, :], values[t, :], False)
        return carry

    lax.fori_loop(0, CHIPS // 2, pair, 0)
    split_rows(dot(o_out[...], wo[1]), mine_out, send)


def gelu_parts(u):
    phi = 0.5 * (1.0 + lax.erf(u * 0.7071067811865476))
    return phi


def up_half_kernel(*refs):
    half_columns(refs[:4], refs[4], 0, 1)


def ffn_kernel(*refs):
    parts, (up_mine, up_pair, down_own, down_pair, vec) = refs[:4], refs[4:9]
    low_out, u_out, a_out, up_out, down_out, mine_out = refs[9:15]
    send = refs[15:]
    chip, _ = place()
    whole_columns(up_mine, up_pair, up_out)
    down_out[...] = pair_rows(down_own, down_pair)
    low = stack_rows(parts)
    low_out[...] = low
    u = dot(low, up_out[...]) + vec[pl.ds(13 + chip, 1), :]
    u_out[...] = u
    a_out[...] = (u * gelu_parts(u)).astype(BF)
    split_rows(dot(a_out[...], down_out[...]), mine_out, send)


def stack_kernel(r0, r1, r2, r3, out, spread_out):
    n = r0.shape[0]
    for k, part in enumerate((r0, r1, r2, r3)):
        out[k * n : (k + 1) * n, :] = part[...]
        for slot in range(SLOTS):
            spread_out[slot, k * n : (k + 1) * n, :] = part[...]


def logits_kernel(length, h0_ref, h1_ref, ids_ref, e_ref, l_ref, pay_ref, h_ref, m_ref, s_ref, p_ref):
    i = pl.program_id(0)
    half = h0_ref.shape[0]

    @pl.when(i == 0)
    def _():
        h_ref[:half, :] = h0_ref[...]
        h_ref[half:, :] = h1_ref[...]
        m_ref[...] = jnp.full_like(m_ref, -3e38)
        s_ref[...] = jnp.zeros_like(s_ref)
        p_ref[...] = jnp.zeros_like(p_ref)

    x = dot(e_ref[...], h_ref[...], NT)
    l_ref[...] = x
    entry = lax.broadcasted_iota(jnp.int32, x.shape, 0) + i * x.shape[0]
    peak = jnp.maximum(m_ref[0:1, :], jnp.max(x, axis=0, keepdims=True))
    total = s_ref[0:1, :] * jnp.exp(m_ref[0:1, :] - peak) + jnp.sum(jnp.exp(x - peak), axis=0, keepdims=True)
    pick = p_ref[0:1, :] + jnp.sum(jnp.where(entry == ids_ref[...], x, 0.0), axis=0, keepdims=True)
    m_ref[0:1, :], s_ref[0:1, :], p_ref[0:1, :] = peak, total, pick

    @pl.when(i == pl.num_programs(0) - 1)
    def _():
        pay_ref[...] = jnp.zeros_like(pay_ref)
        norm = peak + jnp.log(total)
        lane = lax.broadcasted_iota(jnp.int32, (1, 2 * length), 1)
        chip, core = place()
        for n in range(2 * half // (2 * length)):
            s = slice(n * 2 * length, (n + 1) * 2 * length)
            d, rest = divmod(2 * n * length, half)
            first = rest // length
            team, k = first // CHIPS, first % CHIPS
            rows = (
                jnp.where(lane < length, norm[:, s], pltpu.roll(pick[:, s], length, 1)),
                jnp.where(lane < length, pltpu.roll(norm[:, s], length, 1), pick[:, s]),
            )
            for j in range(2):
                q = team * TEAM + (chip ^ (k + j)) * CORES + (core ^ d)
                pay_ref[pl.ds(q, 1), :] = rows[j]


def logits(held, pair, ids, embedding, length, questions):
    half, vocab, width = held.shape[0], embedding.shape[0], embedding.shape[1]
    tile = min(2 * VOCAB_TILE, vocab)
    stat = pltpu.VMEM((8, 2 * half), F32)
    whole = pl.BlockSpec(memory_space=pltpu.VMEM)
    return pl.pallas_call(
        functools.partial(logits_kernel, length),
        grid=(vocab // tile,),
        in_specs=[whole, whole, whole, pl.BlockSpec((tile, width), lambda i: (i, 0))],
        out_specs=[
            pl.BlockSpec((tile, 2 * half), lambda i: (i, 0)),
            pl.BlockSpec((questions, 2 * length), lambda i: (0, 0)),
        ],
        out_shape=[
            pltpu.HBM((vocab, 2 * half), F32),
            jax.ShapeDtypeStruct((questions, 2 * length), F32),
        ],
        scratch_shapes=[pltpu.VMEM((2 * half, width), BF), stat, stat, stat],
        compiler_params=limit(14 + 24 * half * tile // MIB),
        cost_estimate=work(10),
    )(held, pair, ids, embedding)


def merge_kernel(length, all_ref, info_ref, counts_ref, ids_ref, rows_out, own_out, logp_out, prior_out, n_ref, g_ref):
    n_slot, n_pb = n_ref.shape[0], n_ref.shape[1]
    chip, core = place()
    me, slot = lax.axis_index("pb"), lax.axis_index("slot")
    lane = lax.broadcasted_iota(jnp.int32, (1, 2 * length), 1)
    logps, priors = [], None
    for s in range(n_slot):
        blocks = [all_ref[s * n_pb + j, :n_pb, :] for j in range(n_pb)]
        peak = blocks[0]
        for b in blocks[1:]:
            peak = jnp.maximum(peak, b)
        total = jnp.zeros_like(peak)
        pick = jnp.zeros_like(peak)
        for b in blocks:
            total = total + jnp.exp(b - peak)
            pick = pick + b
        norm = peak + jnp.log(total)
        n_ref[s] = norm
        own = info_ref[s * n_pb : (s + 1) * n_pb, :]
        mask = own
        prior = pltpu.roll(own, length, 1)
        logp = pltpu.roll(pick, length, 1) - norm + prior
        logps.append(jnp.where(counts_ref[...] > s, logp, -1e30))
    top = logps[0]
    for p in logps[1:]:
        top = jnp.maximum(top, p)
    total = jnp.zeros_like(top)
    for p in logps:
        total = total + jnp.exp(p - top)
    merged = top + jnp.log(total)
    for s in range(n_slot):
        g_ref[s] = jnp.where(counts_ref[...] > s, -mask * jnp.exp(logps[s] - merged), 0.0)
    n_rows = n_ref.shape[1]
    row = lax.broadcasted_iota(jnp.int32, merged.shape, 0)
    logp_out[...] = jnp.sum(jnp.where(row == me, merged, 0.0), axis=0, keepdims=True)
    own_grad = jnp.where(lane < length, g_ref[slot, pl.ds(me, 1), :], 0.0)
    prior_out[...] = jnp.sum(own_grad, axis=1, keepdims=True)
    rows_out[...] = jnp.zeros_like(rows_out)
    half = rows_out.shape[3]
    for s in range(n_slot):
        for d in range(CORES):
            for n in range(half // (2 * length)):
                team, c = (2 * n) // CHIPS, (2 * n) % CHIPS
                q = [team * TEAM + (chip ^ (c + j)) * CORES + (core ^ d) for j in range(2)]
                t = slice(n * 2 * length, (n + 1) * 2 * length)
                for r, (first, second) in enumerate(
                    (
                        (n_ref[s, pl.ds(q[0], 1), :], n_ref[s, pl.ds(q[1], 1), :]),
                        (g_ref[s, pl.ds(q[0], 1), :], g_ref[s, pl.ds(q[1], 1), :]),
                        (ids_ref[pl.ds(q[0], 1), :], ids_ref[pl.ds(q[1], 1), :]),
                    )
                ):
                    rows_out[s, d, r : r + 1, t] = jnp.where(lane < length, first, pltpu.roll(second, length, 1))
    own_out[0] = rows_out[slot]


def merge(everyone, info, counts, ids, length, n_slot, n_pb, half):
    held = pltpu.VMEM((n_slot, n_pb, 2 * length), F32)
    return pl.pallas_call(
        functools.partial(merge_kernel, length),
        out_shape=[
            jax.ShapeDtypeStruct((n_slot, CORES, 8, half), F32),
            jax.ShapeDtypeStruct((1, CORES, 8, half), F32),
            jax.ShapeDtypeStruct((1, 2 * length), F32),
            jax.ShapeDtypeStruct((1, 1), F32),
        ],
        scratch_shapes=[held, held],
        compiler_params=limit(16 + 2 * everyone.size * 4 // MIB),
        cost_estimate=work(2),
    )(everyone, info, counts, ids)


def logit_gradient(x, rows, first):
    entry = (lax.broadcasted_iota(jnp.int32, x.shape, 0) + first).astype(F32)
    hit = jnp.where(entry == rows[2:3, :], 1.0, 0.0)
    return (rows[1:2, :] * (hit - jnp.exp(x - rows[0:1, :]))).astype(BF)


def state_grad_kernel(l_ref, rows_ref, e_ref, own_ref, pair_ref, d_ref, acc_ref):
    i = pl.program_id(0)
    half = own_ref.shape[0]

    @pl.when(i == 0)
    def _():
        acc_ref[...] = jnp.zeros_like(acc_ref)

    tile = l_ref.shape[0]
    d = [logit_gradient(l_ref[:, c * half : (c + 1) * half], rows_ref[0, c], i * tile) for c in range(CORES)]
    d_ref[...] = jnp.concatenate(d, axis=1)
    acc_ref[...] += dot(d_ref[...], e_ref[...], TN)

    @pl.when(i == pl.num_programs(0) - 1)
    def _():
        own_ref[...] = acc_ref[:half, :].astype(own_ref.dtype)
        pair_ref[...] = acc_ref[half:, :].astype(BF)


def state_grad(scores, rows, embedding, own_type):
    vocab, count = scores.shape
    width = embedding.shape[1]
    half = count // CORES
    tile = min(2 * VOCAB_TILE, vocab)
    last = pl.BlockSpec((half, width), lambda i: (0, 0))
    return pl.pallas_call(
        state_grad_kernel,
        grid=(vocab // tile,),
        in_specs=[
            pl.BlockSpec((tile, count), lambda i: (i, 0)),
            pl.BlockSpec((1,) + rows.shape[1:], lambda i: (0, 0, 0, 0)),
            pl.BlockSpec((tile, width), lambda i: (i, 0)),
        ],
        out_specs=[last, last, pl.BlockSpec((tile, count), lambda i: (i, 0))],
        out_shape=[
            jax.ShapeDtypeStruct((half, width), own_type),
            jax.ShapeDtypeStruct((half, width), BF),
            pltpu.HBM((vocab, count), BF),
        ],
        scratch_shapes=[pltpu.VMEM((count, width), F32)],
        compiler_params=limit(16 + 20 * half * tile // MIB + count * width * 4 // MIB),
        cost_estimate=work(11),
    )(in_hbm(scores), rows, embedding)


def own_embedding_kernel(d_ref, own_ref, pair_ref, *refs):
    half = own_ref.shape[0]
    refs[-1][...] = dot(d_ref[:, :half], own_ref[...]) + dot(d_ref[:, half:], pair_ref[...])


def own_embedding(d, own, pair, held, piece, count):
    vocab, tokens = d.shape
    tile = min(VOCAB_TILE, vocab // count)
    steps = vocab // count // tile
    ahead = [] if held is None else [held]
    whole = pl.BlockSpec(memory_space=pltpu.VMEM)
    shape = (vocab, own.shape[1])
    return pl.pallas_call(
        own_embedding_kernel,
        grid=(steps,),
        in_specs=[pl.BlockSpec((tile, tokens), lambda i: (piece * steps + i, 0)), whole, whole]
        + [pl.BlockSpec(memory_space=pl.ANY)] * len(ahead),
        out_specs=pl.BlockSpec((tile, shape[1]), lambda i: (piece * steps + i, 0)),
        out_shape=pltpu.HBM(shape, F32),
        input_output_aliases={3: 0} if ahead else {},
        compiler_params=limit(14),
        cost_estimate=work(1),
    )(d, own, pair, *ahead)


def embedding_kernel(base, rows_ref, own_ref, pair_ref, e_ref, held_ref, o_ref):
    first = base + pl.program_id(0) * e_ref.shape[0]
    slot = lax.axis_index("slot")
    o_ref[...] = held_ref[...]

    def other(k, carry):
        n = slot ^ k
        for top in range(0, own_ref.shape[1], TOKENS // CORES):
            t = slice(top, top + TOKENS // CORES)
            h = jnp.concatenate([own_ref[n, t, :], pair_ref[n, t, :]], axis=0)
            rows = jnp.concatenate([rows_ref[n, 0, :, t], rows_ref[n, 1, :, t]], axis=1)
            o_ref[...] += dot(logit_gradient(dot(e_ref[...], h, NT), rows, first), h)
        return carry

    lax.fori_loop(1, own_ref.shape[0], other, 0)


def embedding_piece(rows, states, embedding, held, first, size):
    width = embedding.shape[1]
    tile = min(VOCAB_TILE, size)
    steps = size // tile
    whole = pl.BlockSpec(memory_space=pltpu.VMEM)
    block = pl.BlockSpec((tile, width), lambda i: (first // tile + i, 0))
    return pl.pallas_call(
        functools.partial(embedding_kernel, first),
        grid=(steps,),
        in_specs=[whole, whole, whole, block, block],
        out_specs=block,
        out_shape=pltpu.HBM(embedding.shape, F32),
        input_output_aliases={4: 0},
        compiler_params=limit(24),
        cost_estimate=work(3 * size / 1024),
    )(rows, *states, embedding, held)


def add_kernel(mine, got, own_out, *send):
    length = own_out.shape[0]
    for k in range(CHIPS):
        s = slice(k * length, (k + 1) * length)
        y = mine[s, :] + got[s, :].astype(F32)
        if k == 0:
            own_out[...] = y
        else:
            send[k - 1][...] = y.astype(BF)


def norm_back_kernel(row, has_base, *refs):
    base = refs[0] if has_base else None
    mine, r1, r2, r3, z, inv, vec, dr_out, e_out, sums_out = refs[1 if has_base else 0 :]
    dh = mine[...] + r1[...].astype(F32) + r2[...].astype(F32) + r3[...].astype(F32)
    if has_base:
        dh = dh + base[...]
    dr = norm_back(dh, z[...], inv[...], vec[6 + row : 7 + row, :])
    e = dr.astype(BF)
    dr_out[...] = dr
    e_out[...] = e
    sums_out[...] = jnp.zeros_like(sums_out)
    sums_out[0:1, :] = jnp.sum(dh * z[...], axis=0, keepdims=True)
    sums_out[1:2, :] = jnp.sum(dh, axis=0, keepdims=True)
    sums_out[2:3, :] = jnp.sum(e.astype(F32), axis=0, keepdims=True)


def stack_rows(parts):
    return jnp.concatenate([p[...] for p in parts], axis=0)


def split_rows(y, mine_out, send):
    length = mine_out.shape[0]
    mine_out[...] = y[:length]
    for k in range(1, CHIPS):
        send[k - 1][...] = y[k * length : (k + 1) * length].astype(BF)


def column_sum(y):
    return jnp.sum(y.astype(F32), axis=0, keepdims=True)


def ffn_back_kernel(*refs):
    parts, (u_ref, up, down), (e_out, du_out, sum_out, mine_out), send = refs[:4], refs[4:7], refs[7:11], refs[11:]
    e = stack_rows(parts)
    e_out[...] = e
    da = dot(e, down[...], NT).astype(BF).astype(F32)
    u = u_ref[...]
    slope = gelu_parts(u) + u * (jnp.exp(-0.5 * u * u) * 0.3989422804014327)
    du = (da * slope).astype(BF)
    du_out[...] = du
    sum_out[...] = column_sum(du)
    split_rows(dot(du, up[...], NT), mine_out, send)


def pick_core(g, mine_out, other_out, top):
    _, core = place()
    lo, hi = g[:, :, 0], g[:, :, 1]
    n = lo.shape[1] * lo.shape[2]
    mine = jnp.where(core == 0, lo, hi).reshape(CHIPS, n, g.shape[-1])
    other = jnp.where(core == 0, hi, lo).reshape(CHIPS, n, g.shape[-1])
    mine_out[:, top : top + n, :] = mine.astype(BF)
    other_out[:, top : top + n, :] = other.astype(BF)


def place_columns(g, mine_out, other_out, top):
    unit = g.shape[0] // (CHIPS * CHIPS * CORES)
    pick_core(g.reshape(CHIPS, CHIPS, CORES, unit, g.shape[1]), mine_out, other_out, top)


def place_rows(g, mine_out, other_out, top):
    unit = g.shape[0] // (CHIPS * CORES)
    pick_core(g.reshape(CHIPS, 1, CORES, unit, g.shape[1]), mine_out, other_out, top)


def place_row_blocks(g, mine_out, other_out, top, lanes):
    unit = g.shape[0] // (CHIPS * CORES)
    for b in range(g.shape[1] // lanes):
        place_rows(g[:, b * lanes : (b + 1) * lanes], mine_out, other_out, top + b * unit)


def ffn_grads_kernel(low, du, a, e, mine_out, other_out):
    g = dot(low[...], du[...], TN)
    place_columns(g, mine_out, other_out, 0)
    g2 = dot(a[...], e[...], TN)
    place_rows(g2, mine_out, other_out, g.shape[0] // (CHIPS * CORES))


def cross_back_kernel(*refs):
    parts, (w_mine, w_cols, q_ref, k_ref, v_ref) = refs[:4], refs[4:9]
    (e_out, dq_out, dk_out, dv_out, mine_out), send, g_ref = refs[9:14], refs[14:-1], refs[-1]
    quarter = q_ref.shape[1]
    length, memory = q_ref.shape[0] // CHIPS, k_ref.shape[0] // CHIPS
    e = stack_rows(parts)
    e_out[...] = e
    g = dot(e, w_mine[1], NT).astype(BF)
    g_ref[...] = g

    def question(i, carry):
        s, t = rows_at(i * length, length, 16), rows_at(i * memory, memory, 16)
        dq_out[s, :], dk_out[t, :], dv_out[t, :] = attend_back(g_ref[s, :], q_ref[s, :], k_ref[t, :], v_ref[t, :], False)
        return carry

    lax.fori_loop(0, CHIPS, question, 0)
    split_rows(dot(dq_out[...], w_cols[:, :quarter], NT), mine_out, send)


def cross_grads_kernel(low, dq, m, dk, dv, o, e, mine_out, other_out, sums_out):
    n = low.shape[1] // (CHIPS * CORES)
    for j, (a, g) in enumerate(((low, dq), (m, dk), (m, dv))):
        place_columns(dot(a[...], g[...], TN), mine_out, other_out, j * n)
    place_row_blocks(dot(o[...], e[...], TN), mine_out, other_out, 3 * n, dq.shape[1])
    sums_out[...] = jnp.zeros_like(sums_out)
    sums_out[0:1, :] = column_sum(dq[...])
    sums_out[1:2, :] = column_sum(dv[...])


def self_back_kernel(*refs):
    parts, (w_mine, q_ref, k_ref, v_ref), (e_out, d_out, g_ref) = refs[:4], refs[4:8], refs[8:]
    quarter = q_ref.shape[1]
    length = q_ref.shape[0] // CHIPS
    e = stack_rows(parts)
    e_out[...] = e
    g = dot(e, w_mine[0], NT).astype(BF)
    g_ref[...] = g

    def pair(i, carry):
        for j in range(2):
            s = rows_at((2 * i + j) * length, length, 16)
            dq, dk, dv = attend_back(g_ref[s, :], q_ref[s, :], k_ref[s, :], v_ref[s, :], True)
            d_out[s, :quarter] = dq
            d_out[s, quarter : 2 * quarter] = dk
            d_out[s, 2 * quarter :] = dv
        return carry

    lax.fori_loop(0, CHIPS // 2, pair, 0)


SMALL = 16


def self_grads_kernel(x, d, o, e, c_sums, sum_in, one, two, three, mine_out, other_out):
    chip, core = place()
    quarter = d.shape[1] // 3
    n = x.shape[1] // (CHIPS * CORES)
    g = dot(x[...], d[...], TN)
    for j in range(3):
        place_columns(g[:, j * quarter : (j + 1) * quarter], mine_out, other_out, j * n)
    place_row_blocks(dot(o[...], e[...], TN), mine_out, other_out, 3 * n, quarter)

    def spread(row):
        zero = jnp.zeros_like(row)
        return jnp.concatenate([jnp.where(chip == b, row, zero) for b in range(CHIPS)], axis=1)

    rows = [
        spread(column_sum(d[:, :quarter])), spread(column_sum(d[:, 2 * quarter :])), one[2:3, :],
        spread(c_sums[0:1, :]), spread(c_sums[1:2, :]), two[2:3, :], one[0:1, :], two[0:1, :], three[0:1, :],
        one[1:2, :], two[1:2, :], three[1:2, :], three[2:3, :],
    ]
    v = jnp.concatenate(rows + [jnp.zeros((SMALL - len(rows), x.shape[1]), F32)], axis=0)
    unit = x.shape[1] // (CHIPS * CHIPS * CORES)
    wide = sum_in.shape[1] // (CHIPS * CORES)
    last = sum_in[...]
    top = 4 * n
    for out in (mine_out, other_out):
        out[:, top:, :] = jnp.zeros((CHIPS, 2 * SMALL, quarter), BF)
    for s in range(CHIPS):
        halves, ends = [], []
        for c in range(CORES):
            parts = [v[:, ((s * CHIPS + b) * CORES + c) * unit :][:, :unit] for b in range(CHIPS)]
            halves.append(jnp.concatenate(parts, axis=1))
            ends.append(last[:, (s * CORES + c) * wide :][:, :wide])
        for out, swap in ((mine_out, False), (other_out, True)):
            first = (core == 0) != swap
            out[s, top : top + SMALL, : CHIPS * unit] = jnp.where(first, halves[0], halves[1]).astype(BF)
            out[s, top + SMALL : top + SMALL + 1, :wide] = jnp.where(first, ends[0], ends[1]).astype(BF)


def input_back_kernel(d, w_self, dk, dv, w_cross, f_got, mine_out, rest_out, *send):
    chip, _ = place()
    quarter = dk.shape[1]
    length, memory = d.shape[0] // CHIPS, dk.shape[0] // CHIPS
    y = dot(d[...], w_self[...], NT)
    m = dot(dk[...], w_cross[:, quarter : 2 * quarter], NT) + dot(dv[...], w_cross[:, 2 * quarter :], NT)
    f = sum(f_got[n].astype(F32) for n in range(SLOTS)).astype(BF)
    both = length + memory
    unit = (send[0].shape[0] - both)
    rest_out[...] = f[CHIPS * unit :]
    mine_out[:length, :] = y[:length]
    mine_out[length:, :] = m[:memory]
    for k, out in enumerate(send):
        if k:
            out[:length, :] = y[k * length : (k + 1) * length].astype(BF)
            out[length:both, :] = m[k * memory : (k + 1) * memory].astype(BF)
        block = jnp.zeros((unit, f.shape[1]), BF)
        for b in range(CHIPS):
            block = jnp.where((chip ^ k) == b, f[b * unit : (b + 1) * unit], block)
        out[both:, :] = block


def input_total_kernel(base, mine, own, r1, r2, r3, source_out, memory_out, up_out):
    chip, _ = place()
    length = base.shape[0]
    both = mine.shape[0]
    width = base.shape[1]
    y = mine[...]
    for k, r in enumerate((own, r1, r2, r3)):
        if k:
            y = y + r[:both, :].astype(F32)
        up_out[:, rows_at((chip ^ k) * width, width, 128)] = r[both:, :].astype(F32)
    source_out[...] = base[...] + y[:length]
    memory_out[...] = y[length:]


def core_sum_kernel(mine, got, out):
    for n in range(SLOTS):
        out[n] = (mine[n].astype(F32) + got[n].astype(F32)).astype(BF)


def attn_pieces_kernel(s_got, c_got, *outs):
    *pieces, rest = outs
    chip, _ = place()
    s = sum(s_got[n].astype(F32) for n in range(SLOTS)).astype(BF)
    c = sum(c_got[n].astype(F32) for n in range(SLOTS)).astype(BF)
    top = 3 * c.shape[0] // 4
    unit = top // (3 * CHIPS)
    both = [y[:top].reshape(3, CHIPS, unit, y.shape[1]) for y in (s, c)]
    for k in range(CHIPS):
        for m, y in enumerate(both):
            for j in range(3):
                block = jnp.zeros((unit, y.shape[3]), BF)
                for b in range(CHIPS):
                    block = jnp.where((chip ^ k) == b, y[j, b], block)
                pieces[k][(3 * m + j) * unit : (3 * m + j + 1) * unit, :] = block
        pieces[k][6 * unit :, :] = s[c.shape[0] : c.shape[0] + SMALL]
    n = c.shape[0] - top
    rest[:n, :] = s[top : top + n]
    rest[n : 2 * n, :] = c[top:]
    rest[2 * n :, :] = s[c.shape[0] + SMALL :]


def attn_out_kernel(p0, p1, p2, p3, out, bias_out, gain_out, shift_out, last_out):
    chip, _ = place()
    unit, quarter = out.shape[1], p0.shape[1]
    parts = (p0, p1, p2, p3)
    for k, p in enumerate(parts):
        lanes = rows_at((chip ^ k) * quarter, quarter, 128)
        for j in range(6):
            out[j, :, lanes] = p[j * unit : (j + 1) * unit, :].astype(F32)
    total = sum(p[6 * unit :, : CHIPS * unit].astype(F32) for p in parts)
    mine = jnp.zeros((SMALL, unit), F32)
    for b in range(CHIPS):
        mine = jnp.where(chip == b, total[:, b * unit : (b + 1) * unit], mine)
    bias_out[...] = mine[0:6]
    gain_out[...] = mine[6:9]
    shift_out[...] = mine[9:12]
    last_out[...] = mine[12:13]


def rows_out_kernel(owned, f_owned, out, down_out, in_out):
    unit, quarter = out.shape[1], owned.shape[1]
    n = CHIPS * unit
    for m in range(2):
        for b in range(CHIPS):
            out[m, :, b * quarter : (b + 1) * quarter] = owned[m * n + b * unit : m * n + (b + 1) * unit, :].astype(F32)
    down_out[...] = f_owned[...].astype(F32)
    in_out[...] = owned[2 * n : 2 * n + 1, : in_out.shape[1]].astype(F32)


def shards(
    inputs, memory, attn_weight, attn_out, ffn_in, ffn_out, attn_bias, norm_gain, norm_bias,
    bias_in, bias_out, embedding, targets, slot_counts, pad_mask, log_prior,
):
    n_pb, n_slot = lax.axis_size("pb"), lax.axis_size("slot")
    n_all = n_pb * n_slot
    teams = n_pb // TEAM
    me = lax.axis_index("pb")
    length, width = inputs.shape[2], inputs.shape[3]
    passage = memory.shape[2]
    quarter = width // CHIPS
    unit = width // (TEAM * n_slot)
    vocab_rows = embedding.shape[0]
    embedding = in_hbm(embedding)

    def team_rows(w):
        if teams == 1:
            return w
        w = lax.all_gather(w, "pb", axis=0, tiled=True)
        n = w.shape[0] // TEAM
        return lax.dynamic_slice_in_dim(w, (me % TEAM) * n, n)

    x, m = inputs[0, 0], memory[0, 0]
    attn_w = jnp.moveaxis(team_rows(attn_weight), 1, 0)
    out_w = jnp.moveaxis(team_rows(attn_out), 1, 0)
    up_w = team_rows(ffn_in)
    down_w = team_rows(ffn_out)
    rows = attn_w.shape[1]
    ff = up_w.shape[1] // CHIPS
    vec = jnp.concatenate(
        [attn_bias.T, norm_gain.T, norm_bias.T, bias_out[None], bias_in.reshape(CHIPS, -1)], axis=0
    )
    ids = (targets - me * vocab_rows).astype(jnp.int32)
    own_row = jnp.concatenate([pad_mask.astype(F32), jnp.broadcast_to(log_prior, (1, length))], axis=1)
    own_rows_all = lax.all_to_all(
        jnp.broadcast_to(own_row[None], (n_all,) + own_row.shape), ("slot", "pb"), 0, 0, tiled=True
    ).reshape(n_all, 2 * length)

    block = (length, width)
    every = (CHIPS * length, width)
    cols = (CHIPS * length, quarter)
    m_cols = (CHIPS * passage, quarter)
    sends = [(block, BF)] * 3

    def give(send):
        return [from_chip(send[k - 1], k) for k in range(1, CHIPS)]

    def give_far(send):
        return [in_hbm(r) for r in give(send)]

    far_call = functools.partial(call, far=True)

    first = call(functools.partial(pack_kernel, 6, 0), [((CHIPS * length + 6 * rows, quarter), BF)] * CHIPS, x, attn_w)
    got_first = [first[0]] + give(first[1:])
    got_first[3], vec = tie(got_first[3], vec)
    got_first[1], own_rows_all = tie(got_first[1], own_rows_all)
    pair_first = [from_core(g) for g in got_first]
    out_pair = from_core(out_w)
    down_pair = from_core(down_w)
    third = list(call(functools.partial(pack_kernel, 1, 0), [((rows, ff), BF)] * CHIPS, up_w[None]))
    m_send, pair_first[3] = tie(m, pair_first[3])
    got_memory = [m, from_chip(m_send, 1), from_chip(m_send, 2)]

    x_all, w_self, queries, keys, values, mixed, w_out, mine, *send = call(
        self_kernel,
        [(every, BF), ((width, 3 * quarter), BF)] + [(cols, BF)] * 4 + [((2, quarter, width), BF), (block, F32)]
        + sends,
        *got_first, *pair_first, out_w, out_pair, vec,
    )
    got_memory[1], send[0] = tie(got_memory[1], send[0])
    got = give(send)
    got_memory.append(from_chip(got_memory[1], 2))
    *got_memory, got[0], got[1], got[2] = tie(*got_memory, *got)
    norm_outs = [(block, F32), (block, BF), (block, F32), ((length, 1), F32)]
    hidden_one, low_one, z_one, inv_one = call(
        functools.partial(norm_kernel, (2, 6, 9)), norm_outs, x, mine, *got, vec, us=1
    )
    got_low = [low_one] + others(low_one)
    got_third = [third[0], from_chip(third[1], 1), from_chip(third[2], 2)]
    m_all, w_cross, cross_keys, cross_values = call(
        memory_kernel, [((CHIPS * passage, width), BF), ((width, 3 * quarter), BF)] + [(m_cols, BF)] * 2,
        *got_memory, *got_first, *pair_first, vec,
    )
    got_third[1], got_third[2], *got_low = tie(got_third[1], got_third[2], *got_low)
    low_one_all, cross_queries, cross_mixed, mine, *send = call(
        cross_kernel, [(every, BF), (cols, BF), (cols, BF), (block, F32)] + sends,
        *got_low, w_out, w_cross, cross_keys, cross_values, vec,
    )
    got = give(send)
    third[3], got_third[1] = tie(third[3], got_third[1])
    got_third.append(from_chip(third[3], 3))
    got_third[3], *got = tie(got_third[3], *got)
    hidden_two, low_two, z_two, inv_two = call(
        functools.partial(norm_kernel, (5, 7, 10)), norm_outs, hidden_one, mine, *got, vec, us=1
    )
    got_low = [low_two] + others(low_two)
    (up_half,) = call(up_half_kernel, [((CHIPS, rows, ff), BF)], *got_third)
    up_half_pair = from_core(up_half)
    low_two_all, upward, active, w_up, w_down, mine, *send = call(
        ffn_kernel,
        [(every, BF), ((CHIPS * length, ff), F32), ((CHIPS * length, ff), BF), ((width, ff), BF)]
        + [((ff, width), BF), (block, F32)]
        + sends,
        *got_low, up_half, up_half_pair, down_w, down_pair, vec,
    )
    got = give(send)
    _, final_low, z_three, inv_three = call(
        functools.partial(norm_kernel, (12, 8, 11)), norm_outs, hidden_two, mine, *got, vec, us=1
    )

    held, spread_held = call(
        stack_kernel, [(every, BF), ((n_slot,) + every, BF)], final_low, *others(final_low), us=1, far=(1,) if teams == 1 else ()
    )
    pair = from_core(held)

    def all_teams(h):
        return lax.all_gather(h, "pb", axis_index_groups=same_place_groups(), axis=0, tiled=True) if teams > 1 else h

    half = teams * CHIPS * length
    chip, core = place()
    order = [
        t * TEAM + (chip ^ k) * CORES + (core ^ d) for d in range(CORES) for t in range(teams) for k in range(CHIPS)
    ]
    ids_row = jnp.concatenate([lax.dynamic_slice_in_dim(ids, q, 1) for q in order], axis=1)
    states = [all_teams(held), all_teams(pair)]
    scores, payload = logits(*states, ids_row, embedding, length, n_pb)
    everyone = lax.all_to_all(
        jnp.broadcast_to(payload[None], (n_all,) + payload.shape), ("slot", "pb"), 0, 0, tiled=True
    )
    ids_wide = jnp.pad(ids.astype(F32), ((0, 0), (0, length)))
    spread_held, everyone = tie(spread_held, everyone)
    all_held = across_slots(spread_held)
    token_rows, own_rows, token_logprob, prior_grad = merge(
        everyone, own_rows_all, slot_counts.astype(jnp.int32)[:, None], ids_wide, length, n_slot, n_pb, half
    )
    def home(partial):
        if teams == 1:
            return partial
        return lax.psum_scatter(partial, "pb", axis_index_groups=same_place_groups(), scatter_dimension=0, tiled=True)

    own_part, for_pair, own_logits = state_grad(scores, own_rows, embedding, F32)
    own_logits = in_hbm(own_logits)
    own_part, got_pair = home(own_part), from_core(home(for_pair))
    mine, *send = call(add_kernel, [(block, F32)] + sends, own_part, got_pair, us=1)
    got = give(send)
    own_logits, send[0] = tie(own_logits, send[0])
    own_terms = own_embedding(own_logits, *states, None, 0, 2)
    own_terms, *got = tie(own_terms, *got)

    eighth = vocab_rows // 8
    parts = (1, 1, 1, 5)
    made = []

    def piece(*wait):
        n = len(made) - 1
        rows_in, *wait = tie(token_rows, *wait)
        first = sum(parts[:n]) * eighth
        made.append(embedding_piece(rows_in, states, embedding, made[-1], first, parts[n] * eighth))
        return wait

    def pieces(count, *wait):
        for _ in range(count):
            wait = piece(*wait)
        return list(wait)

    def then(*values):
        *values, made[-1] = tie(*values, made[-1])
        return values

    def settle(g):
        if teams == 1:
            return g
        g = lax.psum(g, "pb", axis_index_groups=same_place_groups())
        g = lax.all_gather(g, "pb", axis_index_groups=team_groups(), axis=0, tiled=True)
        n = g.shape[0] // n_pb
        return lax.dynamic_slice_in_dim(g, me * n, n)

    def to_owner(g):
        pairs = []
        for s in range(n_slot):
            for i in range(n_pb):
                t, b, c = i // TEAM, (i % TEAM) // CORES, i % CORES
                pairs.append((s * n_pb + i, b * n_pb + t * TEAM + s * CORES + c))
        return lax.ppermute(g, ("slot", "pb"), pairs)

    x_all, w_self, queries, keys, values, mixed, w_out, m_all, w_cross, cross_keys, cross_values = (
        in_hbm(v)
        for v in (x_all, w_self, queries, keys, values, mixed, w_out, m_all, w_cross, cross_keys, cross_values)
    )
    low_one_all, cross_queries, cross_mixed, low_two_all, upward, active, w_up, w_down = (
        in_hbm(v) for v in (low_one_all, cross_queries, cross_mixed, low_two_all, upward, active, w_up, w_down)
    )
    z_one, z_two, z_three = in_hbm(z_one), in_hbm(z_two), in_hbm(z_three)
    grads = [(block, F32), (block, BF), ((8, width), F32)]
    dr_three, e_three, sums_three = call(
        functools.partial(norm_back_kernel, 2, False), grads, mine, *got, z_three, inv_three, vec, us=1
    )
    got_e = others(e_three)
    own_logits, e_three = tie(own_logits, e_three)
    own_terms = own_embedding(own_logits, *states, own_terms, 1, 2)
    own_terms, *got_e = tie(own_terms, *got_e)
    made.append(own_terms)
    e_all, du, sum_in, mine, *send = call(
        ffn_back_kernel,
        [(every, BF), ((CHIPS * length, ff), BF), ((1, ff), F32), (block, F32)] + sends,
        e_three, *got_e, upward, w_up, w_down,
    )
    got = give(send)
    f_shape = (n_slot, CHIPS * unit + ff // TEAM, width)
    du, send[0] = tie(du, send[0])
    f_mine, f_other = far_call(ffn_grads_kernel, [(f_shape, BF)] * 2, low_two_all, du, active, e_all, us=3)
    f_other, all_held, *got = tie(f_other, all_held, *got)
    all_pair = from_core(all_held)
    dr_two, e_two, sums_two = far_call(
        functools.partial(norm_back_kernel, 1, True), grads, dr_three, mine, *got, z_two, inv_two, vec, us=1
    )
    got_e = give_far([e_two] * 3)
    f_got = from_core(f_other)
    f_got, all_pair, got_e[2] = tie(f_got, all_pair, got_e[2])
    states = [jnp.stack([all_teams(h[n]) for n in range(n_slot)]) if teams > 1 else h for h in (all_held, all_pair)]
    (f_total,) = far_call(core_sum_kernel, [(f_shape, BF)], f_mine, f_got)
    f_got = across_slots(f_total)
    e_all_two, dqc, dkc, dvc, mine, *send = far_call(
        cross_back_kernel,
        [(every, BF), (cols, BF), (m_cols, BF), (m_cols, BF), (block, F32)] + sends,
        e_two, *got_e, w_out, w_cross, cross_queries, cross_keys, cross_values, us=5,
        scratch=[pltpu.VMEM(cols, BF)],
    )
    got = give(send)
    dqc, send[0] = tie(dqc, send[0])
    g_shape = (n_slot, 4 * CHIPS * unit, quarter)
    c_mine, c_other, c_sums = call(
        cross_grads_kernel, [(g_shape, BF)] * 2 + [((8, quarter), F32)],
        low_one_all, dqc, m_all, dkc, dvc, cross_mixed, e_all_two,
    )
    c_got = from_core(c_other)
    (c_mine,) = piece(c_mine)
    got = then(*got)
    dr_one, e_one, sums_one = far_call(
        functools.partial(norm_back_kernel, 0, True), grads, dr_two, mine, *got, z_one, inv_one, vec, us=1
    )
    got_e = give([e_one] * 3)
    c_got, e_one = tie(c_got, e_one)
    (c_total,) = far_call(core_sum_kernel, [(g_shape, BF)], c_mine, c_got)
    (c_total,) = piece(c_total)
    got_e = then(*got_e)
    e_all_one, d_self = far_call(
        self_back_kernel, [(every, BF), ((CHIPS * length, 3 * quarter), BF)], e_one, *got_e, w_out, queries, keys, values, us=4,
        scratch=[pltpu.VMEM(cols, BF)],
    )
    c_total, d_self, f_got = tie(c_total, d_self, f_got)
    c_got = across_slots(c_total)
    s_shape = (n_slot, g_shape[1] + 2 * SMALL, quarter)
    s_mine, s_other = far_call(
        self_grads_kernel, [(s_shape, BF)] * 2, x_all, d_self, mixed, e_all_one, c_sums, sum_in, sums_one, sums_two, sums_three
    )
    s_got = from_core(s_other)
    f_got, s_mine = tie(f_got, s_mine)
    both = (length + passage, width)
    f_rest = (f_shape[1] - CHIPS * unit, width)
    mine, f_rest, *send = far_call(
        input_back_kernel, [(both, F32), (f_rest, BF)] + [((both[0] + unit, width), BF)] * CHIPS,
        d_self, w_self, dkc, dvc, w_cross, f_got, us=3,
    )
    f_owned = to_owner(f_rest)
    s_got, send[0] = tie(s_got, send[0])
    (s_total,) = far_call(core_sum_kernel, [(s_shape, BF)], s_mine, s_got)
    (s_total,) = pieces(1, s_total)
    (c_got,) = then(c_got)
    s_total, send[0], c_got = tie(s_total, send[0], c_got)
    s_got = across_slots(s_total)
    got = give(send[1:])
    (send[0],) = pieces(len(parts) + 1 - len(made), send[0])
    s_got, *got = then(s_got, *got)
    *piece_parts, rest = call(
        attn_pieces_kernel,
        [((6 * unit + SMALL, quarter), BF)] * CHIPS + [((2 * CHIPS * unit + SMALL, quarter), BF)],
        s_got, c_got,
    )
    last = give(piece_parts[1:])
    owned = to_owner(rest)
    grad_source, grad_passage, out_up = call(
        input_total_kernel, [(block, F32), ((passage, width), F32), ((unit, up_w.shape[1]), F32)],
        dr_one, mine, send[0], *got, us=1,
    )
    owned, grad_source, *last = tie(owned, grad_source, *last)
    out_attn, *vectors = call(
        attn_out_kernel,
        [((6, unit, width), F32), ((6, unit), F32), ((3, unit), F32), ((3, unit), F32), ((1, unit), F32)],
        piece_parts[0], *last, us=1,
    )
    outs, out_down, sum_in_out = call(
        rows_out_kernel, [((2, unit, width), F32), (f_rest.shape, F32), ((1, ff // TEAM), F32)], owned, f_owned, us=1
    )
    out_attn = settle(jnp.moveaxis(out_attn, 0, 1))
    out_outputs = settle(jnp.moveaxis(outs, 0, 1))
    out_up, out_down = settle(out_up), settle(out_down)
    vectors = [settle(v) for v in (vectors[0].T, vectors[1].T, vectors[2].T, sum_in_out[0], vectors[3][0])]
    return (
        token_logprob[:, :length],
        grad_source[None, None],
        grad_passage[None, None],
        prior_grad,
        out_attn,
        out_outputs,
        out_up,
        out_down,
        vectors[0],
        vectors[1],
        vectors[2],
        vectors[3],
        vectors[4],
        made[-1],
    )


def solution(mesh):
    placed = (
        P("pb", "slot", None, None),
        P("pb", "slot", None, None),
        P("pb", None, None),
        P("pb", None, None),
        P("pb", None),
        P("pb", None),
        P(),
        P(),
        P(),
        P(),
        P(),
        P("pb", None),
        P(),
        P(),
        P("pb", None),
        P("pb", "slot"),
    )
    both = ("slot", "pb")
    return jax.shard_map(
        shards,
        mesh=mesh,
        in_specs=placed,
        out_specs=(
            P("pb", None),
            P("pb", "slot", None, None),
            P("pb", "slot", None, None),
            P("pb", "slot"),
            P(both, None, None),
            P(both, None, None),
            P(both, None),
            P(both, None),
            P(both, None),
            P(both, None),
            P(both, None),
            P(both),
            P(both),
            P("pb", None),
        ),
        check_vma=False,
    )
```

```python
import functools

import jax
import jax.numpy as jnp
from jax import lax
from jax.experimental import pallas as pl
from jax.experimental.pallas import tpu as pltpu
from jax.sharding import PartitionSpec as P

HEAD = 64
CHIPS = 4
CORES = 2
TEAM = CHIPS * CORES
SLOTS = 4
BF = jnp.bfloat16
F32 = jnp.float32
TOKENS = 512
VOCAB_TILE = 512


def from_chip(x, k):
    pairs = []
    for i in range(lax.axis_size("pb")):
        place = i % TEAM
        pairs.append((i, i - place + ((place // CORES) ^ k) * CORES + place % CORES))
    return lax.ppermute(x, "pb", pairs)


def from_core(x):
    return lax.ppermute(x, "pb", [(i, i ^ 1) for i in range(lax.axis_size("pb"))])


def across_slot(x, k):
    return lax.ppermute(x, "slot", [(i, i ^ k) for i in range(lax.axis_size("slot"))])


def same_place_groups():
    size = lax.axis_size("pb")
    return [[g * TEAM + j for g in range(size // TEAM)] for j in range(TEAM)]


def team_groups():
    size = lax.axis_size("pb")
    return [[g * TEAM + j for j in range(TEAM)] for g in range(size // TEAM)]


def others(x):
    return [from_chip(x, k) for k in range(1, CHIPS)]


def tie(*values):
    return list(lax.optimization_barrier(values))


def across_slots(x):
    return lax.all_to_all(x, "slot", 0, 0, tiled=True)


def at(x, index):
    return lax.dynamic_index_in_dim(x, index, 0, False)


NN = (((1,), (0,)), ((), ()))
NT = (((1,), (1,)), ((), ()))
TN = (((0,), (0,)), ((), ()))


def dot(a, b, dims=NN):
    return lax.dot_general(a, b, dims, preferred_element_type=F32)


def place():
    j = lax.axis_index("pb") % TEAM
    return j // CORES, j % CORES


def rows_at(start, size, unit):
    return pl.ds(pl.multiple_of(start, unit), size)


MIB = 2**20


def limit(mib):
    return pltpu.CompilerParams(vmem_limit_bytes=min(60, mib) * MIB)


def work(us):
    return pl.CostEstimate(flops=int(us * 1e9), bytes_accessed=0, transcendentals=0)


def call(kernel, outs, *args, us=2.0, far=(), scratch=()):
    shapes = [jax.ShapeDtypeStruct(*o) for o in outs]
    held = sum(a.size * a.dtype.itemsize for a in (*args, *shapes))
    params = limit(8 + held * 5 // 4 // MIB)
    far = range(len(outs)) if far is True else far
    places = [pltpu.HBM(*o) if n in far else s for n, (o, s) in enumerate(zip(outs, shapes))]
    results = pl.pallas_call(
        kernel, out_shape=places, scratch_shapes=scratch, compiler_params=params, cost_estimate=work(us)
    )(*args)
    return [in_hbm(r) if n in far else r for n, r in enumerate(results)]


def in_hbm(x):
    return pltpu.with_memory_space_constraint(x, pltpu.HBM)


def norm_rows(r, gain, shift):
    centered = r - jnp.mean(r, axis=-1, keepdims=True)
    inv = lax.rsqrt(jnp.mean(centered * centered, axis=-1, keepdims=True) + 1e-05)
    z = centered * inv
    return z * gain + shift, z, inv


def norm_back(dh, z, inv, gain):
    dz = dh * gain
    return (dz - jnp.mean(dz, axis=-1, keepdims=True) - z * jnp.mean(dz * z, axis=-1, keepdims=True)) * inv


def lane_head(shape, keys):
    return lax.broadcasted_iota(jnp.int32, shape, 1) // keys


def per_head(x):
    head = lane_head(x.shape, HEAD)
    return jnp.concatenate([jnp.where(head == h, x, jnp.zeros_like(x)) for h in range(x.shape[1] // HEAD)], axis=0)


def own_heads(big, keys):
    count = big.shape[1] // HEAD
    head = lane_head((keys, big.shape[1]), HEAD)
    total = jnp.zeros((keys, big.shape[1]), F32)
    for h in range(count):
        total = total + jnp.where(head == h, big[h * keys : (h + 1) * keys], 0.0)
    return total


def head_probs(q, kbig, keys, causal):
    s = dot(q, kbig, NT) * 0.125
    head = lane_head(s.shape, keys)
    count = s.shape[1] // keys
    if causal:
        query = lax.broadcasted_iota(jnp.int32, s.shape, 0)
        key = lax.broadcasted_iota(jnp.int32, s.shape, 1) % keys
        s = jnp.where(query >= key, s, -1e30)
    peak = jnp.zeros_like(s)
    for h in range(count):
        m = jnp.max(jnp.where(head == h, s, -3e38), axis=1, keepdims=True)
        peak = jnp.where(head == h, m, peak)
    e = jnp.exp(s - peak)
    return e / head_sums(e, head, count)


def head_sums(x, head, count):
    total = jnp.zeros_like(x)
    for h in range(count):
        total = jnp.where(head == h, jnp.sum(jnp.where(head == h, x, 0.0), axis=1, keepdims=True), total)
    return total


def attend(q, k, v, causal):
    probs = head_probs(q, per_head(k), k.shape[0], causal)
    return dot(probs.astype(BF), per_head(v)).astype(BF)


def attend_back(g, q, k, v, causal):
    keys = k.shape[0]
    kbig, vbig = per_head(k), per_head(v)
    probs = head_probs(q, kbig, keys, causal)
    dp = dot(g, vbig, NT)
    head = lane_head(dp.shape, keys)
    ds = (probs * (dp - head_sums(dp * probs, head, dp.shape[1] // keys))).astype(BF)
    dq = dot(ds, kbig) * 0.125
    dk = own_heads(dot(ds, q, TN), keys) * 0.125
    dv = own_heads(dot(probs.astype(BF), g, TN), keys)
    return dq.astype(BF), dk.astype(BF), dv.astype(BF)


def pack_kernel(count, first, *refs):
    *rows_in, w_ref, o0, o1, o2, o3 = refs
    outs = (o0, o1, o2, o3)
    chip, _ = place()
    rows, quarter = w_ref.shape[1], w_ref.shape[2] // CHIPS
    for k in range(CHIPS):
        top = 0
        for x_ref in rows_in:
            x = x_ref[...]
            for b in range(CHIPS):
                outs[k][top : top + x.shape[0], :] = x[:, b * quarter : (b + 1) * quarter]
                top += x.shape[0]
        for j in range(count):
            outs[k][top : top + rows, :] = w_ref[first + j, :, rows_at((chip ^ k) * quarter, quarter, 128)]
            top += rows


def natural_columns(own, pair, w_out, top, count):
    chip, core = place()
    rows = w_out.shape[0] // TEAM
    quarter = own[0].shape[1]
    for k in range(CHIPS):
        for refs, c in ((own, core), (pair, 1 - core)):
            start = (chip ^ k) * (CORES * rows) + c * rows
            for j in range(count):
                w_out[rows_at(start, rows, 16), j * quarter : (j + 1) * quarter] = refs[k][
                    top + j * rows : top + (j + 1) * rows, :
                ]


def half_columns(parts, out, top, count):
    chip, _ = place()
    rows = (parts[0].shape[0] - top) // count
    quarter = parts[0].shape[1]
    for k in range(CHIPS):
        for j in range(count):
            out[chip ^ k, :, j * quarter : (j + 1) * quarter] = parts[k][top + j * rows : top + (j + 1) * rows, :]


def whole_columns(mine, pair, out):
    _, core = place()
    rows = mine.shape[1]
    for b in range(CHIPS):
        for part, c in ((mine, core), (pair, 1 - core)):
            out[rows_at(b * CORES * rows + c * rows, rows, 16), :] = part[b]


def pair_rows(own, pair):
    _, core = place()
    a, b = own[...], pair[...]
    return jnp.concatenate([jnp.where(core == 0, a, b), jnp.where(core == 0, b, a)], axis=0)


def self_kernel(*refs):
    own, pair, (o_own, o_pair, vec) = refs[:4], refs[4:8], refs[8:11]
    x_out, w_out, q_out, k_out, v_out, o_out, wo_out, mine_out = refs[11:19]
    send = refs[19:]
    chip, _ = place()
    quarter = own[0].shape[1]
    length = x_out.shape[0] // CHIPS
    natural_columns(own, pair, w_out, CHIPS * length, 3)
    for k in range(CHIPS):
        for b in range(CHIPS):
            x_out[k * length : (k + 1) * length, b * quarter : (b + 1) * quarter] = own[k][b * length : (b + 1) * length, :]
    for j in range(2):
        wo_out[j] = pair_rows(o_own.at[j], o_pair.at[j])
    lanes = rows_at(chip * quarter, quarter, 128)
    y = dot(x_out[...], w_out[...])
    q = (y[:, :quarter] + vec[0:1, lanes]).astype(BF)
    k = y[:, quarter : 2 * quarter].astype(BF)
    v = (y[:, 2 * quarter :] + vec[1:2, lanes]).astype(BF)
    q_out[...], k_out[...], v_out[...] = q, k, v

    def pair(i, carry):
        for j in range(2):
            s = rows_at((2 * i + j) * length, length, 16)
            o_out[s, :] = attend(q_out[s, :], k_out[s, :], v_out[s, :], True)
        return carry

    lax.fori_loop(0, CHIPS // 2, pair, 0)
    split_rows(dot(o_out[...], wo_out[0]), mine_out, send)


def half_kernel(*refs):
    half_columns(refs[:4], refs[4], 0, 3)


def memory_kernel(*refs):
    mem, own, pair, vec, (m_out, w_out, k_out, v_out) = refs[:4], refs[4:8], refs[8:12], refs[12], refs[13:]
    chip, _ = place()
    quarter = k_out.shape[1]
    natural_columns(own, pair, w_out, own[0].shape[0] - 3 * w_out.shape[0] // TEAM, 3)
    m_out[...] = stack_rows(mem)
    y = dot(m_out[...], w_out[:, quarter:])
    k_out[...] = y[:, :quarter].astype(BF)
    v_out[...] = (y[:, quarter:] + vec[4:5, rows_at(chip * quarter, quarter, 128)]).astype(BF)


def norm_kernel(rows, *refs):
    base, mine, r1, r2, r3, vec, h_out, low_out, z_out, inv_out = refs
    y = mine[...] + r1[...].astype(F32) + r2[...].astype(F32) + r3[...].astype(F32)
    r = base[...].astype(F32) + y + vec[rows[0] : rows[0] + 1, :]
    h, z, inv = norm_rows(r, vec[rows[1] : rows[1] + 1, :], vec[rows[2] : rows[2] + 1, :])
    h_out[...] = h
    low_out[...] = h.astype(BF)
    z_out[...] = z
    inv_out[...] = inv


def cross_kernel(*refs):
    parts, (wo, w_cols, keys, values, vec), (low_out, q_out, o_out, mine_out), send = refs[:4], refs[4:9], refs[9:13], refs[13:]
    chip, _ = place()
    quarter = keys.shape[1]
    length = parts[0].shape[0]
    memory = keys.shape[0] // CHIPS
    low = stack_rows(parts)
    low_out[...] = low
    q = (dot(low, w_cols[:, :quarter]) + vec[3:4, rows_at(chip * quarter, quarter, 128)]).astype(BF)
    q_out[...] = q

    def pair(i, carry):
        for j in range(2):
            s, t = rows_at((2 * i + j) * length, length, 16), rows_at((2 * i + j) * memory, memory, 16)
            o_out[s, :] = attend(q_out[s, :], keys[t, :], values[t, :], False)
        return carry

    lax.fori_loop(0, CHIPS // 2, pair, 0)
    split_rows(dot(o_out[...], wo[1]), mine_out, send)


def gelu_parts(u):
    phi = 0.5 * (1.0 + lax.erf(u * 0.7071067811865476))
    return phi


def up_half_kernel(*refs):
    half_columns(refs[:4], refs[4], 0, 1)


def ffn_kernel(*refs):
    parts, (up_mine, up_pair, down_own, down_pair, vec) = refs[:4], refs[4:9]
    low_out, u_out, a_out, up_out, down_out, mine_out = refs[9:15]
    send = refs[15:]
    chip, _ = place()
    whole_columns(up_mine, up_pair, up_out)
    down_out[...] = pair_rows(down_own, down_pair)
    low = stack_rows(parts)
    low_out[...] = low
    u = dot(low, up_out[...]) + vec[pl.ds(13 + chip, 1), :]
    u_out[...] = u
    a_out[...] = (u * gelu_parts(u)).astype(BF)
    split_rows(dot(a_out[...], down_out[...]), mine_out, send)


def stack_kernel(r0, r1, r2, r3, out, spread_out):
    n = r0.shape[0]
    for k, part in enumerate((r0, r1, r2, r3)):
        out[k * n : (k + 1) * n, :] = part[...]
        for slot in range(SLOTS):
            spread_out[slot, k * n : (k + 1) * n, :] = part[...]


def logits_kernel(length, h0_ref, h1_ref, ids_ref, e_ref, l_ref, pay_ref, h_ref, m_ref, s_ref, p_ref):
    i = pl.program_id(0)
    half = h0_ref.shape[0]

    @pl.when(i == 0)
    def _():
        h_ref[:half, :] = h0_ref[...]
        h_ref[half:, :] = h1_ref[...]
        m_ref[...] = jnp.full_like(m_ref, -3e38)
        s_ref[...] = jnp.zeros_like(s_ref)
        p_ref[...] = jnp.zeros_like(p_ref)

    x = dot(e_ref[...], h_ref[...], NT)
    l_ref[...] = x
    entry = lax.broadcasted_iota(jnp.int32, x.shape, 0) + i * x.shape[0]
    peak = jnp.maximum(m_ref[0:1, :], jnp.max(x, axis=0, keepdims=True))
    total = s_ref[0:1, :] * jnp.exp(m_ref[0:1, :] - peak) + jnp.sum(jnp.exp(x - peak), axis=0, keepdims=True)
    pick = p_ref[0:1, :] + jnp.sum(jnp.where(entry == ids_ref[...], x, 0.0), axis=0, keepdims=True)
    m_ref[0:1, :], s_ref[0:1, :], p_ref[0:1, :] = peak, total, pick

    @pl.when(i == pl.num_programs(0) - 1)
    def _():
        pay_ref[...] = jnp.zeros_like(pay_ref)
        norm = peak + jnp.log(total)
        lane = lax.broadcasted_iota(jnp.int32, (1, 2 * length), 1)
        chip, core = place()
        for n in range(2 * half // (2 * length)):
            s = slice(n * 2 * length, (n + 1) * 2 * length)
            d, rest = divmod(2 * n * length, half)
            first = rest // length
            team, k = first // CHIPS, first % CHIPS
            rows = (
                jnp.where(lane < length, norm[:, s], pltpu.roll(pick[:, s], length, 1)),
                jnp.where(lane < length, pltpu.roll(norm[:, s], length, 1), pick[:, s]),
            )
            for j in range(2):
                q = team * TEAM + (chip ^ (k + j)) * CORES + (core ^ d)
                pay_ref[pl.ds(q, 1), :] = rows[j]


def logits(held, pair, ids, embedding, length, questions):
    half, vocab, width = held.shape[0], embedding.shape[0], embedding.shape[1]
    tile = min(2 * VOCAB_TILE, vocab)
    stat = pltpu.VMEM((8, 2 * half), F32)
    whole = pl.BlockSpec(memory_space=pltpu.VMEM)
    return pl.pallas_call(
        functools.partial(logits_kernel, length),
        grid=(vocab // tile,),
        in_specs=[whole, whole, whole, pl.BlockSpec((tile, width), lambda i: (i, 0))],
        out_specs=[
            pl.BlockSpec((tile, 2 * half), lambda i: (i, 0)),
            pl.BlockSpec((questions, 2 * length), lambda i: (0, 0)),
        ],
        out_shape=[
            pltpu.HBM((vocab, 2 * half), F32),
            jax.ShapeDtypeStruct((questions, 2 * length), F32),
        ],
        scratch_shapes=[pltpu.VMEM((2 * half, width), BF), stat, stat, stat],
        compiler_params=limit(14 + 24 * half * tile // MIB),
        cost_estimate=work(10),
    )(held, pair, ids, embedding)


def merge_kernel(length, all_ref, info_ref, counts_ref, ids_ref, rows_out, own_out, logp_out, prior_out, n_ref, g_ref):
    n_slot, n_pb = n_ref.shape[0], n_ref.shape[1]
    chip, core = place()
    me, slot = lax.axis_index("pb"), lax.axis_index("slot")
    lane = lax.broadcasted_iota(jnp.int32, (1, 2 * length), 1)
    logps, priors = [], None
    for s in range(n_slot):
        blocks = [all_ref[s * n_pb + j, :n_pb, :] for j in range(n_pb)]
        peak = blocks[0]
        for b in blocks[1:]:
            peak = jnp.maximum(peak, b)
        total = jnp.zeros_like(peak)
        pick = jnp.zeros_like(peak)
        for b in blocks:
            total = total + jnp.exp(b - peak)
            pick = pick + b
        norm = peak + jnp.log(total)
        n_ref[s] = norm
        own = info_ref[s * n_pb : (s + 1) * n_pb, :]
        mask = own
        prior = pltpu.roll(own, length, 1)
        logp = pltpu.roll(pick, length, 1) - norm + prior
        logps.append(jnp.where(counts_ref[...] > s, logp, -1e30))
    top = logps[0]
    for p in logps[1:]:
        top = jnp.maximum(top, p)
    total = jnp.zeros_like(top)
    for p in logps:
        total = total + jnp.exp(p - top)
    merged = top + jnp.log(total)
    for s in range(n_slot):
        g_ref[s] = jnp.where(counts_ref[...] > s, -mask * jnp.exp(logps[s] - merged), 0.0)
    n_rows = n_ref.shape[1]
    row = lax.broadcasted_iota(jnp.int32, merged.shape, 0)
    logp_out[...] = jnp.sum(jnp.where(row == me, merged, 0.0), axis=0, keepdims=True)
    own_grad = jnp.where(lane < length, g_ref[slot, pl.ds(me, 1), :], 0.0)
    prior_out[...] = jnp.sum(own_grad, axis=1, keepdims=True)
    rows_out[...] = jnp.zeros_like(rows_out)
    half = rows_out.shape[3]
    for s in range(n_slot):
        for d in range(CORES):
            for n in range(half // (2 * length)):
                team, c = (2 * n) // CHIPS, (2 * n) % CHIPS
                q = [team * TEAM + (chip ^ (c + j)) * CORES + (core ^ d) for j in range(2)]
                t = slice(n * 2 * length, (n + 1) * 2 * length)
                for r, (first, second) in enumerate(
                    (
                        (n_ref[s, pl.ds(q[0], 1), :], n_ref[s, pl.ds(q[1], 1), :]),
                        (g_ref[s, pl.ds(q[0], 1), :], g_ref[s, pl.ds(q[1], 1), :]),
                        (ids_ref[pl.ds(q[0], 1), :], ids_ref[pl.ds(q[1], 1), :]),
                    )
                ):
                    rows_out[s, d, r : r + 1, t] = jnp.where(lane < length, first, pltpu.roll(second, length, 1))
    own_out[0] = rows_out[slot]


def merge(everyone, info, counts, ids, length, n_slot, n_pb, half):
    held = pltpu.VMEM((n_slot, n_pb, 2 * length), F32)
    return pl.pallas_call(
        functools.partial(merge_kernel, length),
        out_shape=[
            jax.ShapeDtypeStruct((n_slot, CORES, 8, half), F32),
            jax.ShapeDtypeStruct((1, CORES, 8, half), F32),
            jax.ShapeDtypeStruct((1, 2 * length), F32),
            jax.ShapeDtypeStruct((1, 1), F32),
        ],
        scratch_shapes=[held, held],
        compiler_params=limit(16 + 2 * everyone.size * 4 // MIB),
        cost_estimate=work(2),
    )(everyone, info, counts, ids)


def logit_gradient(x, rows, first):
    entry = (lax.broadcasted_iota(jnp.int32, x.shape, 0) + first).astype(F32)
    hit = jnp.where(entry == rows[2:3, :], 1.0, 0.0)
    return (rows[1:2, :] * (hit - jnp.exp(x - rows[0:1, :]))).astype(BF)


def state_grad_kernel(l_ref, rows_ref, e_ref, own_ref, pair_ref, d_ref, acc_ref):
    i = pl.program_id(0)
    half = own_ref.shape[0]

    @pl.when(i == 0)
    def _():
        acc_ref[...] = jnp.zeros_like(acc_ref)

    tile = l_ref.shape[0]
    d = [logit_gradient(l_ref[:, c * half : (c + 1) * half], rows_ref[0, c], i * tile) for c in range(CORES)]
    d_ref[...] = jnp.concatenate(d, axis=1)
    acc_ref[...] += dot(d_ref[...], e_ref[...], TN)

    @pl.when(i == pl.num_programs(0) - 1)
    def _():
        own_ref[...] = acc_ref[:half, :].astype(own_ref.dtype)
        pair_ref[...] = acc_ref[half:, :].astype(BF)


def state_grad(scores, rows, embedding, own_type):
    vocab, count = scores.shape
    width = embedding.shape[1]
    half = count // CORES
    tile = min(2 * VOCAB_TILE, vocab)
    last = pl.BlockSpec((half, width), lambda i: (0, 0))
    return pl.pallas_call(
        state_grad_kernel,
        grid=(vocab // tile,),
        in_specs=[
            pl.BlockSpec((tile, count), lambda i: (i, 0)),
            pl.BlockSpec((1,) + rows.shape[1:], lambda i: (0, 0, 0, 0)),
            pl.BlockSpec((tile, width), lambda i: (i, 0)),
        ],
        out_specs=[last, last, pl.BlockSpec((tile, count), lambda i: (i, 0))],
        out_shape=[
            jax.ShapeDtypeStruct((half, width), own_type),
            jax.ShapeDtypeStruct((half, width), BF),
            pltpu.HBM((vocab, count), BF),
        ],
        scratch_shapes=[pltpu.VMEM((count, width), F32)],
        compiler_params=limit(16 + 20 * half * tile // MIB + count * width * 4 // MIB),
        cost_estimate=work(11),
    )(in_hbm(scores), rows, embedding)


def own_embedding_kernel(d_ref, own_ref, pair_ref, *refs):
    half = own_ref.shape[0]
    refs[-1][...] = dot(d_ref[:, :half], own_ref[...]) + dot(d_ref[:, half:], pair_ref[...])


def own_embedding(d, own, pair, held, piece, count):
    vocab, tokens = d.shape
    tile = min(VOCAB_TILE, vocab // count)
    steps = vocab // count // tile
    ahead = [] if held is None else [held]
    whole = pl.BlockSpec(memory_space=pltpu.VMEM)
    shape = (vocab, own.shape[1])
    return pl.pallas_call(
        own_embedding_kernel,
        grid=(steps,),
        in_specs=[pl.BlockSpec((tile, tokens), lambda i: (piece * steps + i, 0)), whole, whole]
        + [pl.BlockSpec(memory_space=pl.ANY)] * len(ahead),
        out_specs=pl.BlockSpec((tile, shape[1]), lambda i: (piece * steps + i, 0)),
        out_shape=pltpu.HBM(shape, F32),
        input_output_aliases={3: 0} if ahead else {},
        compiler_params=limit(14),
        cost_estimate=work(1),
    )(d, own, pair, *ahead)


def embedding_kernel(base, rows_ref, own_ref, pair_ref, e_ref, held_ref, o_ref):
    first = base + pl.program_id(0) * e_ref.shape[0]
    slot = lax.axis_index("slot")
    o_ref[...] = held_ref[...]

    def other(k, carry):
        n = slot ^ k
        for top in range(0, own_ref.shape[1], TOKENS // CORES):
            t = slice(top, top + TOKENS // CORES)
            h = jnp.concatenate([own_ref[n, t, :], pair_ref[n, t, :]], axis=0)
            rows = jnp.concatenate([rows_ref[n, 0, :, t], rows_ref[n, 1, :, t]], axis=1)
            o_ref[...] += dot(logit_gradient(dot(e_ref[...], h, NT), rows, first), h)
        return carry

    lax.fori_loop(1, own_ref.shape[0], other, 0)


def embedding_piece(rows, states, embedding, held, first, size):
    width = embedding.shape[1]
    tile = min(VOCAB_TILE, size)
    steps = size // tile
    whole = pl.BlockSpec(memory_space=pltpu.VMEM)
    block = pl.BlockSpec((tile, width), lambda i: (first // tile + i, 0))
    return pl.pallas_call(
        functools.partial(embedding_kernel, first),
        grid=(steps,),
        in_specs=[whole, whole, whole, block, block],
        out_specs=block,
        out_shape=pltpu.HBM(embedding.shape, F32),
        input_output_aliases={4: 0},
        compiler_params=limit(24),
        cost_estimate=work(3 * size / 1024),
    )(rows, *states, embedding, held)


def add_kernel(mine, got, own_out, *send):
    length = own_out.shape[0]
    for k in range(CHIPS):
        s = slice(k * length, (k + 1) * length)
        y = mine[s, :] + got[s, :].astype(F32)
        if k == 0:
            own_out[...] = y
        else:
            send[k - 1][...] = y.astype(BF)


def norm_back_kernel(row, has_base, *refs):
    base = refs[0] if has_base else None
    mine, r1, r2, r3, z, inv, vec, dr_out, e_out, sums_out = refs[1 if has_base else 0 :]
    dh = mine[...] + r1[...].astype(F32) + r2[...].astype(F32) + r3[...].astype(F32)
    if has_base:
        dh = dh + base[...]
    dr = norm_back(dh, z[...], inv[...], vec[6 + row : 7 + row, :])
    e = dr.astype(BF)
    dr_out[...] = dr
    e_out[...] = e
    sums_out[...] = jnp.zeros_like(sums_out)
    sums_out[0:1, :] = jnp.sum(dh * z[...], axis=0, keepdims=True)
    sums_out[1:2, :] = jnp.sum(dh, axis=0, keepdims=True)
    sums_out[2:3, :] = jnp.sum(e.astype(F32), axis=0, keepdims=True)


def stack_rows(parts):
    return jnp.concatenate([p[...] for p in parts], axis=0)


def split_rows(y, mine_out, send):
    length = mine_out.shape[0]
    mine_out[...] = y[:length]
    for k in range(1, CHIPS):
        send[k - 1][...] = y[k * length : (k + 1) * length].astype(BF)


def column_sum(y):
    return jnp.sum(y.astype(F32), axis=0, keepdims=True)


def ffn_back_kernel(*refs):
    parts, (u_ref, up, down), (e_out, du_out, sum_out, mine_out), send = refs[:4], refs[4:7], refs[7:11], refs[11:]
    e = stack_rows(parts)
    e_out[...] = e
    da = dot(e, down[...], NT).astype(BF).astype(F32)
    u = u_ref[...]
    slope = gelu_parts(u) + u * (jnp.exp(-0.5 * u * u) * 0.3989422804014327)
    du = (da * slope).astype(BF)
    du_out[...] = du
    sum_out[...] = column_sum(du)
    split_rows(dot(du, up[...], NT), mine_out, send)


def pick_core(g, mine_out, other_out, top):
    _, core = place()
    lo, hi = g[:, :, 0], g[:, :, 1]
    n = lo.shape[1] * lo.shape[2]
    mine = jnp.where(core == 0, lo, hi).reshape(CHIPS, n, g.shape[-1])
    other = jnp.where(core == 0, hi, lo).reshape(CHIPS, n, g.shape[-1])
    mine_out[:, top : top + n, :] = mine.astype(BF)
    other_out[:, top : top + n, :] = other.astype(BF)


def place_columns(g, mine_out, other_out, top):
    unit = g.shape[0] // (CHIPS * CHIPS * CORES)
    pick_core(g.reshape(CHIPS, CHIPS, CORES, unit, g.shape[1]), mine_out, other_out, top)


def place_rows(g, mine_out, other_out, top):
    unit = g.shape[0] // (CHIPS * CORES)
    pick_core(g.reshape(CHIPS, 1, CORES, unit, g.shape[1]), mine_out, other_out, top)


def place_row_blocks(g, mine_out, other_out, top, lanes):
    unit = g.shape[0] // (CHIPS * CORES)
    for b in range(g.shape[1] // lanes):
        place_rows(g[:, b * lanes : (b + 1) * lanes], mine_out, other_out, top + b * unit)


def ffn_grads_kernel(low, du, a, e, mine_out, other_out):
    g = dot(low[...], du[...], TN)
    place_columns(g, mine_out, other_out, 0)
    g2 = dot(a[...], e[...], TN)
    place_rows(g2, mine_out, other_out, g.shape[0] // (CHIPS * CORES))


def cross_back_kernel(*refs):
    parts, (w_mine, w_cols, q_ref, k_ref, v_ref) = refs[:4], refs[4:9]
    (e_out, dq_out, dk_out, dv_out, mine_out), send, g_ref = refs[9:14], refs[14:-1], refs[-1]
    quarter = q_ref.shape[1]
    length, memory = q_ref.shape[0] // CHIPS, k_ref.shape[0] // CHIPS
    e = stack_rows(parts)
    e_out[...] = e
    g = dot(e, w_mine[1], NT).astype(BF)
    g_ref[...] = g

    def question(i, carry):
        s, t = rows_at(i * length, length, 16), rows_at(i * memory, memory, 16)
        dq_out[s, :], dk_out[t, :], dv_out[t, :] = attend_back(g_ref[s, :], q_ref[s, :], k_ref[t, :], v_ref[t, :], False)
        return carry

    lax.fori_loop(0, CHIPS, question, 0)
    split_rows(dot(dq_out[...], w_cols[:, :quarter], NT), mine_out, send)


def cross_grads_kernel(low, dq, m, dk, dv, o, e, mine_out, other_out, sums_out):
    n = low.shape[1] // (CHIPS * CORES)
    for j, (a, g) in enumerate(((low, dq), (m, dk), (m, dv))):
        place_columns(dot(a[...], g[...], TN), mine_out, other_out, j * n)
    place_row_blocks(dot(o[...], e[...], TN), mine_out, other_out, 3 * n, dq.shape[1])
    sums_out[...] = jnp.zeros_like(sums_out)
    sums_out[0:1, :] = column_sum(dq[...])
    sums_out[1:2, :] = column_sum(dv[...])


def self_back_kernel(*refs):
    parts, (w_mine, q_ref, k_ref, v_ref), (e_out, d_out, g_ref) = refs[:4], refs[4:8], refs[8:]
    quarter = q_ref.shape[1]
    length = q_ref.shape[0] // CHIPS
    e = stack_rows(parts)
    e_out[...] = e
    g = dot(e, w_mine[0], NT).astype(BF)
    g_ref[...] = g

    def pair(i, carry):
        for j in range(2):
            s = rows_at((2 * i + j) * length, length, 16)
            dq, dk, dv = attend_back(g_ref[s, :], q_ref[s, :], k_ref[s, :], v_ref[s, :], True)
            d_out[s, :quarter] = dq
            d_out[s, quarter : 2 * quarter] = dk
            d_out[s, 2 * quarter :] = dv
        return carry

    lax.fori_loop(0, CHIPS // 2, pair, 0)


SMALL = 16


def self_grads_kernel(x, d, o, e, c_sums, sum_in, one, two, three, mine_out, other_out):
    chip, core = place()
    quarter = d.shape[1] // 3
    n = x.shape[1] // (CHIPS * CORES)
    g = dot(x[...], d[...], TN)
    for j in range(3):
        place_columns(g[:, j * quarter : (j + 1) * quarter], mine_out, other_out, j * n)
    place_row_blocks(dot(o[...], e[...], TN), mine_out, other_out, 3 * n, quarter)

    def spread(row):
        zero = jnp.zeros_like(row)
        return jnp.concatenate([jnp.where(chip == b, row, zero) for b in range(CHIPS)], axis=1)

    rows = [
        spread(column_sum(d[:, :quarter])), spread(column_sum(d[:, 2 * quarter :])), one[2:3, :],
        spread(c_sums[0:1, :]), spread(c_sums[1:2, :]), two[2:3, :], one[0:1, :], two[0:1, :], three[0:1, :],
        one[1:2, :], two[1:2, :], three[1:2, :], three[2:3, :],
    ]
    v = jnp.concatenate(rows + [jnp.zeros((SMALL - len(rows), x.shape[1]), F32)], axis=0)
    unit = x.shape[1] // (CHIPS * CHIPS * CORES)
    wide = sum_in.shape[1] // (CHIPS * CORES)
    last = sum_in[...]
    top = 4 * n
    for out in (mine_out, other_out):
        out[:, top:, :] = jnp.zeros((CHIPS, 2 * SMALL, quarter), BF)
    for s in range(CHIPS):
        halves, ends = [], []
        for c in range(CORES):
            parts = [v[:, ((s * CHIPS + b) * CORES + c) * unit :][:, :unit] for b in range(CHIPS)]
            halves.append(jnp.concatenate(parts, axis=1))
            ends.append(last[:, (s * CORES + c) * wide :][:, :wide])
        for out, swap in ((mine_out, False), (other_out, True)):
            first = (core == 0) != swap
            out[s, top : top + SMALL, : CHIPS * unit] = jnp.where(first, halves[0], halves[1]).astype(BF)
            out[s, top + SMALL : top + SMALL + 1, :wide] = jnp.where(first, ends[0], ends[1]).astype(BF)


def input_back_kernel(d, w_self, dk, dv, w_cross, f_got, mine_out, rest_out, *send):
    chip, _ = place()
    quarter = dk.shape[1]
    length, memory = d.shape[0] // CHIPS, dk.shape[0] // CHIPS
    y = dot(d[...], w_self[...], NT)
    m = dot(dk[...], w_cross[:, quarter : 2 * quarter], NT) + dot(dv[...], w_cross[:, 2 * quarter :], NT)
    f = sum(f_got[n].astype(F32) for n in range(SLOTS)).astype(BF)
    both = length + memory
    unit = (send[0].shape[0] - both)
    rest_out[...] = f[CHIPS * unit :]
    mine_out[:length, :] = y[:length]
    mine_out[length:, :] = m[:memory]
    for k, out in enumerate(send):
        if k:
            out[:length, :] = y[k * length : (k + 1) * length].astype(BF)
            out[length:both, :] = m[k * memory : (k + 1) * memory].astype(BF)
        block = jnp.zeros((unit, f.shape[1]), BF)
        for b in range(CHIPS):
            block = jnp.where((chip ^ k) == b, f[b * unit : (b + 1) * unit], block)
        out[both:, :] = block


def input_total_kernel(base, mine, own, r1, r2, r3, source_out, memory_out, up_out):
    chip, _ = place()
    length = base.shape[0]
    both = mine.shape[0]
    width = base.shape[1]
    y = mine[...]
    for k, r in enumerate((own, r1, r2, r3)):
        if k:
            y = y + r[:both, :].astype(F32)
        up_out[:, rows_at((chip ^ k) * width, width, 128)] = r[both:, :].astype(F32)
    source_out[...] = base[...] + y[:length]
    memory_out[...] = y[length:]


def core_sum_kernel(mine, got, out):
    for n in range(SLOTS):
        out[n] = (mine[n].astype(F32) + got[n].astype(F32)).astype(BF)


def attn_pieces_kernel(s_got, c_got, *outs):
    *pieces, rest = outs
    chip, _ = place()
    s = sum(s_got[n].astype(F32) for n in range(SLOTS)).astype(BF)
    c = sum(c_got[n].astype(F32) for n in range(SLOTS)).astype(BF)
    top = 3 * c.shape[0] // 4
    unit = top // (3 * CHIPS)
    both = [y[:top].reshape(3, CHIPS, unit, y.shape[1]) for y in (s, c)]
    for k in range(CHIPS):
        for m, y in enumerate(both):
            for j in range(3):
                block = jnp.zeros((unit, y.shape[3]), BF)
                for b in range(CHIPS):
                    block = jnp.where((chip ^ k) == b, y[j, b], block)
                pieces[k][(3 * m + j) * unit : (3 * m + j + 1) * unit, :] = block
        pieces[k][6 * unit :, :] = s[c.shape[0] : c.shape[0] + SMALL]
    n = c.shape[0] - top
    rest[:n, :] = s[top : top + n]
    rest[n : 2 * n, :] = c[top:]
    rest[2 * n :, :] = s[c.shape[0] + SMALL :]


def attn_out_kernel(p0, p1, p2, p3, out, bias_out, gain_out, shift_out, last_out):
    chip, _ = place()
    unit, quarter = out.shape[1], p0.shape[1]
    parts = (p0, p1, p2, p3)
    for k, p in enumerate(parts):
        lanes = rows_at((chip ^ k) * quarter, quarter, 128)
        for j in range(6):
            out[j, :, lanes] = p[j * unit : (j + 1) * unit, :].astype(F32)
    total = sum(p[6 * unit :, : CHIPS * unit].astype(F32) for p in parts)
    mine = jnp.zeros((SMALL, unit), F32)
    for b in range(CHIPS):
        mine = jnp.where(chip == b, total[:, b * unit : (b + 1) * unit], mine)
    bias_out[...] = mine[0:6]
    gain_out[...] = mine[6:9]
    shift_out[...] = mine[9:12]
    last_out[...] = mine[12:13]


def rows_out_kernel(owned, f_owned, out, down_out, in_out):
    unit, quarter = out.shape[1], owned.shape[1]
    n = CHIPS * unit
    for m in range(2):
        for b in range(CHIPS):
            out[m, :, b * quarter : (b + 1) * quarter] = owned[m * n + b * unit : m * n + (b + 1) * unit, :].astype(F32)
    down_out[...] = f_owned[...].astype(F32)
    in_out[...] = owned[2 * n : 2 * n + 1, : in_out.shape[1]].astype(F32)


def shards(
    inputs, memory, attn_weight, attn_out, ffn_in, ffn_out, attn_bias, norm_gain, norm_bias,
    bias_in, bias_out, embedding, targets, slot_counts, pad_mask, log_prior,
):
    n_pb, n_slot = lax.axis_size("pb"), lax.axis_size("slot")
    n_all = n_pb * n_slot
    teams = n_pb // TEAM
    me = lax.axis_index("pb")
    length, width = inputs.shape[2], inputs.shape[3]
    passage = memory.shape[2]
    quarter = width // CHIPS
    unit = width // (TEAM * n_slot)
    vocab_rows = embedding.shape[0]
    embedding = in_hbm(embedding)

    def team_rows(w):
        if teams == 1:
            return w
        w = lax.all_gather(w, "pb", axis=0, tiled=True)
        n = w.shape[0] // TEAM
        return lax.dynamic_slice_in_dim(w, (me % TEAM) * n, n)

    x, m = inputs[0, 0], memory[0, 0]
    attn_w = jnp.moveaxis(team_rows(attn_weight), 1, 0)
    out_w = jnp.moveaxis(team_rows(attn_out), 1, 0)
    up_w = team_rows(ffn_in)
    down_w = team_rows(ffn_out)
    rows = attn_w.shape[1]
    ff = up_w.shape[1] // CHIPS
    vec = jnp.concatenate(
        [attn_bias.T, norm_gain.T, norm_bias.T, bias_out[None], bias_in.reshape(CHIPS, -1)], axis=0
    )
    ids = (targets - me * vocab_rows).astype(jnp.int32)
    own_row = jnp.concatenate([pad_mask.astype(F32), jnp.broadcast_to(log_prior, (1, length))], axis=1)
    own_rows_all = lax.all_to_all(
        jnp.broadcast_to(own_row[None], (n_all,) + own_row.shape), ("slot", "pb"), 0, 0, tiled=True
    ).reshape(n_all, 2 * length)

    block = (length, width)
    every = (CHIPS * length, width)
    cols = (CHIPS * length, quarter)
    m_cols = (CHIPS * passage, quarter)
    sends = [(block, BF)] * 3

    def give(send):
        return [from_chip(send[k - 1], k) for k in range(1, CHIPS)]

    def give_far(send):
        return [in_hbm(r) for r in give(send)]

    far_call = functools.partial(call, far=True)

    first = call(functools.partial(pack_kernel, 6, 0), [((CHIPS * length + 6 * rows, quarter), BF)] * CHIPS, x, attn_w)
    got_first = [first[0]] + give(first[1:])
    got_first[3], vec = tie(got_first[3], vec)
    got_first[1], own_rows_all = tie(got_first[1], own_rows_all)
    pair_first = [from_core(g) for g in got_first]
    out_pair = from_core(out_w)
    down_pair = from_core(down_w)
    third = list(call(functools.partial(pack_kernel, 1, 0), [((rows, ff), BF)] * CHIPS, up_w[None]))
    m_send, pair_first[3] = tie(m, pair_first[3])
    got_memory = [m, from_chip(m_send, 1), from_chip(m_send, 2)]

    x_all, w_self, queries, keys, values, mixed, w_out, mine, *send = call(
        self_kernel,
        [(every, BF), ((width, 3 * quarter), BF)] + [(cols, BF)] * 4 + [((2, quarter, width), BF), (block, F32)]
        + sends,
        *got_first, *pair_first, out_w, out_pair, vec,
    )
    got_memory[1], send[0] = tie(got_memory[1], send[0])
    got = give(send)
    got_memory.append(from_chip(got_memory[1], 2))
    *got_memory, got[0], got[1], got[2] = tie(*got_memory, *got)
    norm_outs = [(block, F32), (block, BF), (block, F32), ((length, 1), F32)]
    hidden_one, low_one, z_one, inv_one = call(
        functools.partial(norm_kernel, (2, 6, 9)), norm_outs, x, mine, *got, vec, us=1
    )
    got_low = [low_one] + others(low_one)
    got_third = [third[0], from_chip(third[1], 1), from_chip(third[2], 2)]
    m_all, w_cross, cross_keys, cross_values = call(
        memory_kernel, [((CHIPS * passage, width), BF), ((width, 3 * quarter), BF)] + [(m_cols, BF)] * 2,
        *got_memory, *got_first, *pair_first, vec,
    )
    got_third[1], got_third[2], *got_low = tie(got_third[1], got_third[2], *got_low)
    low_one_all, cross_queries, cross_mixed, mine, *send = call(
        cross_kernel, [(every, BF), (cols, BF), (cols, BF), (block, F32)] + sends,
        *got_low, w_out, w_cross, cross_keys, cross_values, vec,
    )
    got = give(send)
    third[3], got_third[1] = tie(third[3], got_third[1])
    got_third.append(from_chip(third[3], 3))
    got_third[3], *got = tie(got_third[3], *got)
    hidden_two, low_two, z_two, inv_two = call(
        functools.partial(norm_kernel, (5, 7, 10)), norm_outs, hidden_one, mine, *got, vec, us=1
    )
    got_low = [low_two] + others(low_two)
    (up_half,) = call(up_half_kernel, [((CHIPS, rows, ff), BF)], *got_third)
    up_half_pair = from_core(up_half)
    low_two_all, upward, active, w_up, w_down, mine, *send = call(
        ffn_kernel,
        [(every, BF), ((CHIPS * length, ff), F32), ((CHIPS * length, ff), BF), ((width, ff), BF)]
        + [((ff, width), BF), (block, F32)]
        + sends,
        *got_low, up_half, up_half_pair, down_w, down_pair, vec,
    )
    got = give(send)
    _, final_low, z_three, inv_three = call(
        functools.partial(norm_kernel, (12, 8, 11)), norm_outs, hidden_two, mine, *got, vec, us=1
    )

    held, spread_held = call(
        stack_kernel, [(every, BF), ((n_slot,) + every, BF)], final_low, *others(final_low), us=1, far=(1,) if teams == 1 else ()
    )
    pair = from_core(held)

    def all_teams(h):
        return lax.all_gather(h, "pb", axis_index_groups=same_place_groups(), axis=0, tiled=True) if teams > 1 else h

    half = teams * CHIPS * length
    chip, core = place()
    order = [
        t * TEAM + (chip ^ k) * CORES + (core ^ d) for d in range(CORES) for t in range(teams) for k in range(CHIPS)
    ]
    ids_row = jnp.concatenate([lax.dynamic_slice_in_dim(ids, q, 1) for q in order], axis=1)
    states = [all_teams(held), all_teams(pair)]
    scores, payload = logits(*states, ids_row, embedding, length, n_pb)
    everyone = lax.all_to_all(
        jnp.broadcast_to(payload[None], (n_all,) + payload.shape), ("slot", "pb"), 0, 0, tiled=True
    )
    ids_wide = jnp.pad(ids.astype(F32), ((0, 0), (0, length)))
    spread_held, everyone = tie(spread_held, everyone)
    all_held = across_slots(spread_held)
    token_rows, own_rows, token_logprob, prior_grad = merge(
        everyone, own_rows_all, slot_counts.astype(jnp.int32)[:, None], ids_wide, length, n_slot, n_pb, half
    )
    def home(partial):
        if teams == 1:
            return partial
        return lax.psum_scatter(partial, "pb", axis_index_groups=same_place_groups(), scatter_dimension=0, tiled=True)

    own_part, for_pair, own_logits = state_grad(scores, own_rows, embedding, F32)
    own_logits = in_hbm(own_logits)
    own_part, got_pair = home(own_part), from_core(home(for_pair))
    mine, *send = call(add_kernel, [(block, F32)] + sends, own_part, got_pair, us=1)
    got = give(send)
    own_logits, send[0] = tie(own_logits, send[0])
    own_terms = own_embedding(own_logits, *states, None, 0, 2)
    own_terms, *got = tie(own_terms, *got)

    eighth = vocab_rows // 8
    parts = (1, 1, 1, 5)
    made = []

    def piece(*wait):
        n = len(made) - 1
        rows_in, *wait = tie(token_rows, *wait)
        first = sum(parts[:n]) * eighth
        made.append(embedding_piece(rows_in, states, embedding, made[-1], first, parts[n] * eighth))
        return wait

    def pieces(count, *wait):
        for _ in range(count):
            wait = piece(*wait)
        return list(wait)

    def then(*values):
        *values, made[-1] = tie(*values, made[-1])
        return values

    def settle(g):
        if teams == 1:
            return g
        g = lax.psum(g, "pb", axis_index_groups=same_place_groups())
        g = lax.all_gather(g, "pb", axis_index_groups=team_groups(), axis=0, tiled=True)
        n = g.shape[0] // n_pb
        return lax.dynamic_slice_in_dim(g, me * n, n)

    def to_owner(g):
        pairs = []
        for s in range(n_slot):
            for i in range(n_pb):
                t, b, c = i // TEAM, (i % TEAM) // CORES, i % CORES
                pairs.append((s * n_pb + i, b * n_pb + t * TEAM + s * CORES + c))
        return lax.ppermute(g, ("slot", "pb"), pairs)

    x_all, w_self, queries, keys, values, mixed, w_out, m_all, w_cross, cross_keys, cross_values = (
        in_hbm(v)
        for v in (x_all, w_self, queries, keys, values, mixed, w_out, m_all, w_cross, cross_keys, cross_values)
    )
    low_one_all, cross_queries, cross_mixed, low_two_all, upward, active, w_up, w_down = (
        in_hbm(v) for v in (low_one_all, cross_queries, cross_mixed, low_two_all, upward, active, w_up, w_down)
    )
    z_one, z_two, z_three = in_hbm(z_one), in_hbm(z_two), in_hbm(z_three)
    grads = [(block, F32), (block, BF), ((8, width), F32)]
    dr_three, e_three, sums_three = call(
        functools.partial(norm_back_kernel, 2, False), grads, mine, *got, z_three, inv_three, vec, us=1
    )
    got_e = others(e_three)
    own_logits, e_three = tie(own_logits, e_three)
    own_terms = own_embedding(own_logits, *states, own_terms, 1, 2)
    own_terms, *got_e = tie(own_terms, *got_e)
    made.append(own_terms)
    e_all, du, sum_in, mine, *send = call(
        ffn_back_kernel,
        [(every, BF), ((CHIPS * length, ff), BF), ((1, ff), F32), (block, F32)] + sends,
        e_three, *got_e, upward, w_up, w_down,
    )
    got = give(send)
    f_shape = (n_slot, CHIPS * unit + ff // TEAM, width)
    du, send[0] = tie(du, send[0])
    f_mine, f_other = far_call(ffn_grads_kernel, [(f_shape, BF)] * 2, low_two_all, du, active, e_all, us=3)
    f_other, all_held, *got = tie(f_other, all_held, *got)
    all_pair = from_core(all_held)
    dr_two, e_two, sums_two = far_call(
        functools.partial(norm_back_kernel, 1, True), grads, dr_three, mine, *got, z_two, inv_two, vec, us=1
    )
    got_e = give_far([e_two] * 3)
    f_got = from_core(f_other)
    f_got, all_pair, got_e[2] = tie(f_got, all_pair, got_e[2])
    states = [jnp.stack([all_teams(h[n]) for n in range(n_slot)]) if teams > 1 else h for h in (all_held, all_pair)]
    (f_total,) = far_call(core_sum_kernel, [(f_shape, BF)], f_mine, f_got)
    f_got = across_slots(f_total)
    e_all_two, dqc, dkc, dvc, mine, *send = far_call(
        cross_back_kernel,
        [(every, BF), (cols, BF), (m_cols, BF), (m_cols, BF), (block, F32)] + sends,
        e_two, *got_e, w_out, w_cross, cross_queries, cross_keys, cross_values, us=5,
        scratch=[pltpu.VMEM(cols, BF)],
    )
    got = give(send)
    dqc, send[0] = tie(dqc, send[0])
    g_shape = (n_slot, 4 * CHIPS * unit, quarter)
    c_mine, c_other, c_sums = call(
        cross_grads_kernel, [(g_shape, BF)] * 2 + [((8, quarter), F32)],
        low_one_all, dqc, m_all, dkc, dvc, cross_mixed, e_all_two,
    )
    c_got = from_core(c_other)
    (c_mine,) = piece(c_mine)
    got = then(*got)
    dr_one, e_one, sums_one = far_call(
        functools.partial(norm_back_kernel, 0, True), grads, dr_two, mine, *got, z_one, inv_one, vec, us=1
    )
    got_e = give([e_one] * 3)
    c_got, e_one = tie(c_got, e_one)
    (c_total,) = far_call(core_sum_kernel, [(g_shape, BF)], c_mine, c_got)
    (c_total,) = piece(c_total)
    c_total, f_got, *got_e = then(c_total, f_got, *got_e)
    c_got = across_slots(c_total)
    e_all_one, d_self = far_call(
        self_back_kernel, [(every, BF), ((CHIPS * length, 3 * quarter), BF)], e_one, *got_e, w_out, queries, keys, values, us=4,
        scratch=[pltpu.VMEM(cols, BF)],
    )
    s_shape = (n_slot, g_shape[1] + 2 * SMALL, quarter)
    s_mine, s_other = far_call(
        self_grads_kernel, [(s_shape, BF)] * 2, x_all, d_self, mixed, e_all_one, c_sums, sum_in, sums_one, sums_two, sums_three
    )
    s_got = from_core(s_other)
    f_got, s_mine = tie(f_got, s_mine)
    both = (length + passage, width)
    f_rest = (f_shape[1] - CHIPS * unit, width)
    mine, f_rest, *send = far_call(
        input_back_kernel, [(both, F32), (f_rest, BF)] + [((both[0] + unit, width), BF)] * CHIPS,
        d_self, w_self, dkc, dvc, w_cross, f_got, us=3,
    )
    f_owned = to_owner(f_rest)
    s_got, send[0] = tie(s_got, send[0])
    (s_total,) = far_call(core_sum_kernel, [(s_shape, BF)], s_mine, s_got)
    (s_total,) = pieces(1, s_total)
    (c_got,) = then(c_got)
    s_total, send[0], c_got = tie(s_total, send[0], c_got)
    s_got = across_slots(s_total)
    got = give(send[1:])
    (send[0],) = pieces(len(parts) + 1 - len(made), send[0])
    s_got, *got = then(s_got, *got)
    *piece_parts, rest = call(
        attn_pieces_kernel,
        [((6 * unit + SMALL, quarter), BF)] * CHIPS + [((2 * CHIPS * unit + SMALL, quarter), BF)],
        s_got, c_got,
    )
    last = give(piece_parts[1:])
    owned = to_owner(rest)
    grad_source, grad_passage, out_up = call(
        input_total_kernel, [(block, F32), ((passage, width), F32), ((unit, up_w.shape[1]), F32)],
        dr_one, mine, send[0], *got, us=1,
    )
    owned, grad_source, *last = tie(owned, grad_source, *last)
    out_attn, *vectors = call(
        attn_out_kernel,
        [((6, unit, width), F32), ((6, unit), F32), ((3, unit), F32), ((3, unit), F32), ((1, unit), F32)],
        piece_parts[0], *last, us=1,
    )
    outs, out_down, sum_in_out = call(
        rows_out_kernel, [((2, unit, width), F32), (f_rest.shape, F32), ((1, ff // TEAM), F32)], owned, f_owned, us=1
    )
    out_attn = settle(jnp.moveaxis(out_attn, 0, 1))
    out_outputs = settle(jnp.moveaxis(outs, 0, 1))
    out_up, out_down = settle(out_up), settle(out_down)
    vectors = [settle(v) for v in (vectors[0].T, vectors[1].T, vectors[2].T, sum_in_out[0], vectors[3][0])]
    return (
        token_logprob[:, :length],
        grad_source[None, None],
        grad_passage[None, None],
        prior_grad,
        out_attn,
        out_outputs,
        out_up,
        out_down,
        vectors[0],
        vectors[1],
        vectors[2],
        vectors[3],
        vectors[4],
        made[-1],
    )


def solution(mesh):
    placed = (
        P("pb", "slot", None, None),
        P("pb", "slot", None, None),
        P("pb", None, None),
        P("pb", None, None),
        P("pb", None),
        P("pb", None),
        P(),
        P(),
        P(),
        P(),
        P(),
        P("pb", None),
        P(),
        P(),
        P("pb", None),
        P("pb", "slot"),
    )
    both = ("slot", "pb")
    return jax.shard_map(
        shards,
        mesh=mesh,
        in_specs=placed,
        out_specs=(
            P("pb", None),
            P("pb", "slot", None, None),
            P("pb", "slot", None, None),
            P("pb", "slot"),
            P(both, None, None),
            P(both, None, None),
            P(both, None),
            P(both, None),
            P(both, None),
            P(both, None),
            P(both, None),
            P(both),
            P(both),
            P("pb", None),
        ),
        check_vma=False,
    )
```
